32 devices in a mesh: section: 2 (over y), tensor: 4 (over z), ctx: 4 (over x, core).
Axes of the slice: x: 2, y: 2, z: 4, core: 2. Of those that a mesh axis runs over, the one named last changes fastest.
Arguments:
- latents: bfloat16 [3, 1024, 1152], P(None, 'ctx'), may hold values from -6 to 6
- condition: float32 [3, 1152], P(None, 'ctx'), may hold values from -6 to 6
- cotangent: bfloat16 [3, 1024, 1152], P(None, 'ctx'), may hold values from -6 to 6
- w_ada: bfloat16 [2, 1152, 6912], P('section', 'ctx', 'tensor'), may hold values from -0.1875 to 0.1875
- b_ada: float32 [2, 6912], P('section', 'tensor'), may hold values from -3 to 3
- w_qkv: bfloat16 [2, 1152, 3, 1152], P('section', None, None, 'tensor'), may hold values from -0.1875 to 0.1875
- b_qv: float32 [2, 2, 1152], P('section', None, 'tensor'), may hold values from -3 to 3
- w_out: bfloat16 [2, 1152, 1152], P('section', 'tensor'), may hold values from -1.5 to 1.5
- b_out: float32 [2, 1152], P('section'), may hold values from -3 to 3
- w_fc1: bfloat16 [2, 1152, 4608], P('section', None, 'tensor'), may hold values from -0.1875 to 0.1875
- b_fc1: float32 [2, 4608], P('section', 'tensor'), may hold values from -3 to 3
- w_fc2: bfloat16 [2, 4608, 1152], P('section', 'tensor'), may hold values from -0.09375 to 0.09375
- b_fc2: float32 [2, 1152], P('section'), may hold values from -3 to 3
Outputs:
- block_out: bfloat16 [2, 3, 1024, 1152], P('section', None, 'ctx')
- in_grad: float32 [2, 3, 1024, 1152], P('section', None, 'ctx')
- cond_grad: float32 [3, 1152], P(None, 'ctx')
- grad_w_ada: float32 [2, 1152, 6912], P('section', 'ctx', 'tensor')
- grad_b_ada: float32 [2, 6912], P('section', 'tensor')
- grad_w_qkv: float32 [2, 1152, 3, 1152], P('section', 'ctx', None, 'tensor')
- grad_b_qv: float32 [2, 2, 1152], P('section', None, 'tensor')
- grad_w_out: float32 [2, 1152, 1152], P('section', 'tensor', 'ctx')
- grad_b_out: float32 [2, 1152], P('section')
- grad_w_fc1: float32 [2, 1152, 4608], P('section', 'ctx', 'tensor')
- grad_b_fc1: float32 [2, 4608], P('section', 'tensor')
- grad_w_fc2: float32 [2, 4608, 1152], P('section', 'tensor', 'ctx')
- grad_b_fc2: float32 [2, 1152], P('section')
The draws below stay inside these ranges and needn't reach their ends.
All inputs are finite; a program needn't handle non-finite values.
Results may differ from the reference program's by a relative error of at most 0.025.
Values may be sent and summed in bfloat16 or wider, within the bound.
A program may use at most 192 MiB of HBM per device.

```python
import math
import jax
import jax.numpy as jnp
from jax import lax

D = 1152
HEADS = 16
HD = 72
FF = 4608
DC = 1152
SEQ = 1024
LAT = 3
N_TENSOR = 4


def block_levels(stream_key, shape, split, smallest, largest):
    loudness, own = 1.0, jax.random.fold_in(stream_key, 6)
    for axis_at, parts in split:
        steps = jnp.exp(jax.random.uniform(jax.random.fold_in(own, axis_at), (parts,), jnp.float32, smallest / len(split), largest / len(split)))
        loudness = loudness * jnp.repeat(steps, shape[axis_at] // parts).reshape([-1 if axis == axis_at else 1 for axis in range(len(shape))])
    return loudness


def scatter_about(rng, shape, scale, reach, pieces=(), kind=jnp.bfloat16):
    result = scale * jax.random.normal(rng, shape, jnp.float32)
    if pieces:
        result = result * block_levels(rng, shape, pieces, -0.22, 0.18)
    return jnp.clip(result, -reach, reach).astype(kind)


def setup_inputs(seed: int = 0) -> dict:
    splits = jax.random.split(jax.random.key(seed), 14)
    return {
        "latents": scatter_about(splits[0], (LAT, SEQ, D), 1.0, 6.0, ((1, 4),)),
        "condition": scatter_about(splits[1], (LAT, DC), 1.0, 6.0, ((1, 4),), jnp.float32),
        "cotangent": scatter_about(splits[2], (LAT, SEQ, D), 1.0, 6.0, ((1, 4),)),
        "w_ada": scatter_about(splits[3], (2, DC, 6 * D), DC ** -0.5, 0.1875, ((0, 2), (1, 4), (2, 4))),
        "b_ada": scatter_about(splits[4], (2, 6 * D), 0.5, 3.0, ((0, 2), (1, 4)), jnp.float32),
        "w_qkv": scatter_about(splits[5], (2, D, 3, D), D ** -0.5, 0.1875, ((0, 2), (3, 4))),
        "b_qv": scatter_about(splits[6], (2, 2, D), 0.5, 3.0, ((0, 2), (2, 4)), jnp.float32),
        "w_out": scatter_about(splits[7], (2, D, D), (D // 64) ** -0.5, 1.5, ((0, 2), (1, 4))),
        "b_out": scatter_about(splits[8], (2, D), 0.5, 3.0, ((0, 2),), jnp.float32),
        "w_fc1": scatter_about(splits[9], (2, D, FF), D ** -0.5, 0.1875, ((0, 2), (2, 4))),
        "b_fc1": scatter_about(splits[10], (2, FF), 0.5, 3.0, ((0, 2), (1, 4)), jnp.float32),
        "w_fc2": scatter_about(splits[11], (2, FF, D), FF ** -0.5, 0.09375, ((0, 2), (1, 4))),
        "b_fc2": scatter_about(splits[12], (2, D), 0.5, 3.0, ((0, 2),), jnp.float32),
    }


EPSILON = 1e-06

def layer_norm(values):
    centre = lax.optimization_barrier(jnp.mean(values, axis=-1, keepdims=True))
    centred = values - centre
    variance = lax.optimization_barrier(jnp.mean(centred * centred, axis=-1, keepdims=True))
    inverse = lax.rsqrt(variance + EPSILON)
    return (centred * inverse, inverse)

def norm_back(normed, inverse, upstream):
    mean_grad = lax.optimization_barrier(jnp.mean(upstream, axis=-1, keepdims=True))
    mean_cross = lax.optimization_barrier(jnp.mean(upstream * normed, axis=-1, keepdims=True))
    return inverse * (upstream - mean_grad - normed * mean_cross)

def rounded_sum(partials):
    rounded = lax.optimization_barrier(partials.astype(jnp.bfloat16))
    return lax.optimization_barrier(jnp.sum(rounded.astype(jnp.float32), axis=0))

def gelu_back(pre_act, upstream):
    unused_out, pullback = jax.vjp(lambda pre_value: jax.nn.gelu(pre_value, approximate=True), pre_act)
    return pullback(upstream)[0]

def head_view(array):
    return array.astype(jnp.float32).reshape(array.shape[0], HEADS, HD)

def block_forward(inputs, modulation, weights):
    w_qkv, b_qv, w_out, b_out, w_fc1, b_fc1, w_fc2, b_fc2 = weights
    length = inputs.shape[0]
    groups = N_TENSOR
    softmax_scale = 1.0 / math.sqrt(HD)
    residual = inputs.astype(jnp.float32)
    normed_a, inverse_a = layer_norm(residual)
    attn_in = (normed_a * (1.0 + modulation[1]) + modulation[0]).astype(jnp.bfloat16)
    projected = jnp.dot(attn_in, w_qkv.reshape(D, 3 * D), preferred_element_type=jnp.float32).reshape(length, 3, D)
    queries = (projected[:, 0] + b_qv[0]).astype(jnp.bfloat16)
    key_rows = projected[:, 1].astype(jnp.bfloat16)
    values = (projected[:, 2] + b_qv[1]).astype(jnp.bfloat16)
    scores = jnp.einsum('qhd,khd->hqk', head_view(queries), head_view(key_rows)) * softmax_scale
    row_peak = lax.optimization_barrier(jnp.max(scores, axis=-1, keepdims=True))
    log_total = row_peak + jnp.log(lax.optimization_barrier(jnp.sum(jnp.exp(scores - row_peak), axis=-1, keepdims=True)))
    prob_bf = jnp.exp(scores - log_total).astype(jnp.bfloat16)
    context = jnp.einsum('hqk,khd->qhd', prob_bf.astype(jnp.float32), head_view(values)).astype(jnp.bfloat16).reshape(length, D)
    attn_terms = jnp.einsum('sgc,gcd->gsd', context.astype(jnp.float32).reshape(length, groups, D // groups), w_out.astype(jnp.float32).reshape(groups, D // groups, D))
    attn_out = rounded_sum(attn_terms) + b_out
    middle = residual + modulation[2] * attn_out
    normed_m, inverse_m = layer_norm(middle)
    mlp_in = (normed_m * (1.0 + modulation[4]) + modulation[3]).astype(jnp.bfloat16)
    pre_act = jnp.dot(mlp_in, w_fc1, preferred_element_type=jnp.float32) + b_fc1
    hidden = jax.nn.gelu(pre_act, approximate=True).astype(jnp.bfloat16)
    mlp_terms = jnp.einsum('sgf,gfd->gsd', hidden.astype(jnp.float32).reshape(length, groups, FF // groups), w_fc2.astype(jnp.float32).reshape(groups, FF // groups, D))
    mlp_out = rounded_sum(mlp_terms) + b_fc2
    output = (middle + modulation[5] * mlp_out).astype(jnp.bfloat16)
    stored = (normed_a, inverse_a, attn_in, queries, key_rows, values, log_total, context, attn_out, normed_m, inverse_m, mlp_in, pre_act, hidden, mlp_out)
    return (output, stored)

def block_backward(upstream, stored, modulation, weights):
    w_qkv, b_qv, w_out, b_out, w_fc1, b_fc1, w_fc2, b_fc2 = weights
    normed_a, inverse_a, attn_in, queries, key_rows, values, log_total, context, attn_out, normed_m, inverse_m, mlp_in, pre_act, hidden, mlp_out = stored
    length = upstream.shape[0]
    groups = N_TENSOR
    softmax_scale = 1.0 / math.sqrt(HD)
    gate_m_grad = lax.optimization_barrier(jnp.sum(upstream * mlp_out, axis=0))
    mlp_grad = upstream * modulation[5]
    mlp_grad_b = mlp_grad.astype(jnp.bfloat16)
    grad_w2 = jnp.dot(hidden.T, mlp_grad_b, preferred_element_type=jnp.float32)
    grad_b2 = lax.optimization_barrier(jnp.sum(mlp_grad, axis=0))
    pre_grad = gelu_back(pre_act, jnp.dot(mlp_grad_b, w_fc2.T, preferred_element_type=jnp.float32))
    pre_grad_b = pre_grad.astype(jnp.bfloat16)
    grad_w1 = jnp.dot(mlp_in.T, pre_grad_b, preferred_element_type=jnp.float32)
    grad_b1 = lax.optimization_barrier(jnp.sum(pre_grad, axis=0))
    mlp_in_grad = rounded_sum(jnp.einsum('sgf,dgf->gsd', pre_grad_b.astype(jnp.float32).reshape(length, groups, FF // groups), w_fc1.astype(jnp.float32).reshape(D, groups, FF // groups)))
    shift_m_grad = lax.optimization_barrier(jnp.sum(mlp_in_grad, axis=0))
    scale_m_grad = lax.optimization_barrier(jnp.sum(mlp_in_grad * normed_m, axis=0))
    middle_grad = upstream + norm_back(normed_m, inverse_m, mlp_in_grad * (1.0 + modulation[4]))
    gate_a_grad = lax.optimization_barrier(jnp.sum(middle_grad * attn_out, axis=0))
    attn_grad = middle_grad * modulation[2]
    attn_grad_b = attn_grad.astype(jnp.bfloat16)
    grad_wo = jnp.dot(context.T, attn_grad_b, preferred_element_type=jnp.float32)
    grad_bo = lax.optimization_barrier(jnp.sum(attn_grad, axis=0))
    context_grad = jnp.dot(attn_grad_b, w_out.T, preferred_element_type=jnp.float32).astype(jnp.bfloat16)
    query_heads = head_view(queries)
    key_heads = head_view(key_rows)
    scores = jnp.einsum('qhd,khd->hqk', query_heads, key_heads) * softmax_scale
    prob_full = jnp.exp(scores - log_total)
    prob_bf = prob_full.astype(jnp.bfloat16)
    grad_heads = head_view(context_grad)
    prob_grad = jnp.einsum('qhd,khd->hqk', grad_heads, head_view(values))
    delta_rows = lax.optimization_barrier(jnp.sum(grad_heads * head_view(context), axis=-1)).T[:, :, None]
    score_grad = (prob_full * (prob_grad - delta_rows)).astype(jnp.bfloat16).astype(jnp.float32)
    query_grad = (jnp.einsum('hqk,khd->qhd', score_grad, key_heads) * softmax_scale).reshape(length, D)
    key_grad = (jnp.einsum('hqk,qhd->khd', score_grad, query_heads) * softmax_scale).reshape(length, D)
    value_grad = jnp.einsum('hqk,qhd->khd', prob_bf.astype(jnp.float32), grad_heads).reshape(length, D)
    grad_bqv = jnp.stack([lax.optimization_barrier(jnp.sum(query_grad, axis=0)), lax.optimization_barrier(jnp.sum(value_grad, axis=0))])
    qkv_grad_b = jnp.stack([query_grad, key_grad, value_grad], axis=1).astype(jnp.bfloat16)
    grad_wqkv = jnp.dot(attn_in.T, qkv_grad_b.reshape(length, 3 * D), preferred_element_type=jnp.float32).reshape(D, 3, D)
    attn_in_grad = rounded_sum(jnp.einsum('sjgc,djgc->gsd', qkv_grad_b.astype(jnp.float32).reshape(length, 3, groups, D // groups), w_qkv.astype(jnp.float32).reshape(D, 3, groups, D // groups)))
    shift_a_grad = lax.optimization_barrier(jnp.sum(attn_in_grad, axis=0))
    scale_a_grad = lax.optimization_barrier(jnp.sum(attn_in_grad * normed_a, axis=0))
    input_grad = middle_grad + norm_back(normed_a, inverse_a, attn_in_grad * (1.0 + modulation[1]))
    mod_grad = jnp.stack([shift_a_grad, scale_a_grad, gate_a_grad, shift_m_grad, scale_m_grad, gate_m_grad])
    return (input_grad, mod_grad, (grad_wqkv, grad_bqv, grad_wo, grad_bo, grad_w1, grad_b1, grad_w2, grad_b2))

def reference(latents, condition, cotangent, w_ada, b_ada, w_qkv, b_qv, w_out, b_out, w_fc1, b_fc1, w_fc2, b_fc2):
    cond_act = jax.nn.silu(condition).astype(jnp.bfloat16)
    section_weights = [tuple((weight[block_id] for weight in (w_qkv, b_qv, w_out, b_out, w_fc1, b_fc1, w_fc2, b_fc2))) for block_id in range(2)]
    modulation = [(jnp.dot(cond_act, w_ada[block_id], preferred_element_type=jnp.float32) + b_ada[block_id]).reshape(LAT, 6, D) for block_id in range(2)]

    def run_forward(block_id, inputs):
        params = section_weights[block_id]
        return lax.map(lambda pair: block_forward(pair[0], pair[1], params)[0], (inputs, modulation[block_id]))

    def run_backward(block_id, inputs, upstream):
        params = section_weights[block_id]

        def step_fn(carry, item):
            block_in, mod_latent, grad_latent = item
            unused_out, stored = block_forward(block_in, mod_latent, params)
            input_grad, mod_grad, grad_terms = block_backward(grad_latent, stored, mod_latent, params)
            return (jax.tree.map(jnp.add, carry, grad_terms), (input_grad, mod_grad))
        zeros_init = tuple((jnp.zeros(weight.shape, jnp.float32) for weight in params))
        return lax.scan(step_fn, zeros_init, (inputs, modulation[block_id], upstream))
    first_out = run_forward(0, latents)
    second_out = run_forward(1, first_out)
    second_grads, (second_in_grad, second_mod) = run_backward(1, first_out, cotangent.astype(jnp.float32))
    first_grads, (first_in_grad, first_mod) = run_backward(0, latents, second_in_grad)
    mod_grads = [first_mod.reshape(LAT, 6 * D), second_mod.reshape(LAT, 6 * D)]
    mod_rounded = [grad_mod.astype(jnp.bfloat16) for grad_mod in mod_grads]
    grad_w_ada = jnp.stack([jnp.dot(cond_act.T, mod_rounded[block_id], preferred_element_type=jnp.float32) for block_id in range(2)])
    grad_b_ada = jnp.stack([lax.optimization_barrier(jnp.sum(mod_grads[block_id], axis=0)) for block_id in range(2)])
    cond_sum = jnp.dot(mod_rounded[0], w_ada[0].T, preferred_element_type=jnp.float32) + jnp.dot(mod_rounded[1], w_ada[1].T, preferred_element_type=jnp.float32)
    sigmoid_c = jax.nn.sigmoid(condition)
    cond_grad = cond_sum * sigmoid_c * (1.0 + condition * (1.0 - sigmoid_c))
    stacked = [jnp.stack([first_grads[which], second_grads[which]]) for which in range(8)]
    return (jnp.stack([first_out, second_out]), jnp.stack([first_in_grad, second_in_grad]), cond_grad, grad_w_ada, grad_b_ada, stacked[0], stacked[1], stacked[2], stacked[3], stacked[4], stacked[5], stacked[6], stacked[7])
```

```python
import functools
import math

import jax
import jax.numpy as jnp
from jax import lax
from jax.experimental import pallas as pl
from jax.experimental.pallas import tpu as pltpu
from jax.sharding import PartitionSpec as P

HD = 72
EPSILON = 1e-06
MESH = pl.DeviceIdType.MESH
ROW_TILE = 16
VMEM = pl.BlockSpec(memory_space=pltpu.VMEM)


def inner_size(n):
    return 2 if n % 2 == 0 else 1


def remote(src, dst, send, recv, **to):
    return pltpu.make_async_remote_copy(
        src_ref=src,
        dst_ref=dst,
        send_sem=send,
        recv_sem=recv,
        device_id=to,
        device_id_type=MESH,
    )


def greet(peers):
    barrier = pltpu.get_barrier_semaphore()
    for peer in peers:
        pl.semaphore_signal(barrier, inc=1, device_id=peer, device_id_type=MESH)
    pl.semaphore_wait(barrier, len(peers))


def link_cost(moved):
    return pl.CostEstimate(flops=0, bytes_accessed=moved, transcendentals=0)


def start_all(copies, sent):
    for copy in copies:
        copy.start()
        sent.append(copy)


def middle_role(d, n, pieces, rows, lag, x_ref, out_ref, acc, from_outer, from_middle, sems):
    up_send, up_recv, mid_send, mid_recv, down_send, down_recv = sems
    half = n // 2
    left = d < half
    outer, inner = (d - 1, d + 1) if left else (d + 1, d - 1)
    has_outer = 0 <= outer < n
    is_middle = d in (half - 1, half)
    to_middle = half - 1 - d if left else d - half

    def hop(src, dst, send, recv, to, p):
        span = pl.ds(p * rows, rows)
        return remote(src.at[span], dst.at[span], send.at[p], recv.at[p], tensor=to)

    sent = []

    def gather(p):
        span = pl.ds(p * rows, rows)
        src = x_ref
        if has_outer:
            hop(x_ref, from_outer, up_send, up_recv, inner, p).wait_recv()
            acc[span] = (
                x_ref[span].astype(jnp.float32) + from_outer[span].astype(jnp.float32)
            ).astype(acc.dtype)
            src = acc
        if is_middle:
            start_all([hop(src, from_middle, mid_send, mid_recv, inner, p)], sent)
        else:
            start_all([hop(src, from_outer, up_send, up_recv, inner, p)], sent)

    def spread(p):
        span = pl.ds(p * rows, rows)
        if is_middle:
            hop(x_ref, from_middle, mid_send, mid_recv, inner, p).wait_recv()
            src = acc if has_outer else x_ref
            out_ref[span] = (
                src[span].astype(jnp.float32) + from_middle[span].astype(jnp.float32)
            ).astype(out_ref.dtype)
        else:
            hop(out_ref, out_ref, down_send, down_recv, inner, p).wait_recv()
        if has_outer:
            start_all([hop(out_ref, out_ref, down_send, down_recv, outer, p)], sent)

    lag = min(pieces, lag * (1 + 2 * to_middle)) if has_outer else pieces
    for p in range(pieces + lag):
        if p < pieces:
            gather(p)
        if p >= lag:
            spread(p - lag)
    for copy in sent:
        copy.wait_send()


def tensor_sum_kernel(n, pieces, rows, lag, x_ref, out_ref, acc, from_outer, from_middle, *sems):
    me = lax.axis_index("tensor")
    for d in range(n):

        @pl.when(me == d)
        def role():
            greet([{"tensor": at} for at in (d - 1, d + 1) if 0 <= at < n])
            middle_role(
                d, n, pieces, rows, lag, x_ref, out_ref, acc, from_outer, from_middle, sems
            )


def piece_count(rows, most):
    units = rows // ROW_TILE
    return max(p for p in range(1, most + 1) if units % p == 0)


def tensor_sum(term):
    n = lax.axis_size("tensor")
    if n == 1:
        return term
    pieces = piece_count(term.shape[0], 12)
    rows = term.shape[0] // pieces
    sem = pltpu.SemaphoreType.DMA((pieces,))
    return pl.pallas_call(
        functools.partial(tensor_sum_kernel, n, pieces, rows, 2),
        out_shape=jax.ShapeDtypeStruct(term.shape, term.dtype),
        in_specs=[VMEM],
        out_specs=VMEM,
        scratch_shapes=[pltpu.VMEM(term.shape, term.dtype)] * 3 + [sem] * 6,
        compiler_params=pltpu.CompilerParams(collective_id=0, has_side_effects=True),
        cost_estimate=link_cost(100 * term.size * term.dtype.itemsize),
        name="tensor_sum",
    )(term)


def opening_kernel(sizes, part_ref, add_ref, mod_ref, held, ctx_send, ctx_recv, col_send, col_recv):
    n_sec, n_ten, n_ctx = sizes
    sec, ten, ctx = (lax.axis_index(name) for name in ("section", "tensor", "ctx"))
    ctxs = [lax.rem(ctx + k, n_ctx) for k in range(n_ctx)]
    steps = [(a, b) for a in range(n_sec) for b in range(n_ten) if (a, b) != (0, 0)]
    places = [
        {"section": lax.rem(sec + a, n_sec), "tensor": lax.rem(ten + b, n_ten)} for a, b in steps
    ]
    greet([{"ctx": c} for c in ctxs[1:]] + places)
    sent = []

    def across(k, slot):
        return remote(
            part_ref, held.at[slot], ctx_send.at[k - 1], ctx_recv.at[k - 1], ctx=ctxs[k]
        )

    for k in range(1, n_ctx):
        start_all([across(k, ctx)], sent)
    held[ctx] = part_ref[...]
    for k in range(1, n_ctx):
        across(k, lax.rem(ctx + n_ctx - k, n_ctx)).wait_recv()
    total = add_ref[...]
    for k in range(n_ctx):
        total = total + held[k]
    mod_ref[sec, ten] = total

    def column(at, block):
        return remote(block, block, col_send.at[at], col_recv.at[at], **places[at])

    for at in range(len(steps)):
        start_all([column(at, mod_ref.at[sec, ten])], sent)
    for at, (a, b) in enumerate(steps):
        theirs = mod_ref.at[lax.rem(sec + n_sec - a, n_sec), lax.rem(ten + n_ten - b, n_ten)]
        column(at, theirs).wait_recv()
    for copy in sent:
        copy.wait_send()


def opening(part, add):
    sizes = n_sec, n_ten, n_ctx = tuple(
        lax.axis_size(name) for name in ("section", "tensor", "ctx")
    )
    dma = pltpu.SemaphoreType.DMA
    return pl.pallas_call(
        functools.partial(opening_kernel, sizes),
        out_shape=jax.ShapeDtypeStruct((n_sec, n_ten) + part.shape, part.dtype),
        in_specs=[VMEM, VMEM],
        out_specs=VMEM,
        scratch_shapes=[
            pltpu.VMEM((n_ctx,) + part.shape, part.dtype),
            dma((max(n_ctx - 1, 1),)),
            dma((max(n_ctx - 1, 1),)),
            dma((n_sec * n_ten,)),
            dma((n_sec * n_ten,)),
        ],
        compiler_params=pltpu.CompilerParams(collective_id=1, has_side_effects=True),
        name="opening",
    )(part, add)


def group_peers(n_sec, n_ctx):
    ni = inner_size(n_ctx)
    no = n_ctx // ni
    sec, ctx = lax.axis_index("section"), lax.axis_index("ctx")
    i, o = lax.rem(ctx, ni), lax.div(ctx, ni)
    far = {
        (a, b): {"section": lax.rem(sec + a, n_sec), "ctx": lax.rem(o + b, no) * ni + i}
        for a in range(n_sec)
        for b in range(no)
        if (a, b) != (0, 0)
    }
    near = {m: {"ctx": o * ni + lax.rem(i + m, ni)} for m in range(1, ni)}
    return sec, i, o, ni, no, far, near


def spread_kernel(n_sec, n_ctx, own_ref, both_ref, own_all, both_all, *sems):
    far_send, far_recv, near_send, near_recv, own_sem = sems
    sec, i, o, ni, no, far, near = group_peers(n_sec, n_ctx)
    greet(list(far.values()) + list(near.values()))
    sent = []
    me = o * ni + i

    def far_copies(step):
        a, b = step
        at = a * no + b
        copies = []
        if a == 0:
            copies.append(
                remote(
                    own_ref, own_all.at[me], far_send.at[0, at], far_recv.at[0, at], **far[step]
                )
            )
        copies.append(
            remote(
                both_ref, both_all.at[sec, me], far_send.at[1, at], far_recv.at[1, at], **far[step]
            )
        )
        return copies

    def near_copies(m, a, b, own_src, both_src, s_at, c_at):
        at = a * no + b
        copies = []
        if a == 0:
            copies.append(
                remote(
                    own_src,
                    own_all.at[c_at],
                    near_send.at[0, m - 1, at],
                    near_recv.at[0, m - 1, at],
                    **near[m],
                )
            )
        copies.append(
            remote(
                both_src,
                both_all.at[s_at, c_at],
                near_send.at[1, m - 1, at],
                near_recv.at[1, m - 1, at],
                **near[m],
            )
        )
        return copies

    for step in far:
        start_all(far_copies(step), sent)
    for m in near:
        start_all(near_copies(m, 0, 0, own_ref, both_ref, sec, me), sent)
    keep = [
        pltpu.make_async_copy(own_ref, own_all.at[me], own_sem.at[0]),
        pltpu.make_async_copy(both_ref, both_all.at[sec, me], own_sem.at[1]),
    ]
    for copy in keep:
        copy.start()
    for step in far:
        a, b = step
        for copy in far_copies(step):
            copy.wait_recv()
        s_at = lax.rem(sec + n_sec - a, n_sec)
        c_at = lax.rem(o + no - b, no) * ni + i
        for m in near:
            start_all(
                near_copies(m, a, b, own_all.at[c_at], both_all.at[s_at, c_at], s_at, c_at), sent
            )
    for m in near:
        for a in range(n_sec):
            for b in range(no):
                s_at = lax.rem(sec + n_sec - a, n_sec)
                c_at = lax.rem(o + no - b, no) * ni + lax.rem(i + ni - m, ni)
                for copy in near_copies(
                    m, a, b, own_all.at[c_at], both_all.at[s_at, c_at], s_at, c_at
                ):
                    copy.wait_recv()
    for copy in keep:
        copy.wait()
    for copy in sent:
        copy.wait_send()


def spread(own, both):
    n_sec, n_ctx = lax.axis_size("section"), lax.axis_size("ctx")
    ni = inner_size(n_ctx)
    no = n_ctx // ni
    dma = pltpu.SemaphoreType.DMA
    return pl.pallas_call(
        functools.partial(spread_kernel, n_sec, n_ctx),
        out_shape=[
            jax.ShapeDtypeStruct((n_ctx,) + own.shape, own.dtype),
            jax.ShapeDtypeStruct((n_sec, n_ctx) + both.shape, both.dtype),
        ],
        in_specs=[VMEM, VMEM],
        out_specs=[VMEM, VMEM],
        scratch_shapes=[
            dma((2, n_sec * no)),
            dma((2, n_sec * no)),
            dma((2, ni, n_sec * no)),
            dma((2, ni, n_sec * no)),
            dma((2,)),
        ],
        compiler_params=pltpu.CompilerParams(collective_id=2, has_side_effects=True),
        name="spread",
    )(own, both)


def owner_kernel(n_sec, n_ctx, own_ref, both_ref, own_out, both_out, *refs):
    own_pair, both_pair, own_far, both_far = refs[:4]
    far_send, far_recv, near_send, near_recv = refs[4:]
    sec, i, o, ni, no, far, near = group_peers(n_sec, n_ctx)
    greet(list(far.values()) + list(near.values()))
    sent = []

    def near_copies(m, a, b):
        to = lax.rem(i + m, ni)
        s_at, o_at = lax.rem(sec + a, n_sec), lax.rem(o + b, no)
        at = a * no + b
        copies = []
        if a == 0:
            copies.append(
                remote(
                    own_ref.at[o_at * ni + to],
                    own_pair.at[m - 1, b],
                    near_send.at[0, m - 1, at],
                    near_recv.at[0, m - 1, at],
                    **near[m],
                )
            )
        copies.append(
            remote(
                both_ref.at[s_at, o_at * ni + to],
                both_pair.at[m - 1, at],
                near_send.at[1, m - 1, at],
                near_recv.at[1, m - 1, at],
                **near[m],
            )
        )
        return copies

    order = list(far) + [(0, 0)]
    for step in order:
        for m in near:
            start_all(near_copies(m, *step), sent)

    def far_copies(a, b):
        at = a * no + b
        copies = []
        if a == 0:
            copies.append(
                remote(
                    own_pair.at[ni - 1, b],
                    own_far.at[b],
                    far_send.at[0, at],
                    far_recv.at[0, at],
                    **far[(a, b)],
                )
            )
        copies.append(
            remote(
                both_pair.at[ni - 1, at],
                both_far.at[at],
                far_send.at[1, at],
                far_recv.at[1, at],
                **far[(a, b)],
            )
        )
        return copies

    for a, b in order:
        s_at, c_at = lax.rem(sec + a, n_sec), lax.rem(o + b, no) * ni + i
        at = a * no + b
        for m in near:
            for copy in near_copies(m, a, b):
                copy.wait_recv()
        total_both = both_ref[s_at, c_at].astype(jnp.float32)
        for m in near:
            total_both = total_both + both_pair[m - 1, at].astype(jnp.float32)
        total_own = None
        if a == 0:
            total_own = own_ref[c_at].astype(jnp.float32)
            for m in near:
                total_own = total_own + own_pair[m - 1, b].astype(jnp.float32)
        if (a, b) == (0, 0):
            own_out[...] = total_own
            both_out[...] = total_both
        else:
            if a == 0:
                own_pair[ni - 1, b] = total_own.astype(own_pair.dtype)
            both_pair[ni - 1, at] = total_both.astype(both_pair.dtype)
            start_all(far_copies(a, b), sent)
    for a, b in far:
        for copy in far_copies(a, b):
            copy.wait_recv()
        if a == 0:
            own_out[...] += own_far[b].astype(jnp.float32)
        both_out[...] += both_far[a * no + b].astype(jnp.float32)
    for copy in sent:
        copy.wait_send()


def owner_sum(own, both):
    n_sec, n_ctx = lax.axis_size("section"), lax.axis_size("ctx")
    ni = inner_size(n_ctx)
    no = n_ctx // ni
    dma = pltpu.SemaphoreType.DMA
    own_shape, both_shape = own.shape[1:], both.shape[2:]
    return pl.pallas_call(
        functools.partial(owner_kernel, n_sec, n_ctx),
        out_shape=[
            jax.ShapeDtypeStruct(own_shape, jnp.float32),
            jax.ShapeDtypeStruct(both_shape, jnp.float32),
        ],
        in_specs=[VMEM, VMEM],
        out_specs=[VMEM, VMEM],
        scratch_shapes=[
            pltpu.VMEM((ni, no) + own_shape, own.dtype),
            pltpu.VMEM((ni, n_sec * no) + both_shape, both.dtype),
            pltpu.VMEM((no,) + own_shape, own.dtype),
            pltpu.VMEM((n_sec * no,) + both_shape, both.dtype),
            dma((2, n_sec * no)),
            dma((2, n_sec * no)),
            dma((2, ni, n_sec * no)),
            dma((2, ni, n_sec * no)),
        ],
        compiler_params=pltpu.CompilerParams(collective_id=3, has_side_effects=True),
        name="owner_sum",
    )(own, both)


def small_kernel(axes, sizes, x_ref, out_ref, held, send, recv):
    at = [lax.axis_index(name) for name in axes]
    steps = [(a, b) for a in range(sizes[0]) for b in range(sizes[1])]
    places = [
        [lax.rem(here + sign * step + size, size) for here, step, size in zip(at, pair, sizes)]
        for sign in (1, -1)
        for pair in steps
    ]
    to, source = places[: len(steps)], places[len(steps) :]
    where = [dict(zip(axes, place)) for place in to]
    greet(where[1:])

    def block(place):
        return place[0] if x_ref.shape[0] > 1 else 0

    def copy(k, slot):
        return remote(
            x_ref.at[block(to[k])],
            held.at[slot[0] * sizes[1] + slot[1]],
            send.at[k - 1],
            recv.at[k - 1],
            **where[k],
        )

    copies = [copy(k, at) for k in range(1, len(steps))]
    for started in copies:
        started.start()
    held[at[0] * sizes[1] + at[1]] = x_ref[block(at)]
    for k in range(1, len(steps)):
        copy(k, source[k]).wait_recv()
    total = held[0]
    for k in range(1, len(steps)):
        total = total + held[k]
    out_ref[...] = total
    for started in copies:
        started.wait_send()


def small_sum(x, axes, collective_id):
    sizes = tuple(lax.axis_size(name) for name in axes)
    n = sizes[0] * sizes[1]
    dma = pltpu.SemaphoreType.DMA((max(n - 1, 1),))
    return pl.pallas_call(
        functools.partial(small_kernel, axes, sizes),
        out_shape=jax.ShapeDtypeStruct(x.shape[1:], x.dtype),
        in_specs=[VMEM],
        out_specs=VMEM,
        scratch_shapes=[pltpu.VMEM((n,) + x.shape[1:], x.dtype), dma, dma],
        compiler_params=pltpu.CompilerParams(collective_id=collective_id, has_side_effects=True),
        name="small_sum",
    )(x)


def packed(pieces, width):
    flat = jnp.concatenate([p.reshape(-1) for p in pieces])
    rows = -(-flat.shape[0] // width)
    rows = -(-rows // 8) * 8
    return jnp.pad(flat, (0, rows * width - flat.shape[0])).reshape(rows, width)


def unpacked(block, shapes):
    flat, at, out = block.reshape(-1), 0, []
    for shape in shapes:
        size = math.prod(shape)
        out.append(flat[at : at + size].reshape(shape))
        at += size
    return out


def layer_norm(values):
    centre = jnp.mean(values, axis=-1, keepdims=True)
    centred = values - centre
    variance = jnp.mean(centred * centred, axis=-1, keepdims=True)
    inverse = lax.rsqrt(variance + EPSILON)
    return (centred * inverse, inverse)


def norm_back(normed, inverse, upstream):
    mean_grad = jnp.mean(upstream, axis=-1, keepdims=True)
    mean_cross = jnp.mean(upstream * normed, axis=-1, keepdims=True)
    return inverse * (upstream - mean_grad - normed * mean_cross)


def gelu_back(pre_act, upstream):
    unused_out, pullback = jax.vjp(
        lambda pre_value: jax.nn.gelu(pre_value, approximate=True), pre_act
    )
    return pullback(upstream)[0]


def heads(array):
    cols = array.shape[-2]
    return array.reshape(*array.shape[:-2], cols // HD, HD, array.shape[-1])


def score_columns(queries, keys):
    softmax_scale = 1.0 / math.sqrt(HD)
    return (
        jnp.einsum(
            "nhdk,hdq->hnkq", heads(keys), heads(queries), preferred_element_type=jnp.float32
        )
        * softmax_scale
    )


def attend(queries, keys, values):
    scores = score_columns(queries, keys)
    row_peak = jnp.max(scores, axis=(1, 2), keepdims=True)
    log_total = row_peak + jnp.log(jnp.sum(jnp.exp(scores - row_peak), axis=(1, 2), keepdims=True))
    prob_bf = jnp.exp(scores - log_total).astype(jnp.bfloat16)
    context = jnp.einsum(
        "nhdk,hnkq->hdq", heads(values), prob_bf, preferred_element_type=jnp.float32
    )
    return context.astype(jnp.bfloat16).reshape(queries.shape), log_total


def attention_grads(queries, keys, values, log_total, context, context_grad):
    softmax_scale = 1.0 / math.sqrt(HD)
    query_heads, grad_heads = heads(queries), heads(context_grad)
    delta = jnp.sum(
        grad_heads.astype(jnp.float32) * heads(context).astype(jnp.float32), axis=1
    )[:, None, None, :]
    prob_full = jnp.exp(score_columns(queries, keys) - log_total)
    prob_bf = prob_full.astype(jnp.bfloat16)
    prob_grad = jnp.einsum(
        "nhdk,hdq->hnkq", heads(values), grad_heads, preferred_element_type=jnp.float32
    )
    score_grad = (prob_full * (prob_grad - delta)).astype(jnp.bfloat16)
    query_grad = (
        jnp.einsum(
            "nhdk,hnkq->hdq", heads(keys), score_grad, preferred_element_type=jnp.float32
        )
        * softmax_scale
    ).reshape(queries.shape)
    key_part = (
        jnp.einsum("hnkq,hdq->nhdk", score_grad, query_heads, preferred_element_type=jnp.float32)
        * softmax_scale
    ).reshape(keys.shape)
    value_part = jnp.einsum(
        "hnkq,hdq->nhdk", prob_bf, grad_heads, preferred_element_type=jnp.float32
    ).reshape(values.shape)
    both = jnp.concatenate(
        [key_part.astype(jnp.bfloat16), value_part.astype(jnp.bfloat16)], axis=1
    )
    return query_grad, both


def contract(left, right, left_dim, right_dim):
    return lax.dot_general(
        left, right, (((left_dim,), (right_dim,)), ((), ())), preferred_element_type=jnp.float32
    )


class Rows:
    def __init__(self, latents, section):
        n_sec = lax.axis_size("section")
        self.n_sec = n_sec
        total, self.tokens, self.width = latents.shape
        self.section = section
        self.full = total // n_sec
        self.rest = total - self.full * n_sec
        self.part = self.tokens // n_sec
        self.own_rows = self.full * self.tokens
        self.both_rows = self.rest * self.part
        self.rows = self.own_rows + self.both_rows

    def take(self, array):
        own = lax.dynamic_slice_in_dim(array, self.section * self.full, self.full, 0)
        both = lax.dynamic_slice_in_dim(
            array[self.full * self.n_sec :], self.section * self.part, self.part, 1
        )
        return jnp.concatenate(
            [own.reshape(self.own_rows, -1), both.reshape(self.both_rows, -1)], axis=0
        )

    def split(self, array):
        return (
            array[: self.own_rows].reshape(self.full, self.tokens, -1),
            array[self.own_rows :].reshape(self.rest, self.part, -1),
        )

    def spans(self):
        out = [(at * self.tokens, self.tokens) for at in range(self.full)]
        return out + [
            (self.own_rows + at * self.part, self.part) for at in range(self.rest)
        ]

    def columns(self, array):
        return [array[:, start : start + size] for start, size in self.spans()]

    def mods(self, modulation):
        own = lax.dynamic_slice_in_dim(modulation, self.section * self.full, self.full, 0)
        return jnp.concatenate([own, modulation[self.full * self.n_sec :]], axis=0)

    def wide(self, pieces):
        row = lax.broadcasted_iota(jnp.int32, (self.rows, 1), 0)
        out = pieces[-1][None, :]
        for (start, size), piece in reversed(list(zip(self.spans(), pieces))[:-1]):
            out = jnp.where(row < start + size, piece[None, :], out)
        return out

    def sums(self, array):
        return jnp.stack([jnp.sum(array[a : a + b], axis=0) for a, b in self.spans()])

    def placed(self, sums):
        total = self.full * self.n_sec + self.rest
        whole = jnp.zeros((total,) + sums.shape[1:], sums.dtype)
        whole = lax.dynamic_update_slice_in_dim(
            whole, sums[: self.full], self.section * self.full, 0
        )
        return lax.dynamic_update_slice_in_dim(
            whole, sums[self.full :], self.full * self.n_sec, 0
        )

    def assembled(self, per_block, received):
        own = per_block[-1]
        for b in range(self.n_sec - 1):
            own = jnp.where(self.section == b, per_block[b], own)
        out = jnp.zeros(
            (self.full * self.n_sec + self.rest, self.tokens, self.width), own.dtype
        )
        for k in range(self.n_sec):
            rows = own
            if k:
                rows = received[-1][k - 1]
                for b in range(self.n_sec - 1):
                    rows = jnp.where(self.section == b, received[b][k - 1], rows)
            source = lax.rem(self.section + k, self.n_sec)
            first, both = self.split(rows)
            out = lax.dynamic_update_slice_in_dim(out, first, source * self.full, 0)
            out = lax.dynamic_update_slice(
                out, both, (self.full * self.n_sec, source * self.part, 0)
            )
        return out


def gathered(key_value, rows):
    spans = rows.spans()
    cols = [key_value[:, start : start + size] for start, size in spans]
    own = jnp.concatenate(cols[: rows.full], axis=0)
    both = jnp.concatenate(cols[rows.full :], axis=0)
    own_all, both_all = spread(own, both)
    both_all = both_all.reshape(-1, *both.shape)
    high = key_value.shape[0]
    return [own_all[:, at * high : (at + 1) * high] for at in range(rows.full)] + [
        both_all[:, at * high : (at + 1) * high] for at in range(rows.rest)
    ]


def returned(parts, rows):
    high = parts[0].shape[1]
    own = jnp.concatenate(parts[: rows.full], axis=1)
    both = jnp.concatenate(parts[rows.full :], axis=1)
    own, both = owner_sum(own, both.reshape(rows.n_sec, -1, *both.shape[1:]))
    return jnp.concatenate(
        [own[at * high : (at + 1) * high] for at in range(rows.full)]
        + [both[at * high : (at + 1) * high] for at in range(rows.rest)],
        axis=1,
    )


def forward_block(rows, residual, mods, attn_weights, biases, sends, mlp_weights):
    w_qkv, w_out = attn_weights
    b_qv, b_out, b_fc1, b_fc2 = biases
    local_cols = w_qkv.shape[-1] // 3
    shift_a, scale_a, gate_a, shift_m, scale_m, gate_m = (
        rows.wide([mods[at, k] for at in range(mods.shape[0])]) for k in range(6)
    )
    normed_a, inverse_a = layer_norm(residual)
    attn_in = (normed_a * (1.0 + scale_a) + shift_a).astype(jnp.bfloat16)
    projected = contract(w_qkv, attn_in, 0, 1)
    bias = jnp.concatenate([b_qv[0], jnp.zeros_like(b_qv[0]), b_qv[1]])
    projected = (projected + bias[:, None]).astype(jnp.bfloat16)
    queries = rows.columns(projected[:local_cols])
    keys_values = gathered(projected[local_cols:], rows)
    attended = [
        attend(q, kv[:, :local_cols], kv[:, local_cols:])
        for q, kv in zip(queries, keys_values)
    ]
    context = jnp.concatenate([c for c, _ in attended], axis=1)
    attn_term = contract(context, w_out, 0, 0)
    attn_sum, moved = beside(tensor_sum, [attn_term.astype(jnp.bfloat16)], sends)
    w_fc1, w_fc2 = mlp_weights(moved)
    attn_out = attn_sum.astype(jnp.float32) + b_out
    middle = residual + gate_a * attn_out
    normed_m, inverse_m = layer_norm(middle)
    mlp_in = (normed_m * (1.0 + scale_m) + shift_m).astype(jnp.bfloat16)
    pre_act = jnp.dot(mlp_in, w_fc1, preferred_element_type=jnp.float32) + b_fc1
    hidden = jax.nn.gelu(pre_act, approximate=True).astype(jnp.bfloat16)
    mlp_term = jnp.dot(hidden, w_fc2, preferred_element_type=jnp.float32)
    mlp_out = tensor_sum(mlp_term.astype(jnp.bfloat16)).astype(jnp.float32) + b_fc2
    block_res = (middle + gate_m * mlp_out).astype(jnp.bfloat16)
    stored = (
        normed_a,
        inverse_a,
        attn_in,
        queries,
        keys_values,
        [log_total for _, log_total in attended],
        context,
        attn_out,
        normed_m,
        inverse_m,
        mlp_in,
        pre_act,
        hidden,
        mlp_out,
    )
    return block_res, stored, moved


def backward_block(rows, upstream, stored, mods, weights, block, first_sends, second_sends):
    w_qkv, w_out, w_fc1, w_fc2 = weights
    (
        normed_a,
        inverse_a,
        attn_in,
        queries,
        keys_values,
        log_totals,
        context,
        attn_out,
        normed_m,
        inverse_m,
        mlp_in,
        pre_act,
        hidden,
        mlp_out,
    ) = stored
    local_cols = w_qkv.shape[-1] // 3
    shift_a, scale_a, gate_a, shift_m, scale_m, gate_m = (
        rows.wide([mods[at, k] for at in range(mods.shape[0])]) for k in range(6)
    )
    gate_m_grad = rows.sums(upstream * mlp_out)
    mlp_grad = upstream * gate_m
    mlp_grad_b = mlp_grad.astype(jnp.bfloat16)
    grad_b2 = jnp.sum(mlp_grad, axis=0)
    pre_grad = gelu_back(pre_act, jnp.dot(mlp_grad_b, w_fc2.T, preferred_element_type=jnp.float32))
    pre_grad_b = pre_grad.astype(jnp.bfloat16)
    grad_b1 = jnp.sum(pre_grad, axis=0)
    mlp_pair = inner_pair(
        per_owner(contract(mlp_grad_b, hidden, 0, 0), contract(mlp_in, pre_grad_b, 0, 0)), 1
    )
    mlp_term = jnp.dot(pre_grad_b, w_fc1.T, preferred_element_type=jnp.float32)
    outer = outer_sends(mlp_pair)
    mlp_in_grad, moved = beside(
        tensor_sum, [mlp_term.astype(jnp.bfloat16)], outer + first_sends
    )
    first_moved = moved[len(outer) :]
    mlp_share = outer_total(mlp_pair, moved[: len(outer)])
    mlp_in_grad = mlp_in_grad.astype(jnp.float32)
    shift_m_grad = rows.sums(mlp_in_grad)
    scale_m_grad = rows.sums(mlp_in_grad * normed_m)
    middle_grad = upstream + norm_back(normed_m, inverse_m, mlp_in_grad * (1.0 + scale_m))
    gate_a_grad = rows.sums(middle_grad * attn_out)
    attn_grad = middle_grad * gate_a
    attn_grad_b = attn_grad.astype(jnp.bfloat16)
    grad_bo = jnp.sum(attn_grad, axis=0)
    context_grad = contract(w_out, attn_grad_b, 1, 1).astype(jnp.bfloat16)
    query_grads, key_value_parts = zip(
        *(
            attention_grads(q, kv[:, :local_cols], kv[:, local_cols:], log_total, c, cg)
            for q, kv, log_total, c, cg in zip(
                queries, keys_values, log_totals, rows.columns(context), rows.columns(context_grad)
            )
        )
    )
    query_grad = jnp.concatenate(query_grads, axis=1)
    key_value_grad = returned(key_value_parts, rows)
    grad_bqv = jnp.stack(
        [jnp.sum(query_grad, axis=1), jnp.sum(key_value_grad[local_cols:], axis=1)]
    )
    qkv_grad_b = jnp.concatenate([query_grad, key_value_grad], axis=0).astype(jnp.bfloat16)
    attn_pair = inner_pair(
        per_owner(contract(attn_in, qkv_grad_b, 0, 1), contract(attn_grad_b, context, 0, 1)), 2
    )
    attn_term = contract(qkv_grad_b, w_qkv, 0, 1)
    outer, across = outer_sends(attn_pair), block_sends(mlp_share, block)
    attn_in_grad, moved = beside(
        tensor_sum, [attn_term.astype(jnp.bfloat16)], outer + across + second_sends
    )
    attn_share = outer_total(attn_pair, moved[: len(outer)])
    mlp_share = block_total(mlp_share, moved[len(outer) : len(outer) + len(across)])
    second_moved = moved[len(outer) + len(across) :]
    attn_in_grad = attn_in_grad.astype(jnp.float32)
    shift_a_grad = rows.sums(attn_in_grad)
    scale_a_grad = rows.sums(attn_in_grad * normed_a)
    input_grad = middle_grad + norm_back(normed_a, inverse_a, attn_in_grad * (1.0 + scale_a))
    mod_grad = jnp.concatenate(
        [shift_a_grad, scale_a_grad, gate_a_grad, shift_m_grad, scale_m_grad, gate_m_grad], axis=1
    )
    return (
        input_grad,
        mod_grad,
        (grad_bqv, grad_bo, grad_b1, grad_b2),
        (mlp_share, attn_share),
        first_moved,
        second_moved,
    )


def per_owner(*terms):
    n = lax.axis_size("ctx")
    return [t.reshape(n, -1, t.shape[-1]) for t in terms]


def to_inner(value, by):
    n = lax.axis_size("ctx")
    ni = inner_size(n)
    return lax.ppermute(value, "ctx", [(a, a // ni * ni + (a + by) % ni) for a in range(n)])


def to_outer(value, by):
    n = lax.axis_size("ctx")
    ni = inner_size(n)
    return lax.ppermute(value, "ctx", [(a, (a + by * ni) % n) for a in range(n)])


def to_section(value, by):
    n = lax.axis_size("section")
    return lax.ppermute(value, "section", [(a, (a + by) % n) for a in range(n)])


def to_block(value, block, by):
    n = lax.axis_size("section")
    return lax.ppermute(value, "section", [((block + by) % n, block)])


def ctx_place():
    n = lax.axis_size("ctx")
    ni = inner_size(n)
    at = lax.axis_index("ctx")
    return n // ni, ni, lax.div(at, ni), lax.rem(at, ni)


def beside(kernel, args, sends):
    args, values = lax.optimization_barrier((args, [value for value, _ in sends]))
    moved = [move(value) for value, (_, move) in zip(values, sends)]
    return lax.optimization_barrier((kernel(*args), moved))


def half_of(weights):
    _, ni, _, i = ctx_place()
    sizes = [w.shape[0] // ni for w in weights]
    return jnp.concatenate(
        [lax.dynamic_slice_in_dim(w, i * size, size, 0) for w, size in zip(weights, sizes)]
    )


def joined(own, passed, weights):
    _, ni, _, i = ctx_place()
    found, start = [], 0
    for w in weights:
        size = w.shape[0] // ni
        parts = [piece[start : start + size] for piece in [own] + passed]
        start += size
        ordered = []
        for at in range(ni):
            piece = parts[0]
            for m in range(1, ni):
                piece = jnp.where(lax.rem(i + ni - m, ni) == at, parts[m], piece)
            ordered.append(piece)
        found.append(jnp.concatenate(ordered))
    return found


def chosen_blocks(weights, others):
    n_sec = lax.axis_size("section")
    section = lax.axis_index("section")
    blocks = []
    for b in range(n_sec):
        chosen = list(weights)
        for k, found in enumerate(others, 1):
            is_source = lax.rem(section + n_sec - k, n_sec) == b
            chosen = [jnp.where(is_source, new, old) for new, old in zip(found, chosen)]
        blocks.append(chosen)
    return blocks


def fetched(weights):
    n_sec = lax.axis_size("section")
    groups = [
        [at for at, w in enumerate(weights) if w.shape[1] == width]
        for width in sorted({w.shape[1] for w in weights})
    ]
    halves = [half_of([weights[at] for at in group]) for group in groups]
    return groups, [[to_section(half, k) for k in range(1, n_sec)] for half in halves]


def passing(fetch):
    _, ni, _, _ = ctx_place()
    return [
        (half, functools.partial(to_inner, by=m))
        for of_group in fetch[1]
        for half in of_group
        for m in range(1, ni)
    ]


def every_block(weights, fetch, passed):
    _, ni, _, _ = ctx_place()
    n_sec = lax.axis_size("section")
    others = [[None] * len(weights) for _ in range(n_sec - 1)]
    passed = list(passed)
    for group, of_group in zip(*fetch):
        for k, half in enumerate(of_group):
            rest = [passed.pop(0) for _ in range(1, ni)]
            for at, whole in zip(group, joined(half, rest, [weights[at] for at in group])):
                others[k][at] = whole
    return chosen_blocks(weights, others)


def inner_pair(terms, axis):
    no, ni, _, i = ctx_place()
    terms = [t.astype(jnp.bfloat16).reshape(no, ni, -1, t.shape[-1]) for t in terms]

    def inner(at):
        return jnp.concatenate(
            [lax.dynamic_index_in_dim(t, at, 1, keepdims=False) for t in terms], axis=axis
        )

    pair = inner(i).astype(jnp.float32)
    for m in range(1, ni):
        pair = pair + to_inner(inner(lax.rem(i + m, ni)), m).astype(jnp.float32)
    return pair.astype(jnp.bfloat16)


def outer_sends(pair):
    no, _, o, _ = ctx_place()
    return [
        (
            lax.dynamic_index_in_dim(pair, lax.rem(o + m, no), 0, keepdims=False),
            functools.partial(to_outer, by=m),
        )
        for m in range(1, no)
    ]


def outer_total(pair, moved):
    _, _, o, _ = ctx_place()
    total = lax.dynamic_index_in_dim(pair, o, 0, keepdims=False).astype(jnp.float32)
    for piece in moved:
        total = total + piece.astype(jnp.float32)
    return total


def block_sends(value, block):
    value = value.astype(jnp.bfloat16)
    return [
        (value, functools.partial(to_block, block=block, by=k))
        for k in range(1, lax.axis_size("section"))
    ]


def block_total(own, moved):
    for piece in moved:
        own = own + piece.astype(jnp.float32)
    return own


def local(
    latents,
    condition,
    cotangent,
    w_ada,
    b_ada,
    w_qkv,
    b_qv,
    w_out,
    b_out,
    w_fc1,
    b_fc1,
    w_fc2,
    b_fc2,
):
    section = lax.axis_index("section")
    n_sec = lax.axis_size("section")
    latent_total, token_count, width = latents.shape
    width_cols = b_ada.shape[-1]
    local_cols = w_qkv.shape[-1]
    rows = Rows(latents, section)
    cond_act = jax.nn.silu(condition).astype(jnp.bfloat16)
    mod_part = jnp.dot(cond_act, w_ada[0], preferred_element_type=jnp.float32)
    bias_shapes = [b_qv.shape[1:], b_out.shape[1:], b_fc1.shape[1:], b_fc2.shape[1:]]
    bias_rows = packed([b_qv, b_out, b_fc1, b_fc2], width_cols)
    add = jnp.concatenate(
        [jnp.broadcast_to(b_ada, (latent_total, width_cols)), bias_rows], axis=0
    )
    height = -(-add.shape[0] // 8) * 8
    add = jnp.pad(add, ((0, height - add.shape[0]), (0, 0)))
    attn_weights = [w_qkv[0].reshape(width, 3 * local_cols), w_out[0]]
    mlp_weights = [w_fc1[0], w_fc2[0]]
    attn_fetch = fetched(attn_weights)
    mod_all = opening(jnp.pad(mod_part, ((0, height - latent_total), (0, 0))), add)
    mod_all, mlp_weights = lax.optimization_barrier((mod_all, mlp_weights))
    attn_blocks = every_block(
        attn_weights, attn_fetch, [move(half) for half, move in passing(attn_fetch)]
    )
    mlp_fetch = fetched(mlp_weights)
    tensor = lax.axis_index("tensor")
    modulation = jnp.swapaxes(mod_all[:, :, :latent_total], 1, 2).reshape(
        n_sec, latent_total, 6, width
    )
    own_cols = lax.dynamic_index_in_dim(mod_all, tensor, 1, keepdims=False)
    biases, mods = [], []
    for b in range(n_sec):
        biases.append(unpacked(own_cols[b, latent_total:], bias_shapes))
        mods.append(rows.mods(modulation[b]))
    residual = rows.take(latents)
    outs, out_moved, kept, mlp_blocks = [], [], [], []
    for b in range(n_sec):
        if b == 0:
            sends = passing(mlp_fetch)

            def finish(moved):
                mlp_blocks.extend(every_block(mlp_weights, mlp_fetch, moved))
                return mlp_blocks[0]

        else:
            sends = block_sends(outs[-1], b - 1)

            def finish(moved, b=b):
                return mlp_blocks[b]

        residual, stored, moved = forward_block(
            rows, residual.astype(jnp.float32), mods[b], attn_blocks[b], biases[b], sends, finish
        )
        if b:
            out_moved.append(moved)
        outs.append(residual)
        kept.append(stored)
    upstream = rows.take(cotangent).astype(jnp.float32)
    in_grads, in_moved, small, shares = ([None] * n_sec for _ in range(4))
    first, second = block_sends(outs[-1], n_sec - 1), []
    for b in reversed(range(n_sec)):
        upstream, mod_grad, bias_grads, shares[b], first_moved, second_moved = backward_block(
            rows,
            upstream,
            kept[b],
            mods[b],
            (*attn_blocks[b], *mlp_blocks[b]),
            b,
            first,
            second,
        )
        if b == n_sec - 1:
            out_moved.append(first_moved)
        else:
            shares[b + 1] = (shares[b + 1][0], block_total(shares[b + 1][1], first_moved))
            in_moved[b + 1] = second_moved
        in_grads[b] = upstream.astype(jnp.bfloat16)
        mod_cols = lax.dynamic_slice_in_dim(mod_grad, tensor * width_cols, width_cols, 1)
        small[b] = packed([rows.placed(mod_cols), *bias_grads], width)
        first, second = block_sends(shares[b][1], b), block_sends(in_grads[b], b)
    block_out = rows.assembled(outs, out_moved)
    last = first + second
    summed, last_values = lax.optimization_barrier(
        (small_sum(jnp.stack(small), ("section", "ctx"), 4), [value for value, _ in last])
    )
    moved = [move(value) for value, (_, move) in zip(last_values, last)]
    shares[0] = (shares[0][0], block_total(shares[0][1], moved[: len(first)]))
    in_moved[0] = moved[len(first) :]
    in_grad = rows.assembled(in_grads, in_moved).astype(jnp.float32)

    def mine(which):
        out = shares[-1][which]
        for b in range(n_sec - 1):
            out = jnp.where(section == b, shares[b][which], out)
        return out

    mlp_share, attn_share = mine(0), mine(1)
    share_rows = mlp_share.shape[0] // 2
    mod_total, grad_bqv, grad_bo, grad_b1, grad_b2 = unpacked(
        summed, [(latent_total, width_cols)] + bias_shapes
    )
    mod_rounded = mod_total.astype(jnp.bfloat16)
    grad_w_ada = jnp.dot(cond_act.T, mod_rounded, preferred_element_type=jnp.float32)[None]
    grad_b_ada = jnp.sum(mod_total, axis=0)[None]
    cond_part = jnp.dot(mod_rounded, w_ada[0].T, preferred_element_type=jnp.float32)
    cond_part = jnp.pad(cond_part, ((0, -latent_total % 8), (0, 0)))
    cond_sum = small_sum(cond_part[None], ("section", "tensor"), 5)[:latent_total]
    sigmoid_c = jax.nn.sigmoid(condition)
    cond_grad = cond_sum * sigmoid_c * (1.0 + condition * (1.0 - sigmoid_c))
    return (
        block_out[None],
        in_grad[None],
        cond_grad,
        grad_w_ada,
        grad_b_ada,
        attn_share[:, : 3 * local_cols].reshape(1, share_rows, 3, local_cols),
        grad_bqv[None],
        attn_share[:, 3 * local_cols :].T[None],
        grad_bo[None],
        mlp_share[share_rows:][None],
        grad_b1[None],
        mlp_share[:share_rows].T[None],
        grad_b2[None],
    )


def solution(mesh):
    return jax.shard_map(
        local,
        mesh=mesh,
        in_specs=(
            P(None, "ctx", None),
            P(None, "ctx"),
            P(None, "ctx", None),
            P("section", "ctx", "tensor"),
            P("section", "tensor"),
            P("section", None, None, "tensor"),
            P("section", None, "tensor"),
            P("section", "tensor", None),
            P("section", None),
            P("section", None, "tensor"),
            P("section", "tensor"),
            P("section", "tensor", None),
            P("section", None),
        ),
        out_specs=(
            P("section", None, "ctx", None),
            P("section", None, "ctx", None),
            P(None, "ctx"),
            P("section", "ctx", "tensor"),
            P("section", "tensor"),
            P("section", "ctx", None, "tensor"),
            P("section", None, "tensor"),
            P("section", "tensor", "ctx"),
            P("section", None),
            P("section", "ctx", "tensor"),
            P("section", "tensor"),
            P("section", "tensor", "ctx"),
            P("section", None),
        ),
        check_vma=False,
    )
```

```python
import functools
import math

import jax
import jax.numpy as jnp
from jax import lax
from jax.experimental import pallas as pl
from jax.experimental.pallas import tpu as pltpu
from jax.sharding import PartitionSpec as P

HD = 72
EPSILON = 1e-06
MESH = pl.DeviceIdType.MESH
ROW_TILE = 16
VMEM = pl.BlockSpec(memory_space=pltpu.VMEM)


def inner_size(n):
    return 2 if n % 2 == 0 else 1


def remote(src, dst, send, recv, **to):
    return pltpu.make_async_remote_copy(
        src_ref=src,
        dst_ref=dst,
        send_sem=send,
        recv_sem=recv,
        device_id=to,
        device_id_type=MESH,
    )


def greet(peers):
    barrier = pltpu.get_barrier_semaphore()
    for peer in peers:
        pl.semaphore_signal(barrier, inc=1, device_id=peer, device_id_type=MESH)
    pl.semaphore_wait(barrier, len(peers))


def link_cost(moved):
    return pl.CostEstimate(flops=0, bytes_accessed=moved, transcendentals=0)


def start_all(copies, sent):
    for copy in copies:
        copy.start()
        sent.append(copy)


def middle_role(d, n, pieces, rows, lag, x_refs, out_refs, acc, from_outer, from_middle, sems):
    up_send, up_recv, mid_send, mid_recv, down_send, down_recv = sems
    half = n // 2
    left = d < half
    outer, inner = (d - 1, d + 1) if left else (d + 1, d - 1)
    has_outer = 0 <= outer < n
    is_middle = d in (half - 1, half)
    to_middle = half - 1 - d if left else d - half
    each = pieces // len(x_refs)

    def term(refs, p):
        return refs[p // each].at[pl.ds(p % each * rows, rows)]

    def held(ref, p):
        return ref.at[pl.ds(p * rows, rows)]

    def hop(src, dst, send, recv, to, p):
        return remote(src, dst, send.at[p], recv.at[p], tensor=to)

    sent = []

    def gather(p):
        x, kept, came = term(x_refs, p), held(acc, p), held(from_outer, p)
        src = x
        if has_outer:
            hop(x, came, up_send, up_recv, inner, p).wait_recv()
            kept[...] = (x[...].astype(jnp.float32) + came[...].astype(jnp.float32)).astype(
                acc.dtype
            )
            src = kept
        if is_middle:
            start_all([hop(src, held(from_middle, p), mid_send, mid_recv, inner, p)], sent)
        else:
            start_all([hop(src, came, up_send, up_recv, inner, p)], sent)

    def spread_out(p):
        out, came = term(out_refs, p), held(from_middle, p)
        if is_middle:
            src = held(acc, p) if has_outer else term(x_refs, p)
            hop(src, came, mid_send, mid_recv, inner, p).wait_recv()
            out[...] = (src[...].astype(jnp.float32) + came[...].astype(jnp.float32)).astype(
                acc.dtype
            )
        else:
            hop(out, out, down_send, down_recv, inner, p).wait_recv()
        if has_outer:
            start_all([hop(out, out, down_send, down_recv, outer, p)], sent)

    lag = min(pieces, lag * (1 + 2 * to_middle)) if has_outer else pieces
    for p in range(pieces + lag):
        if p < pieces:
            gather(p)
        if p >= lag:
            spread_out(p - lag)
    for copy in sent:
        copy.wait_send()


def tensor_sum_kernel(n, count, pieces, rows, lag, *refs):
    x_refs, out_refs = refs[:count], refs[count : 2 * count]
    acc, from_outer, from_middle = refs[2 * count : 2 * count + 3]
    sems = refs[2 * count + 3 :]
    me = lax.axis_index("tensor")
    for d in range(n):

        @pl.when(me == d)
        def role():
            greet([{"tensor": at} for at in (d - 1, d + 1) if 0 <= at < n])
            middle_role(
                d, n, pieces, rows, lag, x_refs, out_refs, acc, from_outer, from_middle, sems
            )


def piece_count(rows, most):
    units = rows // ROW_TILE
    return max(p for p in range(1, most + 1) if units % p == 0)


def tensor_sum(*terms):
    n = lax.axis_size("tensor")
    if n == 1:
        return list(terms)
    count = len(terms)
    shape, dtype = terms[0].shape, terms[0].dtype
    each = piece_count(shape[0], 12)
    rows = shape[0] // each
    pieces = each * count
    sem = pltpu.SemaphoreType.DMA((pieces,))
    return pl.pallas_call(
        functools.partial(tensor_sum_kernel, n, count, pieces, rows, 2),
        out_shape=[jax.ShapeDtypeStruct(shape, dtype)] * count,
        in_specs=[VMEM] * count,
        out_specs=[VMEM] * count,
        scratch_shapes=[pltpu.VMEM((shape[0] * count, shape[1]), dtype)] * 3 + [sem] * 6,
        compiler_params=pltpu.CompilerParams(
            collective_id=0 if count == 1 else 6, has_side_effects=True
        ),
        cost_estimate=link_cost(100 * count * terms[0].size * dtype.itemsize),
        name="tensor_sum",
    )(*terms)


def opening_kernel(sizes, part_ref, add_ref, mod_ref, held, ctx_send, ctx_recv, col_send, col_recv):
    n_sec, n_ten, n_ctx = sizes
    sec, ten, ctx = (lax.axis_index(name) for name in ("section", "tensor", "ctx"))
    ctxs = [lax.rem(ctx + k, n_ctx) for k in range(n_ctx)]
    steps = [(a, b) for a in range(n_sec) for b in range(n_ten) if (a, b) != (0, 0)]
    places = [
        {"section": lax.rem(sec + a, n_sec), "tensor": lax.rem(ten + b, n_ten)} for a, b in steps
    ]
    greet([{"ctx": c} for c in ctxs[1:]] + places)
    sent = []

    def across(k, slot):
        return remote(
            part_ref, held.at[slot], ctx_send.at[k - 1], ctx_recv.at[k - 1], ctx=ctxs[k]
        )

    for k in range(1, n_ctx):
        start_all([across(k, ctx)], sent)
    held[ctx] = part_ref[...]
    for k in range(1, n_ctx):
        across(k, lax.rem(ctx + n_ctx - k, n_ctx)).wait_recv()
    total = add_ref[...]
    for k in range(n_ctx):
        total = total + held[k]
    mod_ref[sec, ten] = total

    def column(at, block):
        return remote(block, block, col_send.at[at], col_recv.at[at], **places[at])

    for at in range(len(steps)):
        start_all([column(at, mod_ref.at[sec, ten])], sent)
    for at, (a, b) in enumerate(steps):
        theirs = mod_ref.at[lax.rem(sec + n_sec - a, n_sec), lax.rem(ten + n_ten - b, n_ten)]
        column(at, theirs).wait_recv()
    for copy in sent:
        copy.wait_send()


def opening(part, add):
    sizes = n_sec, n_ten, n_ctx = tuple(
        lax.axis_size(name) for name in ("section", "tensor", "ctx")
    )
    dma = pltpu.SemaphoreType.DMA
    return pl.pallas_call(
        functools.partial(opening_kernel, sizes),
        out_shape=jax.ShapeDtypeStruct((n_sec, n_ten) + part.shape, part.dtype),
        in_specs=[VMEM, VMEM],
        out_specs=VMEM,
        scratch_shapes=[
            pltpu.VMEM((n_ctx,) + part.shape, part.dtype),
            dma((max(n_ctx - 1, 1),)),
            dma((max(n_ctx - 1, 1),)),
            dma((n_sec * n_ten,)),
            dma((n_sec * n_ten,)),
        ],
        compiler_params=pltpu.CompilerParams(collective_id=1, has_side_effects=True),
        name="opening",
    )(part, add)


def group_peers(n_sec, n_ctx):
    ni = inner_size(n_ctx)
    no = n_ctx // ni
    sec, ctx = lax.axis_index("section"), lax.axis_index("ctx")
    i, o = lax.rem(ctx, ni), lax.div(ctx, ni)
    far = {
        (a, b): {"section": lax.rem(sec + a, n_sec), "ctx": lax.rem(o + b, no) * ni + i}
        for a in range(n_sec)
        for b in range(no)
        if (a, b) != (0, 0)
    }
    near = {m: {"ctx": o * ni + lax.rem(i + m, ni)} for m in range(1, ni)}
    return sec, i, o, ni, no, far, near


def spread_kernel(n_sec, n_ctx, own_ref, both_ref, own_all, both_all, *sems):
    far_send, far_recv, near_send, near_recv, own_sem = sems
    sec, i, o, ni, no, far, near = group_peers(n_sec, n_ctx)
    greet(list(far.values()) + list(near.values()))
    sent = []
    me = o * ni + i

    def far_copies(step):
        a, b = step
        at = a * no + b
        copies = []
        if a == 0:
            copies.append(
                remote(
                    own_ref, own_all.at[me], far_send.at[0, at], far_recv.at[0, at], **far[step]
                )
            )
        copies.append(
            remote(
                both_ref, both_all.at[sec, me], far_send.at[1, at], far_recv.at[1, at], **far[step]
            )
        )
        return copies

    def near_copies(m, a, b, own_src, both_src, s_at, c_at):
        at = a * no + b
        copies = []
        if a == 0:
            copies.append(
                remote(
                    own_src,
                    own_all.at[c_at],
                    near_send.at[0, m - 1, at],
                    near_recv.at[0, m - 1, at],
                    **near[m],
                )
            )
        copies.append(
            remote(
                both_src,
                both_all.at[s_at, c_at],
                near_send.at[1, m - 1, at],
                near_recv.at[1, m - 1, at],
                **near[m],
            )
        )
        return copies

    for step in far:
        start_all(far_copies(step), sent)
    for m in near:
        start_all(near_copies(m, 0, 0, own_ref, both_ref, sec, me), sent)
    keep = [
        pltpu.make_async_copy(own_ref, own_all.at[me], own_sem.at[0]),
        pltpu.make_async_copy(both_ref, both_all.at[sec, me], own_sem.at[1]),
    ]
    for copy in keep:
        copy.start()
    for step in far:
        a, b = step
        for copy in far_copies(step):
            copy.wait_recv()
        s_at = lax.rem(sec + n_sec - a, n_sec)
        c_at = lax.rem(o + no - b, no) * ni + i
        for m in near:
            start_all(
                near_copies(m, a, b, own_all.at[c_at], both_all.at[s_at, c_at], s_at, c_at), sent
            )
    for m in near:
        for a in range(n_sec):
            for b in range(no):
                s_at = lax.rem(sec + n_sec - a, n_sec)
                c_at = lax.rem(o + no - b, no) * ni + lax.rem(i + ni - m, ni)
                for copy in near_copies(
                    m, a, b, own_all.at[c_at], both_all.at[s_at, c_at], s_at, c_at
                ):
                    copy.wait_recv()
    for copy in keep:
        copy.wait()
    for copy in sent:
        copy.wait_send()


def spread(own, both):
    n_sec, n_ctx = lax.axis_size("section"), lax.axis_size("ctx")
    ni = inner_size(n_ctx)
    no = n_ctx // ni
    dma = pltpu.SemaphoreType.DMA
    return pl.pallas_call(
        functools.partial(spread_kernel, n_sec, n_ctx),
        out_shape=[
            jax.ShapeDtypeStruct((n_ctx,) + own.shape, own.dtype),
            jax.ShapeDtypeStruct((n_sec, n_ctx) + both.shape, both.dtype),
        ],
        in_specs=[VMEM, VMEM],
        out_specs=[VMEM, VMEM],
        scratch_shapes=[
            dma((2, n_sec * no)),
            dma((2, n_sec * no)),
            dma((2, ni, n_sec * no)),
            dma((2, ni, n_sec * no)),
            dma((2,)),
        ],
        compiler_params=pltpu.CompilerParams(collective_id=2, has_side_effects=True),
        name="spread",
    )(own, both)


def owner_kernel(n_sec, n_ctx, own_ref, both_ref, own_out, both_out, *refs):
    own_pair, both_pair, own_far, both_far = refs[:4]
    far_send, far_recv, near_send, near_recv = refs[4:]
    sec, i, o, ni, no, far, near = group_peers(n_sec, n_ctx)
    greet(list(far.values()) + list(near.values()))
    sent = []

    def near_copies(m, a, b):
        to = lax.rem(i + m, ni)
        s_at, o_at = lax.rem(sec + a, n_sec), lax.rem(o + b, no)
        at = a * no + b
        copies = []
        if a == 0:
            copies.append(
                remote(
                    own_ref.at[o_at * ni + to],
                    own_pair.at[m - 1, b],
                    near_send.at[0, m - 1, at],
                    near_recv.at[0, m - 1, at],
                    **near[m],
                )
            )
        copies.append(
            remote(
                both_ref.at[s_at, o_at * ni + to],
                both_pair.at[m - 1, at],
                near_send.at[1, m - 1, at],
                near_recv.at[1, m - 1, at],
                **near[m],
            )
        )
        return copies

    order = list(far) + [(0, 0)]
    for step in order:
        for m in near:
            start_all(near_copies(m, *step), sent)

    def far_copies(a, b):
        at = a * no + b
        copies = []
        if a == 0:
            copies.append(
                remote(
                    own_pair.at[ni - 1, b],
                    own_far.at[b],
                    far_send.at[0, at],
                    far_recv.at[0, at],
                    **far[(a, b)],
                )
            )
        copies.append(
            remote(
                both_pair.at[ni - 1, at],
                both_far.at[at],
                far_send.at[1, at],
                far_recv.at[1, at],
                **far[(a, b)],
            )
        )
        return copies

    for a, b in order:
        s_at, c_at = lax.rem(sec + a, n_sec), lax.rem(o + b, no) * ni + i
        at = a * no + b
        for m in near:
            for copy in near_copies(m, a, b):
                copy.wait_recv()
        total_both = both_ref[s_at, c_at].astype(jnp.float32)
        for m in near:
            total_both = total_both + both_pair[m - 1, at].astype(jnp.float32)
        total_own = None
        if a == 0:
            total_own = own_ref[c_at].astype(jnp.float32)
            for m in near:
                total_own = total_own + own_pair[m - 1, b].astype(jnp.float32)
        if (a, b) == (0, 0):
            own_out[...] = total_own
            both_out[...] = total_both
        else:
            if a == 0:
                own_pair[ni - 1, b] = total_own.astype(own_pair.dtype)
            both_pair[ni - 1, at] = total_both.astype(both_pair.dtype)
            start_all(far_copies(a, b), sent)
    for a, b in far:
        for copy in far_copies(a, b):
            copy.wait_recv()
        if a == 0:
            own_out[...] += own_far[b].astype(jnp.float32)
        both_out[...] += both_far[a * no + b].astype(jnp.float32)
    for copy in sent:
        copy.wait_send()


def owner_sum(own, both):
    n_sec, n_ctx = lax.axis_size("section"), lax.axis_size("ctx")
    ni = inner_size(n_ctx)
    no = n_ctx // ni
    dma = pltpu.SemaphoreType.DMA
    own_shape, both_shape = own.shape[1:], both.shape[2:]
    return pl.pallas_call(
        functools.partial(owner_kernel, n_sec, n_ctx),
        out_shape=[
            jax.ShapeDtypeStruct(own_shape, jnp.float32),
            jax.ShapeDtypeStruct(both_shape, jnp.float32),
        ],
        in_specs=[VMEM, VMEM],
        out_specs=[VMEM, VMEM],
        scratch_shapes=[
            pltpu.VMEM((ni, no) + own_shape, own.dtype),
            pltpu.VMEM((ni, n_sec * no) + both_shape, both.dtype),
            pltpu.VMEM((no,) + own_shape, own.dtype),
            pltpu.VMEM((n_sec * no,) + both_shape, both.dtype),
            dma((2, n_sec * no)),
            dma((2, n_sec * no)),
            dma((2, ni, n_sec * no)),
            dma((2, ni, n_sec * no)),
        ],
        compiler_params=pltpu.CompilerParams(collective_id=3, has_side_effects=True),
        name="owner_sum",
    )(own, both)


def small_kernel(axes, sizes, x_ref, out_ref, held, send, recv):
    at = [lax.axis_index(name) for name in axes]
    steps = [(a, b) for a in range(sizes[0]) for b in range(sizes[1])]
    places = [
        [lax.rem(here + sign * step + size, size) for here, step, size in zip(at, pair, sizes)]
        for sign in (1, -1)
        for pair in steps
    ]
    to, source = places[: len(steps)], places[len(steps) :]
    where = [dict(zip(axes, place)) for place in to]
    greet(where[1:])

    def block(place):
        return place[0] if x_ref.shape[0] > 1 else 0

    def copy(k, slot):
        return remote(
            x_ref.at[block(to[k])],
            held.at[slot[0] * sizes[1] + slot[1]],
            send.at[k - 1],
            recv.at[k - 1],
            **where[k],
        )

    copies = [copy(k, at) for k in range(1, len(steps))]
    for started in copies:
        started.start()
    held[at[0] * sizes[1] + at[1]] = x_ref[block(at)]
    for k in range(1, len(steps)):
        copy(k, source[k]).wait_recv()
    total = held[0]
    for k in range(1, len(steps)):
        total = total + held[k]
    out_ref[...] = total
    for started in copies:
        started.wait_send()


def small_sum(x, axes, collective_id):
    sizes = tuple(lax.axis_size(name) for name in axes)
    n = sizes[0] * sizes[1]
    dma = pltpu.SemaphoreType.DMA((max(n - 1, 1),))
    return pl.pallas_call(
        functools.partial(small_kernel, axes, sizes),
        out_shape=jax.ShapeDtypeStruct(x.shape[1:], x.dtype),
        in_specs=[VMEM],
        out_specs=VMEM,
        scratch_shapes=[pltpu.VMEM((n,) + x.shape[1:], x.dtype), dma, dma],
        compiler_params=pltpu.CompilerParams(collective_id=collective_id, has_side_effects=True),
        cost_estimate=link_cost(100 * n * x[0].size * x.dtype.itemsize),
        name="small_sum",
    )(x)


def packed(pieces, width):
    flat = jnp.concatenate([p.reshape(-1) for p in pieces])
    rows = -(-flat.shape[0] // width)
    rows = -(-rows // 8) * 8
    return jnp.pad(flat, (0, rows * width - flat.shape[0])).reshape(rows, width)


def unpacked(block, shapes):
    flat, at, out = block.reshape(-1), 0, []
    for shape in shapes:
        size = math.prod(shape)
        out.append(flat[at : at + size].reshape(shape))
        at += size
    return out


def layer_norm(values):
    centre = jnp.mean(values, axis=-1, keepdims=True)
    centred = values - centre
    variance = jnp.mean(centred * centred, axis=-1, keepdims=True)
    inverse = lax.rsqrt(variance + EPSILON)
    return (centred * inverse, inverse)


def norm_back(normed, inverse, upstream):
    mean_grad = jnp.mean(upstream, axis=-1, keepdims=True)
    mean_cross = jnp.mean(upstream * normed, axis=-1, keepdims=True)
    return inverse * (upstream - mean_grad - normed * mean_cross)


def gelu_back(pre_act, upstream):
    unused_out, pullback = jax.vjp(
        lambda pre_value: jax.nn.gelu(pre_value, approximate=True), pre_act
    )
    return pullback(upstream)[0]


def heads(array):
    cols = array.shape[-2]
    return array.reshape(*array.shape[:-2], cols // HD, HD, array.shape[-1])


def score_columns(queries, keys):
    softmax_scale = 1.0 / math.sqrt(HD)
    return (
        jnp.einsum(
            "nhdk,hdq->hnkq", heads(keys), heads(queries), preferred_element_type=jnp.float32
        )
        * softmax_scale
    )


def attend(queries, keys, values):
    scores = score_columns(queries, keys)
    row_peak = jnp.max(scores, axis=(1, 2), keepdims=True)
    log_total = row_peak + jnp.log(jnp.sum(jnp.exp(scores - row_peak), axis=(1, 2), keepdims=True))
    prob_bf = jnp.exp(scores - log_total).astype(jnp.bfloat16)
    context = jnp.einsum(
        "nhdk,hnkq->hdq", heads(values), prob_bf, preferred_element_type=jnp.float32
    )
    return context.astype(jnp.bfloat16).reshape(queries.shape), log_total


def attention_grads(queries, keys, values, log_total, context, context_grad):
    softmax_scale = 1.0 / math.sqrt(HD)
    query_heads, grad_heads = heads(queries), heads(context_grad)
    delta = jnp.sum(
        grad_heads.astype(jnp.float32) * heads(context).astype(jnp.float32), axis=1
    )[:, None, None, :]
    prob_full = jnp.exp(score_columns(queries, keys) - log_total)
    prob_bf = prob_full.astype(jnp.bfloat16)
    prob_grad = jnp.einsum(
        "nhdk,hdq->hnkq", heads(values), grad_heads, preferred_element_type=jnp.float32
    )
    score_grad = (prob_full * (prob_grad - delta)).astype(jnp.bfloat16)
    query_grad = (
        jnp.einsum(
            "nhdk,hnkq->hdq", heads(keys), score_grad, preferred_element_type=jnp.float32
        )
        * softmax_scale
    ).reshape(queries.shape)
    key_part = (
        jnp.einsum("hnkq,hdq->nhdk", score_grad, query_heads, preferred_element_type=jnp.float32)
        * softmax_scale
    ).reshape(keys.shape)
    value_part = jnp.einsum(
        "hnkq,hdq->nhdk", prob_bf, grad_heads, preferred_element_type=jnp.float32
    ).reshape(values.shape)
    both = jnp.concatenate(
        [key_part.astype(jnp.bfloat16), value_part.astype(jnp.bfloat16)], axis=1
    )
    return query_grad, both


def contract(left, right, left_dim, right_dim):
    return lax.dot_general(
        left, right, (((left_dim,), (right_dim,)), ((), ())), preferred_element_type=jnp.float32
    )


class Rows:
    def __init__(self, latents, section):
        n_sec = lax.axis_size("section")
        self.n_sec = n_sec
        total, self.tokens, self.width = latents.shape
        self.section = section
        self.full = total // n_sec
        self.rest = total - self.full * n_sec
        self.part = self.tokens // n_sec
        self.own_rows = self.full * self.tokens
        self.both_rows = self.rest * self.part
        self.rows = self.own_rows + self.both_rows

    def take(self, array):
        own = lax.dynamic_slice_in_dim(array, self.section * self.full, self.full, 0)
        both = lax.dynamic_slice_in_dim(
            array[self.full * self.n_sec :], self.section * self.part, self.part, 1
        )
        return jnp.concatenate(
            [own.reshape(self.own_rows, -1), both.reshape(self.both_rows, -1)], axis=0
        )

    def split(self, array):
        return (
            array[: self.own_rows].reshape(self.full, self.tokens, -1),
            array[self.own_rows :].reshape(self.rest, self.part, -1),
        )

    def spans(self):
        out = [(at * self.tokens, self.tokens) for at in range(self.full)]
        return out + [
            (self.own_rows + at * self.part, self.part) for at in range(self.rest)
        ]

    def columns(self, array):
        return [array[:, start : start + size] for start, size in self.spans()]

    def mods(self, modulation):
        own = lax.dynamic_slice_in_dim(modulation, self.section * self.full, self.full, 0)
        return jnp.concatenate([own, modulation[self.full * self.n_sec :]], axis=0)

    def wide(self, pieces):
        row = lax.broadcasted_iota(jnp.int32, (self.rows, 1), 0)
        out = pieces[-1][None, :]
        for (start, size), piece in reversed(list(zip(self.spans(), pieces))[:-1]):
            out = jnp.where(row < start + size, piece[None, :], out)
        return out

    def sums(self, array):
        return [jnp.sum(array[a : a + b], axis=0) for a, b in self.spans()]

    def placed(self, sums):
        total = self.full * self.n_sec + self.rest
        whole = jnp.zeros((total,) + sums.shape[1:], sums.dtype)
        whole = lax.dynamic_update_slice_in_dim(
            whole, sums[: self.full], self.section * self.full, 0
        )
        return lax.dynamic_update_slice_in_dim(
            whole, sums[self.full :], self.full * self.n_sec, 0
        )

    def assembled(self, per_block, received):
        own = per_block[-1]
        for b in range(self.n_sec - 1):
            own = jnp.where(self.section == b, per_block[b], own)
        out = jnp.zeros(
            (self.full * self.n_sec + self.rest, self.tokens, self.width), own.dtype
        )
        for k in range(self.n_sec):
            rows = own
            if k:
                rows = received[-1][k - 1]
                for b in range(self.n_sec - 1):
                    rows = jnp.where(self.section == b, received[b][k - 1], rows)
            source = lax.rem(self.section + k, self.n_sec)
            first, both = self.split(rows)
            out = lax.dynamic_update_slice_in_dim(out, first, source * self.full, 0)
            out = lax.dynamic_update_slice(
                out, both, (self.full * self.n_sec, source * self.part, 0)
            )
        return out


def gathered(key_value, rows):
    spans = rows.spans()
    cols = [key_value[:, start : start + size] for start, size in spans]
    own = jnp.concatenate(cols[: rows.full], axis=0)
    both = jnp.concatenate(cols[rows.full :], axis=0)
    own_all, both_all = spread(own, both)
    both_all = both_all.reshape(-1, *both.shape)
    high = key_value.shape[0]
    return [own_all[:, at * high : (at + 1) * high] for at in range(rows.full)] + [
        both_all[:, at * high : (at + 1) * high] for at in range(rows.rest)
    ]


def returned(parts, rows):
    high = parts[0].shape[1]
    own = jnp.concatenate(parts[: rows.full], axis=1)
    both = jnp.concatenate(parts[rows.full :], axis=1)
    own, both = owner_sum(own, both.reshape(rows.n_sec, -1, *both.shape[1:]))
    return jnp.concatenate(
        [own[at * high : (at + 1) * high] for at in range(rows.full)]
        + [both[at * high : (at + 1) * high] for at in range(rows.rest)],
        axis=1,
    )


def forward_block(rows, residual, mods, attn_weights, biases, prepare, mlp_weights, last):
    w_qkv, w_out = attn_weights
    b_qv, b_out, b_fc1, b_fc2 = biases
    local_cols = w_qkv.shape[-1] // 3
    shift_a, scale_a, gate_a, shift_m, scale_m, gate_m = (
        rows.wide([mods[at, k] for at in range(mods.shape[0])]) for k in range(6)
    )
    normed_a, inverse_a = layer_norm(residual)
    attn_in = (normed_a * (1.0 + scale_a) + shift_a).astype(jnp.bfloat16)
    projected = contract(w_qkv, attn_in, 0, 1)
    bias = jnp.concatenate([b_qv[0], jnp.zeros_like(b_qv[0]), b_qv[1]])
    projected = (projected + bias[:, None]).astype(jnp.bfloat16)
    queries = rows.columns(projected[:local_cols])
    keys_values, sends = prepare(gathered(projected[local_cols:], rows))
    attended = [
        attend(q, kv[:, :local_cols], kv[:, local_cols:])
        for q, kv in zip(queries, keys_values)
    ]
    context = jnp.concatenate([c for c, _ in attended], axis=1)
    attn_term = contract(context, w_out, 0, 0)
    (attn_sum,), moved = beside(tensor_sum, [attn_term.astype(jnp.bfloat16)], sends)
    w_fc1, w_fc2 = mlp_weights(moved)
    attn_out = attn_sum.astype(jnp.float32) + b_out
    middle = residual + gate_a * attn_out
    normed_m, inverse_m = layer_norm(middle)
    mlp_in = (normed_m * (1.0 + scale_m) + shift_m).astype(jnp.bfloat16)
    pre_act = jnp.dot(mlp_in, w_fc1, preferred_element_type=jnp.float32) + b_fc1
    hidden = jax.nn.gelu(pre_act, approximate=True).astype(jnp.bfloat16)
    mlp_term = jnp.dot(hidden, w_fc2, preferred_element_type=jnp.float32).astype(jnp.bfloat16)

    def close(mlp_sum):
        mlp_out = mlp_sum.astype(jnp.float32) + b_fc2
        return mlp_out, (middle + gate_m * mlp_out).astype(jnp.bfloat16)

    mlp_out, block_res = (None, None) if last else close(tensor_sum(mlp_term)[0])
    stored = (
        normed_a,
        inverse_a,
        attn_in,
        queries,
        keys_values,
        [log_total for _, log_total in attended],
        context,
        attn_out,
        normed_m,
        inverse_m,
        mlp_in,
        pre_act,
        hidden,
        mlp_out,
    )
    return block_res, stored, moved, (mlp_term, close) if last else None


def backward_block(rows, upstream, stored, mods, weights, block, firsts, seconds, pending):
    w_qkv, w_out, w_fc1, w_fc2 = weights
    (
        normed_a,
        inverse_a,
        attn_in,
        queries,
        keys_values,
        log_totals,
        context,
        attn_out,
        normed_m,
        inverse_m,
        mlp_in,
        pre_act,
        hidden,
        mlp_out,
    ) = stored
    local_cols = w_qkv.shape[-1] // 3
    shift_a, scale_a, gate_a, shift_m, scale_m, gate_m = (
        rows.wide([mods[at, k] for at in range(mods.shape[0])]) for k in range(6)
    )
    mlp_grad = upstream * gate_m
    mlp_grad_b = mlp_grad.astype(jnp.bfloat16)
    grad_b2 = jnp.sum(mlp_grad, axis=0)
    pre_grad = gelu_back(pre_act, jnp.dot(mlp_grad_b, w_fc2.T, preferred_element_type=jnp.float32))
    pre_grad_b = pre_grad.astype(jnp.bfloat16)
    grad_b1 = jnp.sum(pre_grad, axis=0)
    mlp_pair = inner_pair(
        per_owner(contract(mlp_grad_b, hidden, 0, 0), contract(mlp_in, pre_grad_b, 0, 0))
    )
    mlp_term = jnp.dot(pre_grad_b, w_fc1.T, preferred_element_type=jnp.float32)
    terms = [mlp_term.astype(jnp.bfloat16)]
    if pending:
        terms.append(pending[0])
    outer = outer_sends(mlp_pair)
    (mlp_in_grad, *sums), moved = beside(tensor_sum, terms, outer + firsts)
    block_res = None
    if pending:
        mlp_out, block_res = pending[1](sums[0])
    gate_m_grad = rows.sums(upstream * mlp_out)
    first_moved = moved[len(outer) :]
    mlp_share = outer_total(mlp_pair, moved[: len(outer)])
    mlp_in_grad = mlp_in_grad.astype(jnp.float32)
    shift_m_grad = rows.sums(mlp_in_grad)
    scale_m_grad = rows.sums(mlp_in_grad * normed_m)
    middle_grad = upstream + norm_back(normed_m, inverse_m, mlp_in_grad * (1.0 + scale_m))
    gate_a_grad = rows.sums(middle_grad * attn_out)
    attn_grad = middle_grad * gate_a
    attn_grad_b = attn_grad.astype(jnp.bfloat16)
    grad_bo = jnp.sum(attn_grad, axis=0)
    context_grad = contract(w_out, attn_grad_b, 1, 1).astype(jnp.bfloat16)
    query_grads, key_value_parts = zip(
        *(
            attention_grads(q, kv[:, :local_cols], kv[:, local_cols:], log_total, c, cg)
            for q, kv, log_total, c, cg in zip(
                queries, keys_values, log_totals, rows.columns(context), rows.columns(context_grad)
            )
        )
    )
    query_grad = jnp.concatenate(query_grads, axis=1)
    key_value_grad = returned(key_value_parts, rows)
    grad_bqv = jnp.stack(
        [jnp.sum(query_grad, axis=1), jnp.sum(key_value_grad[local_cols:], axis=1)]
    )
    qkv_grad_b = jnp.concatenate([query_grad, key_value_grad], axis=0).astype(jnp.bfloat16)
    qkv_rows, context_rows = lax.optimization_barrier((qkv_grad_b.T, context.T))
    attn_term = contract(qkv_rows, w_qkv, 1, 1)
    attn_pairs = [
        inner_pair(per_owner(contract(attn_in, qkv_rows, 0, 0))),
        inner_pair(per_owner(contract(attn_grad_b, context_rows, 0, 0))),
    ]
    outers = [outer_sends(pair) for pair in attn_pairs]
    across = block_sends(mlp_share, block)
    sends = [*outers, across, seconds]
    ((attn_in_grad,), moved) = beside(
        tensor_sum, [attn_term.astype(jnp.bfloat16)], [send for part in sends for send in part]
    )
    came = []
    for part in sends:
        came.append(moved[: len(part)])
        moved = moved[len(part) :]
    attn_shares = [outer_total(pair, part) for pair, part in zip(attn_pairs, came)]
    mlp_share = block_total(mlp_share, came[-2])
    second_moved = came[-1]
    attn_in_grad = attn_in_grad.astype(jnp.float32)
    shift_a_grad = rows.sums(attn_in_grad)
    scale_a_grad = rows.sums(attn_in_grad * normed_a)
    input_grad = middle_grad + norm_back(normed_a, inverse_a, attn_in_grad * (1.0 + scale_a))
    pieces = (shift_a_grad, scale_a_grad, gate_a_grad, shift_m_grad, scale_m_grad, gate_m_grad)
    count = len(pieces[0])
    mod_grad = jnp.concatenate([piece[at] for at in range(count) for piece in pieces]).reshape(
        count, -1
    )
    return (
        input_grad,
        mod_grad,
        (grad_bqv, grad_bo, grad_b1, grad_b2),
        (mlp_share, *attn_shares),
        block_res,
        first_moved,
        second_moved,
    )


def per_owner(*terms):
    n = lax.axis_size("ctx")
    return [t.reshape(n, -1, t.shape[-1]) for t in terms]


def to_inner(value, by):
    n = lax.axis_size("ctx")
    ni = inner_size(n)
    return lax.ppermute(value, "ctx", [(a, a // ni * ni + (a + by) % ni) for a in range(n)])


def to_outer(value, by):
    n = lax.axis_size("ctx")
    ni = inner_size(n)
    return lax.ppermute(value, "ctx", [(a, (a + by * ni) % n) for a in range(n)])


def to_section(value, by):
    n = lax.axis_size("section")
    return lax.ppermute(value, "section", [(a, (a + by) % n) for a in range(n)])


def to_block(value, block, by):
    n = lax.axis_size("section")
    return lax.ppermute(value, "section", [((block + by) % n, block)])


def ctx_place():
    n = lax.axis_size("ctx")
    ni = inner_size(n)
    at = lax.axis_index("ctx")
    return n // ni, ni, lax.div(at, ni), lax.rem(at, ni)


def beside(kernel, args, sends):
    args, values = lax.optimization_barrier((args, [value for value, _ in sends]))
    moved = [move(value) for value, (_, move) in zip(values, sends)]
    return lax.optimization_barrier((kernel(*args), moved))


def half_of(weights):
    _, ni, _, i = ctx_place()
    sizes = [w.shape[0] // ni for w in weights]
    return jnp.concatenate(
        [lax.dynamic_slice_in_dim(w, i * size, size, 0) for w, size in zip(weights, sizes)]
    )


def joined(own, passed, weights):
    _, ni, _, i = ctx_place()
    found, start = [], 0
    for w in weights:
        size = w.shape[0] // ni
        parts = [piece[start : start + size] for piece in [own] + passed]
        start += size
        ordered = []
        for at in range(ni):
            piece = parts[0]
            for m in range(1, ni):
                piece = jnp.where(lax.rem(i + ni - m, ni) == at, parts[m], piece)
            ordered.append(piece)
        found.append(jnp.concatenate(ordered))
    return found


def chosen_blocks(weights, others):
    n_sec = lax.axis_size("section")
    section = lax.axis_index("section")
    blocks = []
    for b in range(n_sec):
        chosen = list(weights)
        for k, found in enumerate(others, 1):
            is_source = lax.rem(section + n_sec - k, n_sec) == b
            chosen = [jnp.where(is_source, new, old) for new, old in zip(found, chosen)]
        blocks.append(chosen)
    return blocks


def fetched(weights):
    n_sec = lax.axis_size("section")
    groups = [
        [at for at, w in enumerate(weights) if w.shape[1] == width]
        for width in sorted({w.shape[1] for w in weights})
    ]
    halves = [half_of([weights[at] for at in group]) for group in groups]
    return groups, [[to_section(half, k) for k in range(1, n_sec)] for half in halves]


def passing(fetch):
    _, ni, _, _ = ctx_place()
    return [
        (half, functools.partial(to_inner, by=m))
        for of_group in fetch[1]
        for half in of_group
        for m in range(1, ni)
    ]


def every_block(weights, fetch, passed):
    _, ni, _, _ = ctx_place()
    n_sec = lax.axis_size("section")
    others = [[None] * len(weights) for _ in range(n_sec - 1)]
    passed = list(passed)
    for group, of_group in zip(*fetch):
        for k, half in enumerate(of_group):
            rest = [passed.pop(0) for _ in range(1, ni)]
            for at, whole in zip(group, joined(half, rest, [weights[at] for at in group])):
                others[k][at] = whole
    return chosen_blocks(weights, others)


def inner_pair(terms):
    no, ni, _, i = ctx_place()
    terms = [t.astype(jnp.bfloat16).reshape(no, ni, -1, t.shape[-1]) for t in terms]

    def inner(at):
        return jnp.concatenate(
            [lax.dynamic_index_in_dim(t, at, 1, keepdims=False) for t in terms], axis=1
        )

    pair = inner(i).astype(jnp.float32)
    for m in range(1, ni):
        pair = pair + to_inner(inner(lax.rem(i + m, ni)), m).astype(jnp.float32)
    return pair.astype(jnp.bfloat16)


def outer_sends(pair):
    no, _, o, _ = ctx_place()
    return [
        (
            lax.dynamic_index_in_dim(pair, lax.rem(o + m, no), 0, keepdims=False),
            functools.partial(to_outer, by=m),
        )
        for m in range(1, no)
    ]


def outer_total(pair, moved):
    _, _, o, _ = ctx_place()
    total = lax.dynamic_index_in_dim(pair, o, 0, keepdims=False).astype(jnp.float32)
    for piece in moved:
        total = total + piece.astype(jnp.float32)
    return total


def block_sends(value, block):
    value = value.astype(jnp.bfloat16)
    return [
        (value, functools.partial(to_block, block=block, by=k))
        for k in range(1, lax.axis_size("section"))
    ]


def block_total(own, moved):
    for piece in moved:
        own = own + piece.astype(jnp.float32)
    return own


def local(
    latents,
    condition,
    cotangent,
    w_ada,
    b_ada,
    w_qkv,
    b_qv,
    w_out,
    b_out,
    w_fc1,
    b_fc1,
    w_fc2,
    b_fc2,
):
    section = lax.axis_index("section")
    n_sec = lax.axis_size("section")
    latent_total, token_count, width = latents.shape
    width_cols = b_ada.shape[-1]
    local_cols = w_qkv.shape[-1]
    rows = Rows(latents, section)
    cond_act = jax.nn.silu(condition).astype(jnp.bfloat16)
    mod_part = jnp.dot(cond_act, w_ada[0], preferred_element_type=jnp.float32)
    bias_shapes = [b_qv.shape[1:], b_out.shape[1:], b_fc1.shape[1:], b_fc2.shape[1:]]
    bias_rows = packed([b_qv, b_out, b_fc1, b_fc2], width_cols)
    add = jnp.concatenate(
        [jnp.broadcast_to(b_ada, (latent_total, width_cols)), bias_rows], axis=0
    )
    height = -(-add.shape[0] // 8) * 8
    add = jnp.pad(add, ((0, height - add.shape[0]), (0, 0)))
    attn_weights = [w_qkv[0].reshape(width, 3 * local_cols), w_out[0]]
    first_weights, second_weights = [w_fc1[0]], [w_fc2[0]]
    mod_all = opening(jnp.pad(mod_part, ((0, height - latent_total), (0, 0))), add)
    mod_all, attn_weights = lax.optimization_barrier((mod_all, attn_weights))
    attn_fetch = fetched(attn_weights)
    halves, first_weights = lax.optimization_barrier((attn_fetch[1], first_weights))
    attn_fetch = (attn_fetch[0], halves)
    first_fetch = fetched(first_weights)
    attn_blocks = every_block(
        attn_weights, attn_fetch, [move(half) for half, move in passing(attn_fetch)]
    )
    tensor = lax.axis_index("tensor")
    modulation = jnp.swapaxes(mod_all[:, :, :latent_total], 1, 2).reshape(
        n_sec, latent_total, 6, width
    )
    own_cols = lax.dynamic_index_in_dim(mod_all, tensor, 1, keepdims=False)
    biases, mods = [], []
    for b in range(n_sec):
        biases.append(unpacked(own_cols[b, latent_total:], bias_shapes))
        mods.append(rows.mods(modulation[b]))
    residual = rows.take(latents)
    outs, out_moved, kept, mlp_blocks, pending = [], [], [], [], None
    for b in range(n_sec):
        if b == 0:
            fetch = []

            def prepare(keys_values):
                keys_values, weights = lax.optimization_barrier((keys_values, second_weights))
                fetch.append(fetched(weights))
                return keys_values, passing(first_fetch)

            def finish(moved):
                firsts = every_block(first_weights, first_fetch, moved)
                seconds = every_block(
                    second_weights, fetch[0], [move(half) for half, move in passing(fetch[0])]
                )
                mlp_blocks.extend([*one, *two] for one, two in zip(firsts, seconds))
                return mlp_blocks[0]

        else:
            sends = block_sends(outs[-1], b - 1)

            def prepare(keys_values, sends=sends):
                return keys_values, sends

            def finish(moved, b=b):
                return mlp_blocks[b]

        residual, stored, moved, pending = forward_block(
            rows,
            residual.astype(jnp.float32),
            mods[b],
            attn_blocks[b],
            biases[b],
            prepare,
            finish,
            b == n_sec - 1,
        )
        if b:
            out_moved.append(moved)
        outs.append(residual)
        kept.append(stored)
    upstream = rows.take(cotangent).astype(jnp.float32)
    in_grads, in_moved, small, shares = ([None] * n_sec for _ in range(4))
    out_moved.append([])
    firsts, seconds = [[], []], []
    for b in reversed(range(n_sec)):
        upstream, mod_grad, bias_grads, shares[b], block_res, first_moved, second_moved = (
            backward_block(
                rows,
                upstream,
                kept[b],
                mods[b],
                (*attn_blocks[b], *mlp_blocks[b]),
                b,
                [send for part in firsts for send in part],
                seconds,
                pending if b == n_sec - 1 else None,
            )
        )
        if b == n_sec - 1:
            outs[b] = block_res
        else:
            at = 0
            for which in (1, 2):
                part = first_moved[at : at + n_sec - 1]
                at += n_sec - 1
                shares[b + 1][which] = block_total(shares[b + 1][which], part)
            if b == n_sec - 2:
                out_moved[-1] = first_moved[at:]
            in_moved[b + 1] = second_moved
        shares[b] = list(shares[b])
        in_grads[b] = upstream.astype(jnp.bfloat16)
        cols = mod_grad[:, :width_cols]
        for t in range(1, lax.axis_size("tensor")):
            cols = jnp.where(tensor == t, mod_grad[:, t * width_cols : (t + 1) * width_cols], cols)
        small[b] = packed([rows.placed(cols), *bias_grads], width)
        firsts = [block_sends(share, b) for share in shares[b][1:]]
        if b == n_sec - 1:
            firsts.append(block_sends(outs[b], b))
        seconds = block_sends(in_grads[b], b)
    summed, in_moved[0] = beside(
        functools.partial(small_sum, axes=("section", "ctx"), collective_id=4),
        [jnp.stack(small)],
        seconds,
    )
    in_grad = rows.assembled(in_grads, in_moved).astype(jnp.float32)
    block_out = rows.assembled(outs, out_moved)
    mod_total, grad_bqv, grad_bo, grad_b1, grad_b2 = unpacked(
        summed, [(latent_total, width_cols)] + bias_shapes
    )
    mod_rounded = mod_total.astype(jnp.bfloat16)
    cond_part = jnp.dot(mod_rounded, w_ada[0].T, preferred_element_type=jnp.float32)
    cond_part = jnp.pad(cond_part, ((0, -latent_total % 8), (0, 0)))
    cond_sum, moved = beside(
        functools.partial(small_sum, axes=("section", "tensor"), collective_id=5),
        [cond_part[None]],
        firsts[0] + firsts[1],
    )
    cond_sum = cond_sum[:latent_total]
    for which in (1, 2):
        shares[0][which] = block_total(shares[0][which], moved[: n_sec - 1])
        moved = moved[n_sec - 1 :]

    def mine(which):
        out = shares[-1][which]
        for b in range(n_sec - 1):
            out = jnp.where(section == b, shares[b][which], out)
        return out

    mlp_share, qkv_share, out_share = mine(0), mine(1), mine(2)
    share_rows = mlp_share.shape[0] // 2
    grad_w_ada = jnp.dot(cond_act.T, mod_rounded, preferred_element_type=jnp.float32)[None]
    grad_b_ada = jnp.sum(mod_total, axis=0)[None]
    sigmoid_c = jax.nn.sigmoid(condition)
    cond_grad = cond_sum * sigmoid_c * (1.0 + condition * (1.0 - sigmoid_c))
    return (
        block_out[None],
        in_grad[None],
        cond_grad,
        grad_w_ada,
        grad_b_ada,
        qkv_share.reshape(1, share_rows, 3, local_cols),
        grad_bqv[None],
        out_share.T[None],
        grad_bo[None],
        mlp_share[share_rows:][None],
        grad_b1[None],
        mlp_share[:share_rows].T[None],
        grad_b2[None],
    )


def solution(mesh):
    return jax.shard_map(
        local,
        mesh=mesh,
        in_specs=(
            P(None, "ctx", None),
            P(None, "ctx"),
            P(None, "ctx", None),
            P("section", "ctx", "tensor"),
            P("section", "tensor"),
            P("section", None, None, "tensor"),
            P("section", None, "tensor"),
            P("section", "tensor", None),
            P("section", None),
            P("section", None, "tensor"),
            P("section", "tensor"),
            P("section", "tensor", None),
            P("section", None),
        ),
        out_specs=(
            P("section", None, "ctx", None),
            P("section", None, "ctx", None),
            P(None, "ctx"),
            P("section", "ctx", "tensor"),
            P("section", "tensor"),
            P("section", "ctx", None, "tensor"),
            P("section", None, "tensor"),
            P("section", "tensor", "ctx"),
            P("section", None),
            P("section", "ctx", "tensor"),
            P("section", "tensor"),
            P("section", "tensor", "ctx"),
            P("section", None),
        ),
        check_vma=False,
    )
```

```python
import functools
import math

import jax
import jax.numpy as jnp
from jax import lax
from jax.experimental import pallas as pl
from jax.experimental.layout import Layout, with_layout_constraint
from jax.experimental.pallas import tpu as pltpu
from jax.sharding import PartitionSpec as P

HD = 72
EPSILON = 1e-06
MESH = pl.DeviceIdType.MESH
ROW_TILE = 16
VMEM = pl.BlockSpec(memory_space=pltpu.VMEM)


def inner_size(n):
    return 2 if n % 2 == 0 else 1


def remote(src, dst, send, recv, **to):
    return pltpu.make_async_remote_copy(
        src_ref=src,
        dst_ref=dst,
        send_sem=send,
        recv_sem=recv,
        device_id=to,
        device_id_type=MESH,
    )


def greet(peers):
    barrier = pltpu.get_barrier_semaphore()
    for peer in peers:
        pl.semaphore_signal(barrier, inc=1, device_id=peer, device_id_type=MESH)
    pl.semaphore_wait(barrier, len(peers))


def row_major(array):
    return with_layout_constraint(array, Layout(tuple(range(array.ndim))))


def link_cost(moved):
    return pl.CostEstimate(flops=0, bytes_accessed=moved, transcendentals=0)


def start_all(copies, sent):
    for copy in copies:
        copy.start()
        sent.append(copy)


def middle_role(d, n, pieces, rows, lag, x_refs, out_refs, acc, from_outer, from_middle, sems):
    up_send, up_recv, mid_send, mid_recv, down_send, down_recv = sems
    half = n // 2
    left = d < half
    outer, inner = (d - 1, d + 1) if left else (d + 1, d - 1)
    has_outer = 0 <= outer < n
    is_middle = d in (half - 1, half)
    to_middle = half - 1 - d if left else d - half
    each = pieces // len(x_refs)

    def term(refs, p):
        return refs[p // each].at[pl.ds(p % each * rows, rows)]

    def held(ref, p):
        return ref.at[pl.ds(p * rows, rows)]

    def hop(src, dst, send, recv, to, p):
        return remote(src, dst, send.at[p], recv.at[p], tensor=to)

    sent = []

    def gather(p):
        x, kept, came = term(x_refs, p), held(acc, p), held(from_outer, p)
        src = x
        if has_outer:
            hop(x, came, up_send, up_recv, inner, p).wait_recv()
            kept[...] = (x[...].astype(jnp.float32) + came[...].astype(jnp.float32)).astype(
                acc.dtype
            )
            src = kept
        if is_middle:
            start_all([hop(src, held(from_middle, p), mid_send, mid_recv, inner, p)], sent)
        else:
            start_all([hop(src, came, up_send, up_recv, inner, p)], sent)

    def spread_out(p):
        out, came = term(out_refs, p), held(from_middle, p)
        if is_middle:
            src = held(acc, p) if has_outer else term(x_refs, p)
            hop(src, came, mid_send, mid_recv, inner, p).wait_recv()
            out[...] = (src[...].astype(jnp.float32) + came[...].astype(jnp.float32)).astype(
                acc.dtype
            )
        else:
            hop(out, out, down_send, down_recv, inner, p).wait_recv()
        if has_outer:
            start_all([hop(out, out, down_send, down_recv, outer, p)], sent)

    lag = min(pieces, lag * (1 + 2 * to_middle)) if has_outer else pieces
    for p in range(pieces + lag):
        if p < pieces:
            gather(p)
        if p >= lag:
            spread_out(p - lag)
    for copy in sent:
        copy.wait_send()


def tensor_sum_kernel(n, count, pieces, rows, lag, *refs):
    x_refs, out_refs = refs[:count], refs[count : 2 * count]
    acc, from_outer, from_middle = refs[2 * count : 2 * count + 3]
    sems = refs[2 * count + 3 :]
    me = lax.axis_index("tensor")
    for d in range(n):

        @pl.when(me == d)
        def role():
            greet([{"tensor": at} for at in (d - 1, d + 1) if 0 <= at < n])
            middle_role(
                d, n, pieces, rows, lag, x_refs, out_refs, acc, from_outer, from_middle, sems
            )


def piece_count(rows, most):
    units = rows // ROW_TILE
    return max(p for p in range(1, most + 1) if units % p == 0)


def tensor_sum(*terms):
    n = lax.axis_size("tensor")
    if n == 1:
        return list(terms)
    count = len(terms)
    shape, dtype = terms[0].shape, terms[0].dtype
    each = piece_count(shape[0], 12)
    rows = shape[0] // each
    pieces = each * count
    sem = pltpu.SemaphoreType.DMA((pieces,))
    return pl.pallas_call(
        functools.partial(tensor_sum_kernel, n, count, pieces, rows, 2),
        out_shape=[jax.ShapeDtypeStruct(shape, dtype)] * count,
        in_specs=[VMEM] * count,
        out_specs=[VMEM] * count,
        scratch_shapes=[pltpu.VMEM((shape[0] * count, shape[1]), dtype)] * 3 + [sem] * 6,
        compiler_params=pltpu.CompilerParams(
            collective_id=0 if count == 1 else 6, has_side_effects=True
        ),
        cost_estimate=link_cost(100 * count * terms[0].size * dtype.itemsize),
        name="tensor_sum",
    )(*terms)


def opening_kernel(
    sizes,
    part_ref,
    add_ref,
    bias_ref,
    mod_ref,
    bias_all,
    held,
    ctx_send,
    ctx_recv,
    col_send,
    col_recv,
    bias_send,
    bias_recv,
):
    n_sec, n_ten, n_ctx = sizes
    sec, ten, ctx = (lax.axis_index(name) for name in ("section", "tensor", "ctx"))
    ctxs = [lax.rem(ctx + k, n_ctx) for k in range(n_ctx)]
    steps = [(a, b) for a in range(n_sec) for b in range(n_ten) if (a, b) != (0, 0)]
    places = [
        {"section": lax.rem(sec + a, n_sec), "tensor": lax.rem(ten + b, n_ten)} for a, b in steps
    ]
    greet([{"ctx": c} for c in ctxs[1:]] + places)
    sent = []

    def across(k, slot):
        return remote(
            part_ref, held.at[slot], ctx_send.at[k - 1], ctx_recv.at[k - 1], ctx=ctxs[k]
        )

    def biases(k, slot):
        return remote(
            bias_ref,
            bias_all.at[slot],
            bias_send.at[k - 1],
            bias_recv.at[k - 1],
            section=lax.rem(sec + k, n_sec),
        )

    for k in range(1, n_ctx):
        start_all([across(k, ctx)], sent)
    for k in range(1, n_sec):
        start_all([biases(k, sec)], sent)
    held[ctx] = part_ref[...]
    bias_all[sec] = bias_ref[...]
    for k in range(1, n_ctx):
        across(k, lax.rem(ctx + n_ctx - k, n_ctx)).wait_recv()
    total = add_ref[...]
    for k in range(n_ctx):
        total = total + held[k]
    mod_ref[sec, ten] = total

    def column(at, block):
        return remote(block, block, col_send.at[at], col_recv.at[at], **places[at])

    for at in range(len(steps)):
        start_all([column(at, mod_ref.at[sec, ten])], sent)
    for at, (a, b) in enumerate(steps):
        theirs = mod_ref.at[lax.rem(sec + n_sec - a, n_sec), lax.rem(ten + n_ten - b, n_ten)]
        column(at, theirs).wait_recv()
    for k in range(1, n_sec):
        biases(k, lax.rem(sec + n_sec - k, n_sec)).wait_recv()
    for copy in sent:
        copy.wait_send()


def opening(part, add, bias):
    sizes = n_sec, n_ten, n_ctx = tuple(
        lax.axis_size(name) for name in ("section", "tensor", "ctx")
    )
    dma = pltpu.SemaphoreType.DMA
    return pl.pallas_call(
        functools.partial(opening_kernel, sizes),
        out_shape=[
            jax.ShapeDtypeStruct((n_sec, n_ten) + part.shape, part.dtype),
            jax.ShapeDtypeStruct((n_sec,) + bias.shape, bias.dtype),
        ],
        in_specs=[VMEM] * 3,
        out_specs=[VMEM] * 2,
        scratch_shapes=[
            pltpu.VMEM((n_ctx,) + part.shape, part.dtype),
            dma((max(n_ctx - 1, 1),)),
            dma((max(n_ctx - 1, 1),)),
            dma((n_sec * n_ten,)),
            dma((n_sec * n_ten,)),
            dma((max(n_sec - 1, 1),)),
            dma((max(n_sec - 1, 1),)),
        ],
        compiler_params=pltpu.CompilerParams(collective_id=1, has_side_effects=True),
        cost_estimate=link_cost(40 * n_sec * n_ten * part.size * part.dtype.itemsize),
        name="opening",
    )(part, add, bias)


def group_peers(n_sec, n_ctx):
    ni = inner_size(n_ctx)
    no = n_ctx // ni
    sec, ctx = lax.axis_index("section"), lax.axis_index("ctx")
    i, o = lax.rem(ctx, ni), lax.div(ctx, ni)
    far = {
        (a, b): {"section": lax.rem(sec + a, n_sec), "ctx": lax.rem(o + b, no) * ni + i}
        for a in range(n_sec)
        for b in range(no)
        if (a, b) != (0, 0)
    }
    near = {m: {"ctx": o * ni + lax.rem(i + m, ni)} for m in range(1, ni)}
    return sec, i, o, ni, no, far, near


def spread_kernel(n_sec, n_ctx, own_ref, both_ref, own_all, both_all, *sems):
    far_send, far_recv, near_send, near_recv, own_sem = sems
    sec, i, o, ni, no, far, near = group_peers(n_sec, n_ctx)
    greet(list(far.values()) + list(near.values()))
    sent = []
    me = o * ni + i

    def far_copies(step):
        a, b = step
        at = a * no + b
        copies = []
        if a == 0:
            copies.append(
                remote(
                    own_ref, own_all.at[me], far_send.at[0, at], far_recv.at[0, at], **far[step]
                )
            )
        copies.append(
            remote(
                both_ref, both_all.at[sec, me], far_send.at[1, at], far_recv.at[1, at], **far[step]
            )
        )
        return copies

    def near_copies(m, a, b, own_src, both_src, s_at, c_at):
        at = a * no + b
        copies = []
        if a == 0:
            copies.append(
                remote(
                    own_src,
                    own_all.at[c_at],
                    near_send.at[0, m - 1, at],
                    near_recv.at[0, m - 1, at],
                    **near[m],
                )
            )
        copies.append(
            remote(
                both_src,
                both_all.at[s_at, c_at],
                near_send.at[1, m - 1, at],
                near_recv.at[1, m - 1, at],
                **near[m],
            )
        )
        return copies

    for step in far:
        start_all(far_copies(step), sent)
    for m in near:
        start_all(near_copies(m, 0, 0, own_ref, both_ref, sec, me), sent)
    keep = [
        pltpu.make_async_copy(own_ref, own_all.at[me], own_sem.at[0]),
        pltpu.make_async_copy(both_ref, both_all.at[sec, me], own_sem.at[1]),
    ]
    for copy in keep:
        copy.start()
    for step in far:
        a, b = step
        for copy in far_copies(step):
            copy.wait_recv()
        s_at = lax.rem(sec + n_sec - a, n_sec)
        c_at = lax.rem(o + no - b, no) * ni + i
        for m in near:
            start_all(
                near_copies(m, a, b, own_all.at[c_at], both_all.at[s_at, c_at], s_at, c_at), sent
            )
    for m in near:
        for a in range(n_sec):
            for b in range(no):
                s_at = lax.rem(sec + n_sec - a, n_sec)
                c_at = lax.rem(o + no - b, no) * ni + lax.rem(i + ni - m, ni)
                for copy in near_copies(
                    m, a, b, own_all.at[c_at], both_all.at[s_at, c_at], s_at, c_at
                ):
                    copy.wait_recv()
    for copy in keep:
        copy.wait()
    for copy in sent:
        copy.wait_send()


def spread(own, both):
    n_sec, n_ctx = lax.axis_size("section"), lax.axis_size("ctx")
    ni = inner_size(n_ctx)
    no = n_ctx // ni
    dma = pltpu.SemaphoreType.DMA
    return pl.pallas_call(
        functools.partial(spread_kernel, n_sec, n_ctx),
        out_shape=[
            jax.ShapeDtypeStruct((n_ctx,) + own.shape, own.dtype),
            jax.ShapeDtypeStruct((n_sec, n_ctx) + both.shape, both.dtype),
        ],
        in_specs=[VMEM, VMEM],
        out_specs=[VMEM, VMEM],
        scratch_shapes=[
            dma((2, n_sec * no)),
            dma((2, n_sec * no)),
            dma((2, ni, n_sec * no)),
            dma((2, ni, n_sec * no)),
            dma((2,)),
        ],
        compiler_params=pltpu.CompilerParams(collective_id=2, has_side_effects=True),
        name="spread",
    )(own, both)


def owner_kernel(n_sec, n_ctx, own_ref, both_ref, own_out, both_out, *refs):
    own_pair, both_pair, own_far, both_far = refs[:4]
    far_send, far_recv, near_send, near_recv = refs[4:]
    sec, i, o, ni, no, far, near = group_peers(n_sec, n_ctx)
    greet(list(far.values()) + list(near.values()))
    sent = []

    def near_copies(m, a, b):
        to = lax.rem(i + m, ni)
        s_at, o_at = lax.rem(sec + a, n_sec), lax.rem(o + b, no)
        at = a * no + b
        copies = []
        if a == 0:
            copies.append(
                remote(
                    own_ref.at[o_at * ni + to],
                    own_pair.at[m - 1, b],
                    near_send.at[0, m - 1, at],
                    near_recv.at[0, m - 1, at],
                    **near[m],
                )
            )
        copies.append(
            remote(
                both_ref.at[s_at, o_at * ni + to],
                both_pair.at[m - 1, at],
                near_send.at[1, m - 1, at],
                near_recv.at[1, m - 1, at],
                **near[m],
            )
        )
        return copies

    order = list(far) + [(0, 0)]
    for step in order:
        for m in near:
            start_all(near_copies(m, *step), sent)

    def far_copies(a, b):
        at = a * no + b
        copies = []
        if a == 0:
            copies.append(
                remote(
                    own_pair.at[ni - 1, b],
                    own_far.at[b],
                    far_send.at[0, at],
                    far_recv.at[0, at],
                    **far[(a, b)],
                )
            )
        copies.append(
            remote(
                both_pair.at[ni - 1, at],
                both_far.at[at],
                far_send.at[1, at],
                far_recv.at[1, at],
                **far[(a, b)],
            )
        )
        return copies

    for a, b in order:
        s_at, c_at = lax.rem(sec + a, n_sec), lax.rem(o + b, no) * ni + i
        at = a * no + b
        for m in near:
            for copy in near_copies(m, a, b):
                copy.wait_recv()
        total_both = both_ref[s_at, c_at].astype(jnp.float32)
        for m in near:
            total_both = total_both + both_pair[m - 1, at].astype(jnp.float32)
        total_own = None
        if a == 0:
            total_own = own_ref[c_at].astype(jnp.float32)
            for m in near:
                total_own = total_own + own_pair[m - 1, b].astype(jnp.float32)
        if (a, b) == (0, 0):
            own_out[...] = total_own
            both_out[...] = total_both
        else:
            if a == 0:
                own_pair[ni - 1, b] = total_own.astype(own_pair.dtype)
            both_pair[ni - 1, at] = total_both.astype(both_pair.dtype)
            start_all(far_copies(a, b), sent)
    for a, b in far:
        for copy in far_copies(a, b):
            copy.wait_recv()
        if a == 0:
            own_out[...] += own_far[b].astype(jnp.float32)
        both_out[...] += both_far[a * no + b].astype(jnp.float32)
    for copy in sent:
        copy.wait_send()


def owner_sum(own, both):
    n_sec, n_ctx = lax.axis_size("section"), lax.axis_size("ctx")
    ni = inner_size(n_ctx)
    no = n_ctx // ni
    dma = pltpu.SemaphoreType.DMA
    own_shape, both_shape = own.shape[1:], both.shape[2:]
    return pl.pallas_call(
        functools.partial(owner_kernel, n_sec, n_ctx),
        out_shape=[
            jax.ShapeDtypeStruct(own_shape, jnp.float32),
            jax.ShapeDtypeStruct(both_shape, jnp.float32),
        ],
        in_specs=[VMEM, VMEM],
        out_specs=[VMEM, VMEM],
        scratch_shapes=[
            pltpu.VMEM((ni, no) + own_shape, own.dtype),
            pltpu.VMEM((ni, n_sec * no) + both_shape, both.dtype),
            pltpu.VMEM((no,) + own_shape, own.dtype),
            pltpu.VMEM((n_sec * no,) + both_shape, both.dtype),
            dma((2, n_sec * no)),
            dma((2, n_sec * no)),
            dma((2, ni, n_sec * no)),
            dma((2, ni, n_sec * no)),
        ],
        compiler_params=pltpu.CompilerParams(collective_id=3, has_side_effects=True),
        name="owner_sum",
    )(own, both)


def small_kernel(axes, sizes, x_ref, out_ref, held, send, recv):
    at = [lax.axis_index(name) for name in axes]
    steps = [(a, b) for a in range(sizes[0]) for b in range(sizes[1])]
    places = [
        [lax.rem(here + sign * step + size, size) for here, step, size in zip(at, pair, sizes)]
        for sign in (1, -1)
        for pair in steps
    ]
    to, source = places[: len(steps)], places[len(steps) :]
    where = [dict(zip(axes, place)) for place in to]
    greet(where[1:])

    def block(place):
        return place[0] if x_ref.shape[0] > 1 else 0

    def copy(k, slot):
        return remote(
            x_ref.at[block(to[k])],
            held.at[slot[0] * sizes[1] + slot[1]],
            send.at[k - 1],
            recv.at[k - 1],
            **where[k],
        )

    copies = [copy(k, at) for k in range(1, len(steps))]
    for started in copies:
        started.start()
    held[at[0] * sizes[1] + at[1]] = x_ref[block(at)]
    for k in range(1, len(steps)):
        copy(k, source[k]).wait_recv()
    total = held[0]
    for k in range(1, len(steps)):
        total = total + held[k]
    out_ref[...] = total
    for started in copies:
        started.wait_send()


def small_sum(x, axes, collective_id):
    sizes = tuple(lax.axis_size(name) for name in axes)
    n = sizes[0] * sizes[1]
    dma = pltpu.SemaphoreType.DMA((max(n - 1, 1),))
    return pl.pallas_call(
        functools.partial(small_kernel, axes, sizes),
        out_shape=jax.ShapeDtypeStruct(x.shape[1:], x.dtype),
        in_specs=[VMEM],
        out_specs=VMEM,
        scratch_shapes=[pltpu.VMEM((n,) + x.shape[1:], x.dtype), dma, dma],
        compiler_params=pltpu.CompilerParams(collective_id=collective_id, has_side_effects=True),
        cost_estimate=link_cost(100 * n * x[0].size * x.dtype.itemsize),
        name="small_sum",
    )(x)


def packed(pieces, width):
    flat = jnp.concatenate([p.reshape(-1) for p in pieces])
    rows = -(-flat.shape[0] // width)
    rows = -(-rows // 8) * 8
    return jnp.pad(flat, (0, rows * width - flat.shape[0])).reshape(rows, width)


def compact(array):
    return packed([array], -(-array.size // 8))


def unpacked(block, shapes):
    flat, at, out = block.reshape(-1), 0, []
    for shape in shapes:
        size = math.prod(shape)
        out.append(flat[at : at + size].reshape(shape))
        at += size
    return out


def layer_norm(values):
    centre = jnp.mean(values, axis=-1, keepdims=True)
    centred = values - centre
    variance = jnp.mean(centred * centred, axis=-1, keepdims=True)
    inverse = lax.rsqrt(variance + EPSILON)
    return (centred * inverse, inverse)


def norm_back(normed, inverse, upstream):
    mean_grad = jnp.mean(upstream, axis=-1, keepdims=True)
    mean_cross = jnp.mean(upstream * normed, axis=-1, keepdims=True)
    return inverse * (upstream - mean_grad - normed * mean_cross)


def gelu_back(pre_act, upstream):
    unused_out, pullback = jax.vjp(
        lambda pre_value: jax.nn.gelu(pre_value, approximate=True), pre_act
    )
    return pullback(upstream)[0]


def heads(array):
    cols = array.shape[-2]
    return array.reshape(*array.shape[:-2], cols // HD, HD, array.shape[-1])


def score_columns(queries, keys):
    softmax_scale = 1.0 / math.sqrt(HD)
    return (
        jnp.einsum(
            "nhdk,hdq->hnkq", heads(keys), heads(queries), preferred_element_type=jnp.float32
        )
        * softmax_scale
    )


def attend(queries, keys, values):
    scores = score_columns(queries, keys)
    row_peak = jnp.max(scores, axis=(1, 2), keepdims=True)
    log_total = row_peak + jnp.log(jnp.sum(jnp.exp(scores - row_peak), axis=(1, 2), keepdims=True))
    prob_bf = jnp.exp(scores - log_total).astype(jnp.bfloat16)
    context = jnp.einsum(
        "nhdk,hnkq->hdq", heads(values), prob_bf, preferred_element_type=jnp.float32
    )
    return context.astype(jnp.bfloat16).reshape(queries.shape), log_total


def attention_grads(queries, keys, values, log_total, context, context_grad):
    softmax_scale = 1.0 / math.sqrt(HD)
    query_heads, grad_heads = heads(queries), heads(context_grad)
    delta = jnp.sum(
        grad_heads.astype(jnp.float32) * heads(context).astype(jnp.float32), axis=1
    )[:, None, None, :]
    prob_full = jnp.exp(score_columns(queries, keys) - log_total)
    prob_bf = prob_full.astype(jnp.bfloat16)
    prob_grad = jnp.einsum(
        "nhdk,hdq->hnkq", heads(values), grad_heads, preferred_element_type=jnp.float32
    )
    score_grad = (prob_full * (prob_grad - delta)).astype(jnp.bfloat16)
    query_grad = (
        jnp.einsum(
            "nhdk,hnkq->hdq", heads(keys), score_grad, preferred_element_type=jnp.float32
        )
        * softmax_scale
    ).reshape(queries.shape)
    key_part = (
        jnp.einsum("hnkq,hdq->nhdk", score_grad, query_heads, preferred_element_type=jnp.float32)
        * softmax_scale
    ).reshape(keys.shape)
    value_part = jnp.einsum(
        "hnkq,hdq->nhdk", prob_bf, grad_heads, preferred_element_type=jnp.float32
    ).reshape(values.shape)
    both = jnp.concatenate(
        [key_part.astype(jnp.bfloat16), value_part.astype(jnp.bfloat16)], axis=1
    )
    return query_grad, both


def contract(left, right, left_dim, right_dim):
    return lax.dot_general(
        left, right, (((left_dim,), (right_dim,)), ((), ())), preferred_element_type=jnp.float32
    )


class Rows:
    def __init__(self, latents, section):
        n_sec = lax.axis_size("section")
        self.n_sec = n_sec
        total, self.tokens, self.width = latents.shape
        self.section = section
        self.full = total // n_sec
        self.rest = total - self.full * n_sec
        self.part = self.tokens // n_sec
        self.own_rows = self.full * self.tokens
        self.both_rows = self.rest * self.part
        self.rows = self.own_rows + self.both_rows

    def take(self, array):
        own = lax.dynamic_slice_in_dim(array, self.section * self.full, self.full, 0)
        both = lax.dynamic_slice_in_dim(
            array[self.full * self.n_sec :], self.section * self.part, self.part, 1
        )
        return jnp.concatenate(
            [own.reshape(self.own_rows, -1), both.reshape(self.both_rows, -1)], axis=0
        )

    def split(self, array):
        return (
            array[: self.own_rows].reshape(self.full, self.tokens, -1),
            array[self.own_rows :].reshape(self.rest, self.part, -1),
        )

    def spans(self):
        out = [(at * self.tokens, self.tokens) for at in range(self.full)]
        return out + [
            (self.own_rows + at * self.part, self.part) for at in range(self.rest)
        ]

    def columns(self, array):
        return [array[:, start : start + size] for start, size in self.spans()]

    def mods(self, modulation):
        own = lax.dynamic_slice_in_dim(modulation, self.section * self.full, self.full, 0)
        return jnp.concatenate([own, modulation[self.full * self.n_sec :]], axis=0)

    def wide(self, pieces):
        row = lax.broadcasted_iota(jnp.int32, (self.rows, 1), 0)
        out = pieces[-1][None, :]
        for (start, size), piece in reversed(list(zip(self.spans(), pieces))[:-1]):
            out = jnp.where(row < start + size, piece[None, :], out)
        return out

    def sums(self, array):
        return jnp.sum(array.reshape(-1, self.part, self.width), axis=1)

    def placed(self, sums):
        runs = self.tokens // self.part
        own = sums[: self.full * runs].reshape(self.full, runs, -1).sum(axis=1)
        mine = [
            jnp.where(self.section == at // self.full, own[at % self.full], 0.0)
            for at in range(self.full * self.n_sec)
        ]
        both = [sums[self.full * runs + at] for at in range(self.rest)]
        return jnp.stack(mine + both)

    def assembled(self, per_block, received):
        own = per_block[-1]
        for b in range(self.n_sec - 1):
            own = jnp.where(self.section == b, per_block[b], own)
        others = []
        for k in range(1, self.n_sec):
            rows = received[-1][k - 1]
            for b in range(self.n_sec - 1):
                rows = jnp.where(self.section == b, received[b][k - 1], rows)
            others.append(rows)
        whole, shared = [], []
        for source in range(self.n_sec):
            rows = own
            for k, other in enumerate(others, 1):
                rows = jnp.where(lax.rem(self.section + k, self.n_sec) == source, other, rows)
            first, both = self.split(rows)
            whole.append(first)
            shared.append(both)
        return jnp.concatenate(whole + [jnp.concatenate(shared, axis=1)], axis=0)


def gathered(key_value, rows):
    spans = rows.spans()
    cols = [key_value[:, start : start + size] for start, size in spans]
    own = jnp.concatenate(cols[: rows.full], axis=0)
    both = jnp.concatenate(cols[rows.full :], axis=0)
    own_all, both_all = spread(own, both)
    both_all = both_all.reshape(-1, *both.shape)
    high = key_value.shape[0]
    return [own_all[:, at * high : (at + 1) * high] for at in range(rows.full)] + [
        both_all[:, at * high : (at + 1) * high] for at in range(rows.rest)
    ]


def returned(parts, rows):
    high = parts[0].shape[1]
    own = jnp.concatenate(parts[: rows.full], axis=1)
    both = jnp.concatenate(parts[rows.full :], axis=1)
    own, both = owner_sum(own, both.reshape(rows.n_sec, -1, *both.shape[1:]))
    return jnp.concatenate(
        [own[at * high : (at + 1) * high] for at in range(rows.full)]
        + [both[at * high : (at + 1) * high] for at in range(rows.rest)],
        axis=1,
    )


def forward_block(rows, residual, mods, w_qkv, biases, prepare, mlp_weights, last):
    b_qv, b_out, b_fc1, b_fc2 = biases
    local_cols = w_qkv.shape[0] // 3
    shift_a, scale_a, gate_a, shift_m, scale_m, gate_m = (
        rows.wide([mods[at, k] for at in range(mods.shape[0])]) for k in range(6)
    )
    normed_a, inverse_a = layer_norm(residual)
    attn_in = (normed_a * (1.0 + scale_a) + shift_a).astype(jnp.bfloat16)
    projected = contract(w_qkv, attn_in, 1, 1)
    bias = jnp.concatenate([b_qv[0], jnp.zeros_like(b_qv[0]), b_qv[1]])
    projected = (projected + bias[:, None]).astype(jnp.bfloat16)
    queries = rows.columns(projected[:local_cols])
    keys_values, w_out, sends = prepare(gathered(projected[local_cols:], rows))
    attended = [
        attend(q, kv[:, :local_cols], kv[:, local_cols:])
        for q, kv in zip(queries, keys_values)
    ]
    context = row_major(jnp.concatenate([row_major(c) for c, _ in attended], axis=1))
    attn_term = contract(context, w_out, 0, 0)
    (attn_sum,), moved = beside(tensor_sum, [attn_term.astype(jnp.bfloat16)], sends)
    w_fc1, w_fc2 = mlp_weights(moved)
    attn_out = attn_sum.astype(jnp.float32) + b_out
    middle = residual + gate_a * attn_out
    normed_m, inverse_m = layer_norm(middle)
    mlp_in = (normed_m * (1.0 + scale_m) + shift_m).astype(jnp.bfloat16)
    pre_act = jnp.dot(mlp_in, w_fc1, preferred_element_type=jnp.float32) + b_fc1
    hidden = jax.nn.gelu(pre_act, approximate=True).astype(jnp.bfloat16)
    mlp_term = jnp.dot(hidden, w_fc2, preferred_element_type=jnp.float32).astype(jnp.bfloat16)

    def close(mlp_sum):
        mlp_out = mlp_sum.astype(jnp.float32) + b_fc2
        return mlp_out, (middle + gate_m * mlp_out).astype(jnp.bfloat16)

    mlp_out, block_res = (None, None) if last else close(tensor_sum(mlp_term)[0])
    stored = (
        normed_a,
        inverse_a,
        attn_in,
        queries,
        keys_values,
        [log_total for _, log_total in attended],
        context,
        attn_out,
        normed_m,
        inverse_m,
        mlp_in,
        pre_act,
        hidden,
        mlp_out,
    )
    return block_res, stored, moved, (mlp_term, close) if last else None


def backward_block(rows, upstream, stored, mods, weights, block, firsts, seconds, pending):
    w_qkv, w_out, w_fc1, w_fc2 = weights
    (
        normed_a,
        inverse_a,
        attn_in,
        queries,
        keys_values,
        log_totals,
        context,
        attn_out,
        normed_m,
        inverse_m,
        mlp_in,
        pre_act,
        hidden,
        mlp_out,
    ) = stored
    local_cols = w_qkv.shape[0] // 3
    shift_a, scale_a, gate_a, shift_m, scale_m, gate_m = (
        rows.wide([mods[at, k] for at in range(mods.shape[0])]) for k in range(6)
    )
    mlp_grad = upstream * gate_m
    mlp_grad_b = mlp_grad.astype(jnp.bfloat16)
    grad_b2 = jnp.sum(mlp_grad, axis=0)
    pre_grad = gelu_back(pre_act, jnp.dot(mlp_grad_b, w_fc2.T, preferred_element_type=jnp.float32))
    pre_grad_b = pre_grad.astype(jnp.bfloat16)
    grad_b1 = jnp.sum(pre_grad, axis=0)
    mlp_pair = inner_pair(
        [contract(mlp_grad_b, hidden, 0, 0), contract(mlp_in, pre_grad_b, 0, 0)]
    )
    mlp_term = jnp.dot(pre_grad_b, w_fc1.T, preferred_element_type=jnp.float32)
    terms = [mlp_term.astype(jnp.bfloat16)]
    if pending:
        terms.append(pending[0])
    outer = outer_sends(mlp_pair)
    (mlp_in_grad, *sums), moved = beside(tensor_sum, terms, outer + firsts)
    block_res = None
    if pending:
        mlp_out, block_res = pending[1](sums[0])
    gate_m_grad = rows.sums(upstream * mlp_out)
    first_moved = moved[len(outer) :]
    mlp_share = outer_total(mlp_pair, moved[: len(outer)])
    mlp_in_grad = mlp_in_grad.astype(jnp.float32)
    shift_m_grad = rows.sums(mlp_in_grad)
    scale_m_grad = rows.sums(mlp_in_grad * normed_m)
    middle_grad = upstream + norm_back(normed_m, inverse_m, mlp_in_grad * (1.0 + scale_m))
    gate_a_grad = rows.sums(middle_grad * attn_out)
    attn_grad = middle_grad * gate_a
    attn_grad_b = attn_grad.astype(jnp.bfloat16)
    grad_bo = jnp.sum(attn_grad, axis=0)
    context_grad = contract(w_out, attn_grad_b, 1, 1).astype(jnp.bfloat16)
    query_grads, key_value_parts = zip(
        *(
            attention_grads(q, kv[:, :local_cols], kv[:, local_cols:], log_total, c, cg)
            for q, kv, log_total, c, cg in zip(
                queries, keys_values, log_totals, rows.columns(context), rows.columns(context_grad)
            )
        )
    )
    query_grad = row_major(jnp.concatenate([row_major(g) for g in query_grads], axis=1))
    key_value_grad = returned(key_value_parts, rows)
    grad_bqv = jnp.stack(
        [jnp.sum(query_grad, axis=1), jnp.sum(key_value_grad[local_cols:], axis=1)]
    )
    qkv_grad_b = jnp.concatenate([query_grad, key_value_grad], axis=0).astype(jnp.bfloat16)
    qkv_rows, context_rows = row_major(row_major(qkv_grad_b).T), row_major(row_major(context).T)
    attn_term = contract(qkv_rows, w_qkv, 1, 0)
    attn_pairs = [
        inner_pair([contract(attn_in, qkv_rows, 0, 0)]),
        inner_pair([contract(attn_grad_b, context_rows, 0, 0)]),
    ]
    outers = [outer_sends(pair) for pair in attn_pairs]
    across = block_sends(mlp_share, block)
    sends = [*outers, across, seconds]
    ((attn_in_grad,), moved) = beside(
        tensor_sum, [attn_term.astype(jnp.bfloat16)], [send for part in sends for send in part]
    )
    came = []
    for part in sends:
        came.append(moved[: len(part)])
        moved = moved[len(part) :]
    attn_shares = [outer_total(pair, part) for pair, part in zip(attn_pairs, came)]
    mlp_share = block_total(mlp_share, came[-2])
    second_moved = came[-1]
    attn_in_grad = attn_in_grad.astype(jnp.float32)
    shift_a_grad = rows.sums(attn_in_grad)
    scale_a_grad = rows.sums(attn_in_grad * normed_a)
    input_grad = middle_grad + norm_back(normed_a, inverse_a, attn_in_grad * (1.0 + scale_a))
    mod_grad = jnp.concatenate(
        [shift_a_grad, scale_a_grad, gate_a_grad, shift_m_grad, scale_m_grad, gate_m_grad], axis=1
    )
    return (
        input_grad,
        mod_grad,
        (grad_bqv, grad_bo, grad_b1, grad_b2),
        (mlp_share, *attn_shares),
        block_res,
        first_moved,
        second_moved,
    )


def to_inner(value, by):
    n = lax.axis_size("ctx")
    ni = inner_size(n)
    return lax.ppermute(value, "ctx", [(a, a // ni * ni + (a + by) % ni) for a in range(n)])


def to_outer(value, by):
    n = lax.axis_size("ctx")
    ni = inner_size(n)
    return lax.ppermute(value, "ctx", [(a, (a + by * ni) % n) for a in range(n)])


def to_section(value, by):
    n = lax.axis_size("section")
    return lax.ppermute(value, "section", [(a, (a + by) % n) for a in range(n)])


def to_block(value, block, by):
    n = lax.axis_size("section")
    return lax.ppermute(value, "section", [((block + by) % n, block)])


def ctx_place():
    n = lax.axis_size("ctx")
    ni = inner_size(n)
    at = lax.axis_index("ctx")
    return n // ni, ni, lax.div(at, ni), lax.rem(at, ni)


def beside(kernel, args, sends):
    args, values = lax.optimization_barrier((args, [value for value, _ in sends]))
    moved = [move(value) for value, (_, move) in zip(values, sends)]
    return lax.optimization_barrier((kernel(*args), moved))


def half_of(weights):
    _, ni, _, i = ctx_place()
    sizes = [w.shape[0] // ni for w in weights]
    return jnp.concatenate(
        [lax.dynamic_slice_in_dim(w, i * size, size, 0) for w, size in zip(weights, sizes)]
    )


def joined(own, passed, weights):
    _, ni, _, i = ctx_place()
    found, start = [], 0
    for w in weights:
        size = w.shape[0] // ni
        parts = [piece[start : start + size] for piece in [own] + passed]
        start += size
        ordered = []
        for at in range(ni):
            piece = parts[0]
            for m in range(1, ni):
                piece = jnp.where(lax.rem(i + ni - m, ni) == at, parts[m], piece)
            ordered.append(piece)
        found.append(jnp.concatenate(ordered))
    return found


def chosen_blocks(weights, others):
    n_sec = lax.axis_size("section")
    section = lax.axis_index("section")
    blocks = []
    for b in range(n_sec):
        chosen = list(weights)
        for k, found in enumerate(others, 1):
            is_source = lax.rem(section + n_sec - k, n_sec) == b
            chosen = [jnp.where(is_source, new, old) for new, old in zip(found, chosen)]
        blocks.append(chosen)
    return blocks


def fetched(weights):
    n_sec = lax.axis_size("section")
    groups = [
        [at for at, w in enumerate(weights) if w.shape[1] == width]
        for width in sorted({w.shape[1] for w in weights})
    ]
    halves = [half_of([weights[at] for at in group]) for group in groups]
    return groups, [[to_section(half, k) for k in range(1, n_sec)] for half in halves]


def passing(fetch):
    _, ni, _, _ = ctx_place()
    return [
        (half, functools.partial(to_inner, by=m))
        for of_group in fetch[1]
        for half in of_group
        for m in range(1, ni)
    ]


def every_block(weights, fetch, passed):
    _, ni, _, _ = ctx_place()
    n_sec = lax.axis_size("section")
    others = [[None] * len(weights) for _ in range(n_sec - 1)]
    passed = list(passed)
    for group, of_group in zip(*fetch):
        for k, half in enumerate(of_group):
            rest = [passed.pop(0) for _ in range(1, ni)]
            for at, whole in zip(group, joined(half, rest, [weights[at] for at in group])):
                others[k][at] = whole
    return chosen_blocks(weights, others)


def inner_pair(terms):
    no, ni, _, i = ctx_place()
    terms = [
        row_major(t.astype(jnp.bfloat16)).reshape(no, ni, -1, t.shape[-1]) for t in terms
    ]

    def inner(at):
        return row_major(
            jnp.concatenate(
                [lax.dynamic_index_in_dim(t, at, 1, keepdims=False) for t in terms], axis=1
            )
        )

    pair = inner(i).astype(jnp.float32)
    for m in range(1, ni):
        pair = pair + to_inner(inner(lax.rem(i + m, ni)), m).astype(jnp.float32)
    return pair.astype(jnp.bfloat16)


def outer_sends(pair):
    no, _, o, _ = ctx_place()
    return [
        (
            lax.dynamic_index_in_dim(pair, lax.rem(o + m, no), 0, keepdims=False),
            functools.partial(to_outer, by=m),
        )
        for m in range(1, no)
    ]


def outer_total(pair, moved):
    _, _, o, _ = ctx_place()
    total = lax.dynamic_index_in_dim(pair, o, 0, keepdims=False).astype(jnp.float32)
    for piece in moved:
        total = total + piece.astype(jnp.float32)
    return total


def block_sends(value, block):
    value = value.astype(jnp.bfloat16)
    return [
        (value, functools.partial(to_block, block=block, by=k))
        for k in range(1, lax.axis_size("section"))
    ]


def block_total(own, moved):
    for piece in moved:
        own = own + piece.astype(jnp.float32)
    return own


def local(
    latents,
    condition,
    cotangent,
    w_ada,
    b_ada,
    w_qkv,
    b_qv,
    w_out,
    b_out,
    w_fc1,
    b_fc1,
    w_fc2,
    b_fc2,
):
    section = lax.axis_index("section")
    n_sec = lax.axis_size("section")
    latent_total, token_count, width = latents.shape
    width_cols = b_ada.shape[-1]
    local_cols = w_qkv.shape[-1]
    rows = Rows(latents, section)
    cond_act = jax.nn.silu(condition).astype(jnp.bfloat16)
    mod_part = jnp.dot(cond_act, w_ada[0], preferred_element_type=jnp.float32)
    bias_shapes = [b_qv.shape[1:], b_out.shape[1:], b_fc1.shape[1:], b_fc2.shape[1:]]
    bias_flat = jnp.concatenate([b.reshape(-1) for b in (b_qv, b_out, b_fc1, b_fc2)])
    qkv_weights = [row_major(jnp.transpose(w_qkv[0], (1, 2, 0)).reshape(3 * local_cols, width))]
    qkv_fetch = fetched(qkv_weights)
    mod_all, bias_all = opening(
        compact(mod_part),
        compact(jnp.broadcast_to(b_ada, (latent_total, width_cols))),
        compact(bias_flat),
    )
    mod_all, fc1_weights = lax.optimization_barrier((mod_all, [w_fc1[0]]))
    fc1_fetch = fetched(fc1_weights)
    qkv_blocks = every_block(
        qkv_weights, qkv_fetch, [move(half) for half, move in passing(qkv_fetch)]
    )
    tensor = lax.axis_index("tensor")
    columns = mod_all.reshape(n_sec, -1, mod_all.shape[-2] * mod_all.shape[-1])
    columns = columns[..., : latent_total * width_cols]
    columns = columns.reshape(n_sec, -1, latent_total, width_cols)
    modulation = jnp.swapaxes(columns, 1, 2).reshape(n_sec, latent_total, 6, width)
    biases, mods = [], []
    for b in range(n_sec):
        biases.append(unpacked(bias_all[b], bias_shapes))
        mods.append(rows.mods(modulation[b]))
    residual = rows.take(latents)
    outs, out_moved, kept, out_blocks, mlp_blocks, pending = [], [], [], [], [], None
    for b in range(n_sec):
        if b == 0:
            late = []

            def prepare(keys_values):
                keys_values, weights = lax.optimization_barrier(
                    (keys_values, [w_out[0], w_fc2[0]])
                )
                for weight in weights:
                    late.append(([weight], fetched([weight])))
                weights, fetch = late[0]
                out_blocks.extend(
                    every_block(weights, fetch, [move(half) for half, move in passing(fetch)])
                )
                return keys_values, out_blocks[0][0], passing(fc1_fetch)

            def finish(moved):
                firsts = every_block(fc1_weights, fc1_fetch, moved)
                weights, fetch = late[1]
                seconds = every_block(
                    weights, fetch, [move(half) for half, move in passing(fetch)]
                )
                mlp_blocks.extend([*one, *two] for one, two in zip(firsts, seconds))
                return mlp_blocks[0]

        else:
            sends = block_sends(outs[-1], b - 1)

            def prepare(keys_values, sends=sends, b=b):
                return keys_values, out_blocks[b][0], sends

            def finish(moved, b=b):
                return mlp_blocks[b]

        residual, stored, moved, pending = forward_block(
            rows,
            residual.astype(jnp.float32),
            mods[b],
            qkv_blocks[b][0],
            biases[b],
            prepare,
            finish,
            b == n_sec - 1,
        )
        if b:
            out_moved.append(moved)
        outs.append(residual)
        kept.append(stored)
    upstream = rows.take(cotangent).astype(jnp.float32)
    in_grads, in_moved, small, shares = ([None] * n_sec for _ in range(4))
    out_moved.append([])
    firsts, seconds = [[], []], []
    for b in reversed(range(n_sec)):
        upstream, mod_grad, bias_grads, shares[b], block_res, first_moved, second_moved = (
            backward_block(
                rows,
                upstream,
                kept[b],
                mods[b],
                (*qkv_blocks[b], *out_blocks[b], *mlp_blocks[b]),
                b,
                [send for part in firsts for send in part],
                seconds,
                pending if b == n_sec - 1 else None,
            )
        )
        if b == n_sec - 1:
            outs[b] = block_res
        else:
            at = 0
            for which in (1, 2):
                part = first_moved[at : at + n_sec - 1]
                at += n_sec - 1
                shares[b + 1][which] = block_total(shares[b + 1][which], part)
            if b == n_sec - 2:
                out_moved[-1] = first_moved[at:]
            in_moved[b + 1] = second_moved
        shares[b] = list(shares[b])
        in_grads[b] = upstream.astype(jnp.bfloat16)
        cols = mod_grad[:, :width_cols]
        for t in range(1, lax.axis_size("tensor")):
            cols = jnp.where(tensor == t, mod_grad[:, t * width_cols : (t + 1) * width_cols], cols)
        small[b] = packed([rows.placed(cols), *bias_grads], width)
        firsts = [block_sends(share, b) for share in shares[b][1:]]
        if b == n_sec - 1:
            firsts.append(block_sends(outs[b], b))
        seconds = block_sends(in_grads[b], b)
    summed, in_moved[0] = beside(
        functools.partial(small_sum, axes=("section", "ctx"), collective_id=4),
        [jnp.stack(small)],
        seconds,
    )
    in_grad = rows.assembled(in_grads, in_moved).astype(jnp.float32)
    block_out = rows.assembled(outs, out_moved)
    mod_total, grad_bqv, grad_bo, grad_b1, grad_b2 = unpacked(
        summed, [(latent_total, width_cols)] + bias_shapes
    )
    mod_rounded = mod_total.astype(jnp.bfloat16)
    cond_part = jnp.dot(mod_rounded, w_ada[0].T, preferred_element_type=jnp.float32)
    cond_part = jnp.pad(cond_part, ((0, -latent_total % 8), (0, 0)))
    cond_sum, moved = beside(
        functools.partial(small_sum, axes=("section", "tensor"), collective_id=5),
        [cond_part[None]],
        firsts[0] + firsts[1],
    )
    cond_sum = cond_sum[:latent_total]
    for which in (1, 2):
        shares[0][which] = block_total(shares[0][which], moved[: n_sec - 1])
        moved = moved[n_sec - 1 :]

    def mine(which):
        out = shares[-1][which]
        for b in range(n_sec - 1):
            out = jnp.where(section == b, shares[b][which], out)
        return out

    mlp_share, qkv_share, out_share = mine(0), mine(1), mine(2)
    share_rows = mlp_share.shape[0] // 2
    grad_w_ada = jnp.dot(cond_act.T, mod_rounded, preferred_element_type=jnp.float32)[None]
    grad_b_ada = jnp.sum(mod_total, axis=0)[None]
    sigmoid_c = jax.nn.sigmoid(condition)
    cond_grad = cond_sum * sigmoid_c * (1.0 + condition * (1.0 - sigmoid_c))
    return (
        block_out[None],
        in_grad[None],
        cond_grad,
        grad_w_ada,
        grad_b_ada,
        qkv_share.reshape(1, share_rows, 3, local_cols),
        grad_bqv[None],
        out_share.T[None],
        grad_bo[None],
        mlp_share[share_rows:][None],
        grad_b1[None],
        mlp_share[:share_rows].T[None],
        grad_b2[None],
    )


def solution(mesh):
    return jax.shard_map(
        local,
        mesh=mesh,
        in_specs=(
            P(None, "ctx", None),
            P(None, "ctx"),
            P(None, "ctx", None),
            P("section", "ctx", "tensor"),
            P("section", "tensor"),
            P("section", None, None, "tensor"),
            P("section", None, "tensor"),
            P("section", "tensor", None),
            P("section", None),
            P("section", None, "tensor"),
            P("section", "tensor"),
            P("section", "tensor", None),
            P("section", None),
        ),
        out_specs=(
            P("section", None, "ctx", None),
            P("section", None, "ctx", None),
            P(None, "ctx"),
            P("section", "ctx", "tensor"),
            P("section", "tensor"),
            P("section", "ctx", None, "tensor"),
            P("section", None, "tensor"),
            P("section", "tensor", "ctx"),
            P("section", None),
            P("section", "ctx", "tensor"),
            P("section", "tensor"),
            P("section", "tensor", "ctx"),
            P("section", None),
        ),
        check_vma=False,
    )
```

```python
import functools
import math

import jax
import jax.numpy as jnp
from jax import lax
from jax.experimental import pallas as pl
from jax.experimental.layout import Layout, with_layout_constraint
from jax.experimental.pallas import tpu as pltpu
from jax.sharding import PartitionSpec as P

HD = 72
EPSILON = 1e-06
MESH = pl.DeviceIdType.MESH
ROW_TILE = 16
VMEM = pl.BlockSpec(memory_space=pltpu.VMEM)


def inner_size(n):
    return 2 if n % 2 == 0 else 1


def remote(src, dst, send, recv, **to):
    return pltpu.make_async_remote_copy(
        src_ref=src,
        dst_ref=dst,
        send_sem=send,
        recv_sem=recv,
        device_id=to,
        device_id_type=MESH,
    )


def greet(peers):
    barrier = pltpu.get_barrier_semaphore()
    for peer in peers:
        pl.semaphore_signal(barrier, inc=1, device_id=peer, device_id_type=MESH)
    pl.semaphore_wait(barrier, len(peers))


def row_major(array):
    return with_layout_constraint(array, Layout(tuple(range(array.ndim))))


def link_cost(moved):
    return pl.CostEstimate(flops=0, bytes_accessed=moved, transcendentals=0)


def start_all(copies, sent):
    for copy in copies:
        copy.start()
        sent.append(copy)


def middle_role(d, n, pieces, rows, lag, x_refs, out_refs, acc, from_outer, from_middle, sems):
    up_send, up_recv, mid_send, mid_recv, down_send, down_recv = sems
    half = n // 2
    left = d < half
    outer, inner = (d - 1, d + 1) if left else (d + 1, d - 1)
    has_outer = 0 <= outer < n
    is_middle = d in (half - 1, half)
    to_middle = half - 1 - d if left else d - half
    each = pieces // len(x_refs)

    def term(refs, p):
        return refs[p // each].at[pl.ds(p % each * rows, rows)]

    def held(ref, p):
        return ref.at[pl.ds(p * rows, rows)]

    def hop(src, dst, send, recv, to, p):
        return remote(src, dst, send.at[p], recv.at[p], tensor=to)

    sent = []

    def gather(p):
        x, kept, came = term(x_refs, p), held(acc, p), held(from_outer, p)
        src = x
        if has_outer:
            hop(x, came, up_send, up_recv, inner, p).wait_recv()
            kept[...] = (x[...].astype(jnp.float32) + came[...].astype(jnp.float32)).astype(
                acc.dtype
            )
            src = kept
        if is_middle:
            start_all([hop(src, held(from_middle, p), mid_send, mid_recv, inner, p)], sent)
        else:
            start_all([hop(src, came, up_send, up_recv, inner, p)], sent)

    def spread_out(p):
        out, came = term(out_refs, p), held(from_middle, p)
        if is_middle:
            src = held(acc, p) if has_outer else term(x_refs, p)
            hop(src, came, mid_send, mid_recv, inner, p).wait_recv()
            out[...] = (src[...].astype(jnp.float32) + came[...].astype(jnp.float32)).astype(
                acc.dtype
            )
        else:
            hop(out, out, down_send, down_recv, inner, p).wait_recv()
        if has_outer:
            start_all([hop(out, out, down_send, down_recv, outer, p)], sent)

    lag = min(pieces, lag * (1 + 2 * to_middle)) if has_outer else pieces
    for p in range(pieces + lag):
        if p < pieces:
            gather(p)
        if p >= lag:
            spread_out(p - lag)
    for copy in sent:
        copy.wait_send()


def tensor_sum_kernel(n, count, pieces, rows, lag, *refs):
    x_refs, out_refs = refs[:count], refs[count : 2 * count]
    acc, from_outer, from_middle = refs[2 * count : 2 * count + 3]
    sems = refs[2 * count + 3 :]
    me = lax.axis_index("tensor")
    for d in range(n):

        @pl.when(me == d)
        def role():
            greet([{"tensor": at} for at in (d - 1, d + 1) if 0 <= at < n])
            middle_role(
                d, n, pieces, rows, lag, x_refs, out_refs, acc, from_outer, from_middle, sems
            )


def piece_count(rows, most):
    units = rows // ROW_TILE
    return max(p for p in range(1, most + 1) if units % p == 0)


def tensor_sum(*terms):
    n = lax.axis_size("tensor")
    if n == 1:
        return list(terms)
    count = len(terms)
    shape, dtype = terms[0].shape, terms[0].dtype
    each = piece_count(shape[0], 12)
    rows = shape[0] // each
    pieces = each * count
    sem = pltpu.SemaphoreType.DMA((pieces,))
    return pl.pallas_call(
        functools.partial(tensor_sum_kernel, n, count, pieces, rows, 2),
        out_shape=[jax.ShapeDtypeStruct(shape, dtype)] * count,
        in_specs=[VMEM] * count,
        out_specs=[VMEM] * count,
        scratch_shapes=[pltpu.VMEM((shape[0] * count, shape[1]), dtype)] * 3 + [sem] * 6,
        compiler_params=pltpu.CompilerParams(
            collective_id=0 if count == 1 else 6, has_side_effects=True
        ),
        cost_estimate=link_cost(100 * count * terms[0].size * dtype.itemsize),
        name="tensor_sum",
    )(*terms)


def opening_kernel(
    sizes,
    part_ref,
    add_ref,
    bias_ref,
    mod_ref,
    bias_all,
    held,
    ctx_send,
    ctx_recv,
    col_send,
    col_recv,
    bias_send,
    bias_recv,
):
    n_sec, n_ten, n_ctx = sizes
    sec, ten, ctx = (lax.axis_index(name) for name in ("section", "tensor", "ctx"))
    ctxs = [lax.rem(ctx + k, n_ctx) for k in range(n_ctx)]
    steps = [(a, b) for a in range(n_sec) for b in range(n_ten) if (a, b) != (0, 0)]
    places = [
        {"section": lax.rem(sec + a, n_sec), "tensor": lax.rem(ten + b, n_ten)} for a, b in steps
    ]
    greet([{"ctx": c} for c in ctxs[1:]] + places)
    sent = []

    def across(k, slot):
        return remote(
            part_ref, held.at[slot], ctx_send.at[k - 1], ctx_recv.at[k - 1], ctx=ctxs[k]
        )

    def biases(k, slot):
        return remote(
            bias_ref,
            bias_all.at[slot],
            bias_send.at[k - 1],
            bias_recv.at[k - 1],
            section=lax.rem(sec + k, n_sec),
        )

    for k in range(1, n_ctx):
        start_all([across(k, ctx)], sent)
    for k in range(1, n_sec):
        start_all([biases(k, sec)], sent)
    held[ctx] = part_ref[...]
    bias_all[sec] = bias_ref[...]
    for k in range(1, n_ctx):
        across(k, lax.rem(ctx + n_ctx - k, n_ctx)).wait_recv()
    total = add_ref[...]
    for k in range(n_ctx):
        total = total + held[k]
    mod_ref[sec, ten] = total

    def column(at, block):
        return remote(block, block, col_send.at[at], col_recv.at[at], **places[at])

    for at in range(len(steps)):
        start_all([column(at, mod_ref.at[sec, ten])], sent)
    for at, (a, b) in enumerate(steps):
        theirs = mod_ref.at[lax.rem(sec + n_sec - a, n_sec), lax.rem(ten + n_ten - b, n_ten)]
        column(at, theirs).wait_recv()
    for k in range(1, n_sec):
        biases(k, lax.rem(sec + n_sec - k, n_sec)).wait_recv()
    for copy in sent:
        copy.wait_send()


def opening(part, add, bias):
    sizes = n_sec, n_ten, n_ctx = tuple(
        lax.axis_size(name) for name in ("section", "tensor", "ctx")
    )
    dma = pltpu.SemaphoreType.DMA
    return pl.pallas_call(
        functools.partial(opening_kernel, sizes),
        out_shape=[
            jax.ShapeDtypeStruct((n_sec, n_ten) + part.shape, part.dtype),
            jax.ShapeDtypeStruct((n_sec,) + bias.shape, bias.dtype),
        ],
        in_specs=[VMEM] * 3,
        out_specs=[VMEM] * 2,
        scratch_shapes=[
            pltpu.VMEM((n_ctx,) + part.shape, part.dtype),
            dma((max(n_ctx - 1, 1),)),
            dma((max(n_ctx - 1, 1),)),
            dma((n_sec * n_ten,)),
            dma((n_sec * n_ten,)),
            dma((max(n_sec - 1, 1),)),
            dma((max(n_sec - 1, 1),)),
        ],
        compiler_params=pltpu.CompilerParams(collective_id=1, has_side_effects=True),
        cost_estimate=link_cost(40 * n_sec * n_ten * part.size * part.dtype.itemsize),
        name="opening",
    )(part, add, bias)


def group_peers(n_sec, n_ctx):
    ni = inner_size(n_ctx)
    no = n_ctx // ni
    sec, ctx = lax.axis_index("section"), lax.axis_index("ctx")
    i, o = lax.rem(ctx, ni), lax.div(ctx, ni)
    far = {
        (a, b): {"section": lax.rem(sec + a, n_sec), "ctx": lax.rem(o + b, no) * ni + i}
        for a in range(n_sec)
        for b in range(no)
        if (a, b) != (0, 0)
    }
    near = {m: {"ctx": o * ni + lax.rem(i + m, ni)} for m in range(1, ni)}
    return sec, i, o, ni, no, far, near


def spread_kernel(n_sec, n_ctx, own_ref, both_ref, own_all, both_all, *sems):
    far_send, far_recv, near_send, near_recv, own_sem = sems
    sec, i, o, ni, no, far, near = group_peers(n_sec, n_ctx)
    greet(list(far.values()) + list(near.values()))
    sent = []
    me = o * ni + i

    def far_copies(step):
        a, b = step
        at = a * no + b
        copies = []
        if a == 0:
            copies.append(
                remote(
                    own_ref, own_all.at[me], far_send.at[0, at], far_recv.at[0, at], **far[step]
                )
            )
        copies.append(
            remote(
                both_ref, both_all.at[sec, me], far_send.at[1, at], far_recv.at[1, at], **far[step]
            )
        )
        return copies

    def near_copies(m, a, b, own_src, both_src, s_at, c_at):
        at = a * no + b
        copies = []
        if a == 0:
            copies.append(
                remote(
                    own_src,
                    own_all.at[c_at],
                    near_send.at[0, m - 1, at],
                    near_recv.at[0, m - 1, at],
                    **near[m],
                )
            )
        copies.append(
            remote(
                both_src,
                both_all.at[s_at, c_at],
                near_send.at[1, m - 1, at],
                near_recv.at[1, m - 1, at],
                **near[m],
            )
        )
        return copies

    for step in far:
        start_all(far_copies(step), sent)
    for m in near:
        start_all(near_copies(m, 0, 0, own_ref, both_ref, sec, me), sent)
    keep = [
        pltpu.make_async_copy(own_ref, own_all.at[me], own_sem.at[0]),
        pltpu.make_async_copy(both_ref, both_all.at[sec, me], own_sem.at[1]),
    ]
    for copy in keep:
        copy.start()
    for step in far:
        a, b = step
        for copy in far_copies(step):
            copy.wait_recv()
        s_at = lax.rem(sec + n_sec - a, n_sec)
        c_at = lax.rem(o + no - b, no) * ni + i
        for m in near:
            start_all(
                near_copies(m, a, b, own_all.at[c_at], both_all.at[s_at, c_at], s_at, c_at), sent
            )
    for m in near:
        for a in range(n_sec):
            for b in range(no):
                s_at = lax.rem(sec + n_sec - a, n_sec)
                c_at = lax.rem(o + no - b, no) * ni + lax.rem(i + ni - m, ni)
                for copy in near_copies(
                    m, a, b, own_all.at[c_at], both_all.at[s_at, c_at], s_at, c_at
                ):
                    copy.wait_recv()
    for copy in keep:
        copy.wait()
    for copy in sent:
        copy.wait_send()


def spread(own, both):
    n_sec, n_ctx = lax.axis_size("section"), lax.axis_size("ctx")
    ni = inner_size(n_ctx)
    no = n_ctx // ni
    dma = pltpu.SemaphoreType.DMA
    return pl.pallas_call(
        functools.partial(spread_kernel, n_sec, n_ctx),
        out_shape=[
            jax.ShapeDtypeStruct((n_ctx,) + own.shape, own.dtype),
            jax.ShapeDtypeStruct((n_sec, n_ctx) + both.shape, both.dtype),
        ],
        in_specs=[VMEM, VMEM],
        out_specs=[VMEM, VMEM],
        scratch_shapes=[
            dma((2, n_sec * no)),
            dma((2, n_sec * no)),
            dma((2, ni, n_sec * no)),
            dma((2, ni, n_sec * no)),
            dma((2,)),
        ],
        compiler_params=pltpu.CompilerParams(collective_id=2, has_side_effects=True),
        name="spread",
    )(own, both)


def owner_kernel(n_sec, n_ctx, own_ref, both_ref, own_out, both_out, *refs):
    own_pair, both_pair, own_far, both_far = refs[:4]
    far_send, far_recv, near_send, near_recv = refs[4:]
    sec, i, o, ni, no, far, near = group_peers(n_sec, n_ctx)
    greet(list(far.values()) + list(near.values()))
    sent = []

    def near_copies(m, a, b):
        to = lax.rem(i + m, ni)
        s_at, o_at = lax.rem(sec + a, n_sec), lax.rem(o + b, no)
        at = a * no + b
        copies = []
        if a == 0:
            copies.append(
                remote(
                    own_ref.at[o_at * ni + to],
                    own_pair.at[m - 1, b],
                    near_send.at[0, m - 1, at],
                    near_recv.at[0, m - 1, at],
                    **near[m],
                )
            )
        copies.append(
            remote(
                both_ref.at[s_at, o_at * ni + to],
                both_pair.at[m - 1, at],
                near_send.at[1, m - 1, at],
                near_recv.at[1, m - 1, at],
                **near[m],
            )
        )
        return copies

    order = list(far) + [(0, 0)]
    for step in order:
        for m in near:
            start_all(near_copies(m, *step), sent)

    def far_copies(a, b):
        at = a * no + b
        copies = []
        if a == 0:
            copies.append(
                remote(
                    own_pair.at[ni - 1, b],
                    own_far.at[b],
                    far_send.at[0, at],
                    far_recv.at[0, at],
                    **far[(a, b)],
                )
            )
        copies.append(
            remote(
                both_pair.at[ni - 1, at],
                both_far.at[at],
                far_send.at[1, at],
                far_recv.at[1, at],
                **far[(a, b)],
            )
        )
        return copies

    for a, b in order:
        s_at, c_at = lax.rem(sec + a, n_sec), lax.rem(o + b, no) * ni + i
        at = a * no + b
        for m in near:
            for copy in near_copies(m, a, b):
                copy.wait_recv()
        total_both = both_ref[s_at, c_at].astype(jnp.float32)
        for m in near:
            total_both = total_both + both_pair[m - 1, at].astype(jnp.float32)
        total_own = None
        if a == 0:
            total_own = own_ref[c_at].astype(jnp.float32)
            for m in near:
                total_own = total_own + own_pair[m - 1, b].astype(jnp.float32)
        if (a, b) == (0, 0):
            own_out[...] = total_own
            both_out[...] = total_both
        else:
            if a == 0:
                own_pair[ni - 1, b] = total_own.astype(own_pair.dtype)
            both_pair[ni - 1, at] = total_both.astype(both_pair.dtype)
            start_all(far_copies(a, b), sent)
    for a, b in far:
        for copy in far_copies(a, b):
            copy.wait_recv()
        if a == 0:
            own_out[...] += own_far[b].astype(jnp.float32)
        both_out[...] += both_far[a * no + b].astype(jnp.float32)
    for copy in sent:
        copy.wait_send()


def owner_sum(own, both):
    n_sec, n_ctx = lax.axis_size("section"), lax.axis_size("ctx")
    ni = inner_size(n_ctx)
    no = n_ctx // ni
    dma = pltpu.SemaphoreType.DMA
    own_shape, both_shape = own.shape[1:], both.shape[2:]
    return pl.pallas_call(
        functools.partial(owner_kernel, n_sec, n_ctx),
        out_shape=[
            jax.ShapeDtypeStruct(own_shape, jnp.float32),
            jax.ShapeDtypeStruct(both_shape, jnp.float32),
        ],
        in_specs=[VMEM, VMEM],
        out_specs=[VMEM, VMEM],
        scratch_shapes=[
            pltpu.VMEM((ni, no) + own_shape, own.dtype),
            pltpu.VMEM((ni, n_sec * no) + both_shape, both.dtype),
            pltpu.VMEM((no,) + own_shape, own.dtype),
            pltpu.VMEM((n_sec * no,) + both_shape, both.dtype),
            dma((2, n_sec * no)),
            dma((2, n_sec * no)),
            dma((2, ni, n_sec * no)),
            dma((2, ni, n_sec * no)),
        ],
        compiler_params=pltpu.CompilerParams(collective_id=3, has_side_effects=True),
        name="owner_sum",
    )(own, both)


def small_kernel(axes, sizes, x_ref, out_ref, held, send, recv):
    at = [lax.axis_index(name) for name in axes]
    steps = [(a, b) for a in range(sizes[0]) for b in range(sizes[1])]
    places = [
        [lax.rem(here + sign * step + size, size) for here, step, size in zip(at, pair, sizes)]
        for sign in (1, -1)
        for pair in steps
    ]
    to, source = places[: len(steps)], places[len(steps) :]
    where = [dict(zip(axes, place)) for place in to]
    greet(where[1:])

    def block(place):
        return place[0] if x_ref.shape[0] > 1 else 0

    def copy(k, slot):
        return remote(
            x_ref.at[block(to[k])],
            held.at[slot[0] * sizes[1] + slot[1]],
            send.at[k - 1],
            recv.at[k - 1],
            **where[k],
        )

    copies = [copy(k, at) for k in range(1, len(steps))]
    for started in copies:
        started.start()
    held[at[0] * sizes[1] + at[1]] = x_ref[block(at)]
    for k in range(1, len(steps)):
        copy(k, source[k]).wait_recv()
    total = held[0]
    for k in range(1, len(steps)):
        total = total + held[k]
    out_ref[...] = total
    for started in copies:
        started.wait_send()


def small_sum(x, axes, collective_id):
    sizes = tuple(lax.axis_size(name) for name in axes)
    n = sizes[0] * sizes[1]
    dma = pltpu.SemaphoreType.DMA((max(n - 1, 1),))
    return pl.pallas_call(
        functools.partial(small_kernel, axes, sizes),
        out_shape=jax.ShapeDtypeStruct(x.shape[1:], x.dtype),
        in_specs=[VMEM],
        out_specs=VMEM,
        scratch_shapes=[pltpu.VMEM((n,) + x.shape[1:], x.dtype), dma, dma],
        compiler_params=pltpu.CompilerParams(collective_id=collective_id, has_side_effects=True),
        cost_estimate=link_cost(100 * n * x[0].size * x.dtype.itemsize),
        name="small_sum",
    )(x)


def packed(pieces, width):
    flat = jnp.concatenate([p.reshape(-1) for p in pieces])
    rows = -(-flat.shape[0] // width)
    rows = -(-rows // 8) * 8
    return jnp.pad(flat, (0, rows * width - flat.shape[0])).reshape(rows, width)


def compact(array):
    return packed([array], -(-array.size // 8))


def unpacked(block, shapes):
    flat, at, out = block.reshape(-1), 0, []
    for shape in shapes:
        size = math.prod(shape)
        out.append(flat[at : at + size].reshape(shape))
        at += size
    return out


def layer_norm(values):
    centre = jnp.mean(values, axis=-1, keepdims=True)
    centred = values - centre
    variance = jnp.mean(centred * centred, axis=-1, keepdims=True)
    inverse = lax.rsqrt(variance + EPSILON)
    return centred * inverse


def norm_back_kernel(scale_at, gate_at, up_ref, x_ref, base_ref, mod_ref, *refs):
    x = x_ref[...].astype(jnp.float32)
    centred = x - jnp.mean(x, axis=-1, keepdims=True)
    inverse = lax.rsqrt(jnp.mean(centred * centred, axis=-1, keepdims=True) + EPSILON)
    normed = centred * inverse
    upstream = up_ref[...].astype(jnp.float32)
    scaled = upstream * (1.0 + mod_ref[0, scale_at : scale_at + 1, :])
    mean_grad = jnp.mean(scaled, axis=-1, keepdims=True)
    mean_cross = jnp.mean(scaled * normed, axis=-1, keepdims=True)
    grad = base_ref[...] + inverse * (scaled - mean_grad - normed * mean_cross)
    if gate_at is None:
        grad_ref, sums_ref = refs
    else:
        term_ref, bias_ref, gate_ref, grad_ref, gated_ref, sums_ref = refs
        gated = grad * gate_ref[0, gate_at : gate_at + 1, :]
        gated_ref[...] = gated.astype(gated_ref.dtype)
        term = term_ref[...].astype(jnp.float32) + bias_ref[...]
        sums_ref[0, 2:3, :] = jnp.sum(grad * term, axis=0, keepdims=True)
        sums_ref[0, 3:4, :] = jnp.sum(gated, axis=0, keepdims=True)
    grad_ref[...] = grad
    sums_ref[0, 0:1, :] = jnp.sum(upstream, axis=0, keepdims=True)
    sums_ref[0, 1:2, :] = jnp.sum(upstream * normed, axis=0, keepdims=True)


def norm_back(rows, upstream, x, base, mods, scale_at, gate=None):
    part, width = rows.part, rows.width
    runs = rows.rows // part
    tile = pl.BlockSpec((part, width), lambda at: (at, 0))
    per_run = pl.BlockSpec((1, mods.shape[1], width), lambda at: (at, 0, 0))
    sums = pl.BlockSpec((1, 8, width), lambda at: (at, 0, 0))
    args, in_specs = [upstream, x, base, mods], [tile] * 3 + [per_run]
    shape = jax.ShapeDtypeStruct((rows.rows, width), jnp.float32)
    out_shape, out_specs = [shape], [tile]
    if gate:
        term, bias, gate_mods, gate_at = gate
        args += [term, bias[None], gate_mods]
        in_specs += [tile, pl.BlockSpec((1, width), lambda at: (0, 0)), per_run]
        out_shape.append(jax.ShapeDtypeStruct((rows.rows, width), jnp.bfloat16))
        out_specs.append(tile)
    return pl.pallas_call(
        functools.partial(norm_back_kernel, scale_at, gate_at if gate else None),
        grid=(runs,),
        out_shape=out_shape + [jax.ShapeDtypeStruct((runs, 8, width), jnp.float32)],
        in_specs=in_specs,
        out_specs=out_specs + [sums],
        compiler_params=pltpu.CompilerParams(vmem_limit_bytes=32 * 1024 * 1024),
        cost_estimate=pl.CostEstimate(
            flops=30 * rows.rows * width,
            bytes_accessed=18 * rows.rows * width,
            transcendentals=rows.rows,
        ),
        name="norm_back",
    )(*args)


def gelu_back(pre_act, upstream):
    unused_out, pullback = jax.vjp(
        lambda pre_value: jax.nn.gelu(pre_value, approximate=True), pre_act
    )
    return pullback(upstream)[0]


def heads(array):
    cols = array.shape[-2]
    return array.reshape(*array.shape[:-2], cols // HD, HD, array.shape[-1])


def score_columns(queries, keys):
    softmax_scale = 1.0 / math.sqrt(HD)
    return (
        jnp.einsum(
            "nhdk,hdq->hnkq", heads(keys), heads(queries), preferred_element_type=jnp.float32
        )
        * softmax_scale
    )


def attend(queries, keys, values):
    scores = score_columns(queries, keys)
    row_peak = jnp.max(scores, axis=(1, 2), keepdims=True)
    log_total = row_peak + jnp.log(jnp.sum(jnp.exp(scores - row_peak), axis=(1, 2), keepdims=True))
    prob_bf = jnp.exp(scores - log_total).astype(jnp.bfloat16)
    context = jnp.einsum(
        "nhdk,hnkq->hdq", heads(values), prob_bf, preferred_element_type=jnp.float32
    )
    return context.astype(jnp.bfloat16).reshape(queries.shape), log_total


def attention_grads(queries, keys, values, log_total, context, context_grad):
    softmax_scale = 1.0 / math.sqrt(HD)
    query_heads, grad_heads = heads(queries), heads(context_grad)
    delta = jnp.sum(
        grad_heads.astype(jnp.float32) * heads(context).astype(jnp.float32), axis=1
    )[:, None, None, :]
    prob_full = jnp.exp(score_columns(queries, keys) - log_total)
    prob_bf = prob_full.astype(jnp.bfloat16)
    prob_grad = jnp.einsum(
        "nhdk,hdq->hnkq", heads(values), grad_heads, preferred_element_type=jnp.float32
    )
    score_grad = (prob_full * (prob_grad - delta)).astype(jnp.bfloat16)
    query_grad = (
        jnp.einsum(
            "nhdk,hnkq->hdq", heads(keys), score_grad, preferred_element_type=jnp.float32
        )
        * softmax_scale
    ).reshape(queries.shape)
    key_part = (
        jnp.einsum("hnkq,hdq->nhdk", score_grad, query_heads, preferred_element_type=jnp.float32)
        * softmax_scale
    ).reshape(keys.shape)
    value_part = jnp.einsum(
        "hnkq,hdq->nhdk", prob_bf, grad_heads, preferred_element_type=jnp.float32
    ).reshape(values.shape)
    both = jnp.concatenate(
        [key_part.astype(jnp.bfloat16), value_part.astype(jnp.bfloat16)], axis=1
    )
    return query_grad, both


def contract(left, right, left_dim, right_dim):
    return lax.dot_general(
        left, right, (((left_dim,), (right_dim,)), ((), ())), preferred_element_type=jnp.float32
    )


class Rows:
    def __init__(self, latents, section):
        n_sec = lax.axis_size("section")
        self.n_sec = n_sec
        total, self.tokens, self.width = latents.shape
        self.section = section
        self.full = total // n_sec
        self.rest = total - self.full * n_sec
        self.part = self.tokens // n_sec
        self.own_rows = self.full * self.tokens
        self.both_rows = self.rest * self.part
        self.rows = self.own_rows + self.both_rows

    def take(self, array):
        own = lax.dynamic_slice_in_dim(array, self.section * self.full, self.full, 0)
        both = lax.dynamic_slice_in_dim(
            array[self.full * self.n_sec :], self.section * self.part, self.part, 1
        )
        return jnp.concatenate(
            [own.reshape(self.own_rows, -1), both.reshape(self.both_rows, -1)], axis=0
        )

    def split(self, array):
        return (
            array[: self.own_rows].reshape(self.full, self.tokens, -1),
            array[self.own_rows :].reshape(self.rest, self.part, -1),
        )

    def spans(self):
        out = [(at * self.tokens, self.tokens) for at in range(self.full)]
        return out + [
            (self.own_rows + at * self.part, self.part) for at in range(self.rest)
        ]

    def columns(self, array):
        return [array[:, start : start + size] for start, size in self.spans()]

    def mods(self, modulation):
        own = lax.dynamic_slice_in_dim(modulation, self.section * self.full, self.full, 0)
        return jnp.concatenate([own, modulation[self.full * self.n_sec :]], axis=0)

    def by_run(self, mods):
        runs = self.tokens // self.part
        return jnp.concatenate(
            [mods[at : at + 1] for at in range(self.full) for _ in range(runs)] + [mods[self.full :]]
        )

    def wide(self, pieces):
        row = lax.broadcasted_iota(jnp.int32, (self.rows, 1), 0)
        out = pieces[-1][None, :]
        for (start, size), piece in reversed(list(zip(self.spans(), pieces))[:-1]):
            out = jnp.where(row < start + size, piece[None, :], out)
        return out

    def sums(self, array):
        return jnp.sum(array.reshape(-1, self.part, self.width), axis=1)

    def placed(self, sums):
        runs = self.tokens // self.part
        own = sums[: self.full * runs].reshape(self.full, runs, -1).sum(axis=1)
        mine = [
            jnp.where(self.section == at // self.full, own[at % self.full], 0.0)
            for at in range(self.full * self.n_sec)
        ]
        both = [sums[self.full * runs + at] for at in range(self.rest)]
        return jnp.stack(mine + both)

    def assembled(self, per_block, received):
        own = per_block[-1]
        for b in range(self.n_sec - 1):
            own = jnp.where(self.section == b, per_block[b], own)
        others = []
        for k in range(1, self.n_sec):
            rows = received[-1][k - 1]
            for b in range(self.n_sec - 1):
                rows = jnp.where(self.section == b, received[b][k - 1], rows)
            others.append(rows)
        whole, shared = [], []
        for source in range(self.n_sec):
            rows = own
            for k, other in enumerate(others, 1):
                rows = jnp.where(lax.rem(self.section + k, self.n_sec) == source, other, rows)
            first, both = self.split(rows)
            whole.append(first)
            shared.append(both)
        return jnp.concatenate(whole + [jnp.concatenate(shared, axis=1)], axis=0)


def gathered(key_value, rows):
    spans = rows.spans()
    cols = [key_value[:, start : start + size] for start, size in spans]
    own = jnp.concatenate(cols[: rows.full], axis=0)
    both = jnp.concatenate(cols[rows.full :], axis=0)
    own_all, both_all = spread(own, both)
    both_all = both_all.reshape(-1, *both.shape)
    high = key_value.shape[0]
    return [own_all[:, at * high : (at + 1) * high] for at in range(rows.full)] + [
        both_all[:, at * high : (at + 1) * high] for at in range(rows.rest)
    ]


def returned(parts, rows):
    high = parts[0].shape[1]
    own = jnp.concatenate(parts[: rows.full], axis=1)
    both = jnp.concatenate(parts[rows.full :], axis=1)
    own, both = owner_sum(own, both.reshape(rows.n_sec, -1, *both.shape[1:]))
    return jnp.concatenate(
        [own[at * high : (at + 1) * high] for at in range(rows.full)]
        + [both[at * high : (at + 1) * high] for at in range(rows.rest)],
        axis=1,
    )


def forward_block(rows, block_in, mods, w_qkv, biases, prepare, mlp_weights, last):
    b_qv, b_out, b_fc1, b_fc2 = biases
    local_cols = w_qkv.shape[0] // 3
    shift_a, scale_a, gate_a, shift_m, scale_m, gate_m = (
        rows.wide([mods[at, k] for at in range(mods.shape[0])]) for k in range(6)
    )
    residual = block_in.astype(jnp.float32)
    normed_a = layer_norm(residual)
    attn_in = (normed_a * (1.0 + scale_a) + shift_a).astype(jnp.bfloat16)
    projected = contract(w_qkv, attn_in, 1, 1)
    bias = jnp.concatenate([b_qv[0], jnp.zeros_like(b_qv[0]), b_qv[1]])
    projected = (projected + bias[:, None]).astype(jnp.bfloat16)
    queries = rows.columns(projected[:local_cols])
    keys_values, w_out, sends = prepare(gathered(projected[local_cols:], rows))
    attended = [
        attend(q, kv[:, :local_cols], kv[:, local_cols:])
        for q, kv in zip(queries, keys_values)
    ]
    context = row_major(jnp.concatenate([row_major(c) for c, _ in attended], axis=1))
    attn_term = contract(context, w_out, 0, 0)
    (attn_sum,), moved = beside(tensor_sum, [attn_term.astype(jnp.bfloat16)], sends)
    w_fc1, w_fc2 = mlp_weights(moved)
    attn_out = attn_sum.astype(jnp.float32) + b_out
    middle = residual + gate_a * attn_out
    normed_m = layer_norm(middle)
    mlp_in = (normed_m * (1.0 + scale_m) + shift_m).astype(jnp.bfloat16)
    pre_act = jnp.dot(mlp_in, w_fc1, preferred_element_type=jnp.float32) + b_fc1
    hidden = jax.nn.gelu(pre_act, approximate=True).astype(jnp.bfloat16)
    mlp_term = jnp.dot(hidden, w_fc2, preferred_element_type=jnp.float32).astype(jnp.bfloat16)

    def close(mlp_sum):
        mlp_out = mlp_sum.astype(jnp.float32) + b_fc2
        return mlp_out, (middle + gate_m * mlp_out).astype(jnp.bfloat16)

    block_res, mlp_sum = None, None
    if not last:
        (mlp_sum,) = tensor_sum(mlp_term)
        block_res = close(mlp_sum)[1]
    stored = (
        block_in,
        attn_in,
        queries,
        keys_values,
        [log_total for _, log_total in attended],
        context,
        attn_sum,
        middle,
        mlp_in,
        pre_act,
        hidden,
        mlp_sum,
    )
    return block_res, stored, moved, (mlp_term, close) if last else None


def backward_block(
    rows, upstream, gated, stored, run_mods, weights, block, firsts, seconds, pending, b_out, below
):
    w_qkv, w_out, w_fc1, w_fc2 = weights
    (
        block_in,
        attn_in,
        queries,
        keys_values,
        log_totals,
        context,
        attn_sum,
        middle,
        mlp_in,
        pre_act,
        hidden,
        mlp_sum,
    ) = stored
    mlp_grad_b, gate_m_grad, grad_b2 = gated
    local_cols = w_qkv.shape[0] // 3
    pre_grad = gelu_back(pre_act, jnp.dot(mlp_grad_b, w_fc2.T, preferred_element_type=jnp.float32))
    pre_grad_b = pre_grad.astype(jnp.bfloat16)
    grad_b1 = jnp.sum(pre_grad, axis=0)
    mlp_pair = inner_pair(
        [contract(mlp_grad_b, hidden, 0, 0), contract(mlp_in, pre_grad_b, 0, 0)]
    )
    mlp_term = jnp.dot(pre_grad_b, w_fc1.T, preferred_element_type=jnp.float32)
    terms = [mlp_term.astype(jnp.bfloat16)]
    if pending:
        terms.append(pending[0])
    outer = outer_sends(mlp_pair)
    (mlp_in_grad, *sums), moved = beside(tensor_sum, terms, outer + firsts)
    block_res = None
    if pending:
        mlp_out, block_res = pending[1](sums[0])
        gate_m_grad = rows.sums(upstream * mlp_out)
    first_moved = moved[len(outer) :]
    mlp_share = outer_total(mlp_pair, moved[: len(outer)])
    middle_grad, attn_grad_b, m_sums = norm_back(
        rows, mlp_in_grad, middle, upstream, run_mods, 4, (attn_sum, b_out, run_mods, 2)
    )
    grad_bo = jnp.sum(m_sums[:, 3], axis=0)
    context_grad = contract(w_out, attn_grad_b, 1, 1).astype(jnp.bfloat16)
    query_grads, key_value_parts = zip(
        *(
            attention_grads(q, kv[:, :local_cols], kv[:, local_cols:], log_total, c, cg)
            for q, kv, log_total, c, cg in zip(
                queries, keys_values, log_totals, rows.columns(context), rows.columns(context_grad)
            )
        )
    )
    query_grad = row_major(jnp.concatenate([row_major(g) for g in query_grads], axis=1))
    key_value_grad = returned(key_value_parts, rows)
    grad_bqv = jnp.stack(
        [jnp.sum(query_grad, axis=1), jnp.sum(key_value_grad[local_cols:], axis=1)]
    )
    qkv_grad_b = jnp.concatenate([query_grad, key_value_grad], axis=0).astype(jnp.bfloat16)
    qkv_rows, context_rows = row_major(row_major(qkv_grad_b).T), row_major(row_major(context).T)
    attn_term = contract(qkv_rows, w_qkv, 1, 0)
    attn_pairs = [
        inner_pair([contract(attn_in, qkv_rows, 0, 0)]),
        inner_pair([contract(attn_grad_b, context_rows, 0, 0)]),
    ]
    outers = [outer_sends(pair) for pair in attn_pairs]
    across = block_sends(mlp_share, block)
    sends = [*outers, across, seconds]
    ((attn_in_grad,), moved) = beside(
        tensor_sum, [attn_term.astype(jnp.bfloat16)], [send for part in sends for send in part]
    )
    came = []
    for part in sends:
        came.append(moved[: len(part)])
        moved = moved[len(part) :]
    attn_shares = [outer_total(pair, part) for pair, part in zip(attn_pairs, came)]
    mlp_share = block_total(mlp_share, came[-2])
    second_moved = came[-1]
    input_grad, *gated, a_sums = norm_back(
        rows, attn_in_grad, block_in, middle_grad, run_mods, 1, below
    )
    if below:
        gated += [a_sums[:, 2], jnp.sum(a_sums[:, 3], axis=0)]
    mod_grad = jnp.concatenate(
        [a_sums[:, 0], a_sums[:, 1], m_sums[:, 2], m_sums[:, 0], m_sums[:, 1], gate_m_grad], axis=1
    )
    return (
        input_grad,
        gated,
        mod_grad,
        (grad_bqv, grad_bo, grad_b1, grad_b2),
        (mlp_share, *attn_shares),
        block_res,
        first_moved,
        second_moved,
    )


def to_inner(value, by):
    n = lax.axis_size("ctx")
    ni = inner_size(n)
    return lax.ppermute(value, "ctx", [(a, a // ni * ni + (a + by) % ni) for a in range(n)])


def to_outer(value, by):
    n = lax.axis_size("ctx")
    ni = inner_size(n)
    return lax.ppermute(value, "ctx", [(a, (a + by * ni) % n) for a in range(n)])


def to_section(value, by):
    n = lax.axis_size("section")
    return lax.ppermute(value, "section", [(a, (a + by) % n) for a in range(n)])


def to_block(value, block, by):
    n = lax.axis_size("section")
    return lax.ppermute(value, "section", [((block + by) % n, block)])


def ctx_place():
    n = lax.axis_size("ctx")
    ni = inner_size(n)
    at = lax.axis_index("ctx")
    return n // ni, ni, lax.div(at, ni), lax.rem(at, ni)


def beside(kernel, args, sends):
    args, values = lax.optimization_barrier((args, [value for value, _ in sends]))
    moved = [move(value) for value, (_, move) in zip(values, sends)]
    return lax.optimization_barrier((kernel(*args), moved))


def half_of(weights):
    _, ni, _, i = ctx_place()
    sizes = [w.shape[0] // ni for w in weights]
    return jnp.concatenate(
        [lax.dynamic_slice_in_dim(w, i * size, size, 0) for w, size in zip(weights, sizes)]
    )


def joined(own, passed, weights):
    _, ni, _, i = ctx_place()
    found, start = [], 0
    for w in weights:
        size = w.shape[0] // ni
        parts = [piece[start : start + size] for piece in [own] + passed]
        start += size
        ordered = []
        for at in range(ni):
            piece = parts[0]
            for m in range(1, ni):
                piece = jnp.where(lax.rem(i + ni - m, ni) == at, parts[m], piece)
            ordered.append(piece)
        found.append(jnp.concatenate(ordered))
    return found


def chosen_blocks(weights, others):
    n_sec = lax.axis_size("section")
    section = lax.axis_index("section")
    blocks = []
    for b in range(n_sec):
        chosen = list(weights)
        for k, found in enumerate(others, 1):
            is_source = lax.rem(section + n_sec - k, n_sec) == b
            chosen = [jnp.where(is_source, new, old) for new, old in zip(found, chosen)]
        blocks.append(chosen)
    return blocks


def fetched(weights):
    n_sec = lax.axis_size("section")
    groups = [
        [at for at, w in enumerate(weights) if w.shape[1] == width]
        for width in sorted({w.shape[1] for w in weights})
    ]
    halves = [half_of([weights[at] for at in group]) for group in groups]
    return groups, [[to_section(half, k) for k in range(1, n_sec)] for half in halves]


def passing(fetch):
    _, ni, _, _ = ctx_place()
    return [
        (half, functools.partial(to_inner, by=m))
        for of_group in fetch[1]
        for half in of_group
        for m in range(1, ni)
    ]


def every_block(weights, fetch, passed):
    _, ni, _, _ = ctx_place()
    n_sec = lax.axis_size("section")
    others = [[None] * len(weights) for _ in range(n_sec - 1)]
    passed = list(passed)
    for group, of_group in zip(*fetch):
        for k, half in enumerate(of_group):
            rest = [passed.pop(0) for _ in range(1, ni)]
            for at, whole in zip(group, joined(half, rest, [weights[at] for at in group])):
                others[k][at] = whole
    return chosen_blocks(weights, others)


def inner_pair(terms):
    no, ni, _, i = ctx_place()
    terms = [
        row_major(t.astype(jnp.bfloat16)).reshape(no, ni, -1, t.shape[-1]) for t in terms
    ]

    def inner(at):
        return row_major(
            jnp.concatenate(
                [lax.dynamic_index_in_dim(t, at, 1, keepdims=False) for t in terms], axis=1
            )
        )

    pair = inner(i).astype(jnp.float32)
    for m in range(1, ni):
        pair = pair + to_inner(inner(lax.rem(i + m, ni)), m).astype(jnp.float32)
    return pair.astype(jnp.bfloat16)


def outer_sends(pair):
    no, _, o, _ = ctx_place()
    return [
        (
            lax.dynamic_index_in_dim(pair, lax.rem(o + m, no), 0, keepdims=False),
            functools.partial(to_outer, by=m),
        )
        for m in range(1, no)
    ]


def outer_total(pair, moved):
    _, _, o, _ = ctx_place()
    total = lax.dynamic_index_in_dim(pair, o, 0, keepdims=False).astype(jnp.float32)
    for piece in moved:
        total = total + piece.astype(jnp.float32)
    return total


def block_sends(value, block):
    value = value.astype(jnp.bfloat16)
    return [
        (value, functools.partial(to_block, block=block, by=k))
        for k in range(1, lax.axis_size("section"))
    ]


def block_total(own, moved):
    for piece in moved:
        own = own + piece.astype(jnp.float32)
    return own


def local(
    latents,
    condition,
    cotangent,
    w_ada,
    b_ada,
    w_qkv,
    b_qv,
    w_out,
    b_out,
    w_fc1,
    b_fc1,
    w_fc2,
    b_fc2,
):
    section = lax.axis_index("section")
    n_sec = lax.axis_size("section")
    latent_total, token_count, width = latents.shape
    width_cols = b_ada.shape[-1]
    local_cols = w_qkv.shape[-1]
    rows = Rows(latents, section)
    cond_act = jax.nn.silu(condition).astype(jnp.bfloat16)
    mod_part = jnp.dot(cond_act, w_ada[0], preferred_element_type=jnp.float32)
    bias_shapes = [b_qv.shape[1:], b_out.shape[1:], b_fc1.shape[1:], b_fc2.shape[1:]]
    bias_flat = jnp.concatenate([b.reshape(-1) for b in (b_qv, b_out, b_fc1, b_fc2)])
    qkv_weights = [row_major(jnp.transpose(w_qkv[0], (1, 2, 0)).reshape(3 * local_cols, width))]
    qkv_fetch = fetched(qkv_weights)
    mod_all, bias_all = opening(
        compact(mod_part),
        compact(jnp.broadcast_to(b_ada, (latent_total, width_cols))),
        compact(bias_flat),
    )
    mod_all, fc1_weights = lax.optimization_barrier((mod_all, [w_fc1[0]]))
    fc1_fetch = fetched(fc1_weights)
    qkv_blocks = every_block(
        qkv_weights, qkv_fetch, [move(half) for half, move in passing(qkv_fetch)]
    )
    tensor = lax.axis_index("tensor")
    columns = mod_all.reshape(n_sec, -1, mod_all.shape[-2] * mod_all.shape[-1])
    columns = columns[..., : latent_total * width_cols]
    columns = columns.reshape(n_sec, -1, latent_total, width_cols)
    modulation = jnp.swapaxes(columns, 1, 2).reshape(n_sec, latent_total, 6, width)
    biases, mods = [], []
    for b in range(n_sec):
        biases.append(unpacked(bias_all[b], bias_shapes))
        mods.append(rows.mods(modulation[b]))
    residual = rows.take(latents)
    outs, out_moved, kept, out_blocks, mlp_blocks, pending = [], [], [], [], [], None
    for b in range(n_sec):
        if b == 0:
            late = []

            def prepare(keys_values):
                keys_values, weights = lax.optimization_barrier(
                    (keys_values, [w_out[0], w_fc2[0]])
                )
                for weight in weights:
                    late.append(([weight], fetched([weight])))
                weights, fetch = late[0]
                out_blocks.extend(
                    every_block(weights, fetch, [move(half) for half, move in passing(fetch)])
                )
                return keys_values, out_blocks[0][0], passing(fc1_fetch)

            def finish(moved):
                firsts = every_block(fc1_weights, fc1_fetch, moved)
                weights, fetch = late[1]
                seconds = every_block(
                    weights, fetch, [move(half) for half, move in passing(fetch)]
                )
                mlp_blocks.extend([*one, *two] for one, two in zip(firsts, seconds))
                return mlp_blocks[0]

        else:
            sends = block_sends(outs[-1], b - 1)

            def prepare(keys_values, sends=sends, b=b):
                return keys_values, out_blocks[b][0], sends

            def finish(moved, b=b):
                return mlp_blocks[b]

        residual, stored, moved, pending = forward_block(
            rows,
            residual,
            mods[b],
            qkv_blocks[b][0],
            biases[b],
            prepare,
            finish,
            b == n_sec - 1,
        )
        if b:
            out_moved.append(moved)
        outs.append(residual)
        kept.append(stored)
    upstream = rows.take(cotangent).astype(jnp.float32)
    run_mods = [rows.by_run(block_mods) for block_mods in mods]
    top_grad = upstream * rows.wide([mods[-1][at, 5] for at in range(mods[-1].shape[0])])
    gated = (top_grad.astype(jnp.bfloat16), None, jnp.sum(top_grad, axis=0))
    in_grads, in_moved, small, shares = ([None] * n_sec for _ in range(4))
    out_moved.append([])
    firsts, seconds = [[], []], []
    for b in reversed(range(n_sec)):
        below = (kept[b - 1][-1], biases[b - 1][3], run_mods[b - 1], 5) if b else None
        upstream, gated, mod_grad, bias_grads, shares[b], block_res, first_moved, second_moved = (
            backward_block(
                rows,
                upstream,
                gated,
                kept[b],
                run_mods[b],
                (*qkv_blocks[b], *out_blocks[b], *mlp_blocks[b]),
                b,
                [send for part in firsts for send in part],
                seconds,
                pending if b == n_sec - 1 else None,
                biases[b][1],
                below,
            )
        )
        if b == n_sec - 1:
            outs[b] = block_res
        else:
            at = 0
            for which in (1, 2):
                part = first_moved[at : at + n_sec - 1]
                at += n_sec - 1
                shares[b + 1][which] = block_total(shares[b + 1][which], part)
            if b == n_sec - 2:
                out_moved[-1] = first_moved[at:]
            in_moved[b + 1] = second_moved
        shares[b] = list(shares[b])
        in_grads[b] = upstream.astype(jnp.bfloat16)
        cols = mod_grad[:, :width_cols]
        for t in range(1, lax.axis_size("tensor")):
            cols = jnp.where(tensor == t, mod_grad[:, t * width_cols : (t + 1) * width_cols], cols)
        small[b] = packed([rows.placed(cols), *bias_grads], width)
        firsts = [block_sends(share, b) for share in shares[b][1:]]
        if b == n_sec - 1:
            firsts.append(block_sends(outs[b], b))
        seconds = block_sends(in_grads[b], b)
    summed, in_moved[0] = beside(
        functools.partial(small_sum, axes=("section", "ctx"), collective_id=4),
        [jnp.stack(small)],
        seconds,
    )
    in_grad = rows.assembled(in_grads, in_moved).astype(jnp.float32)
    block_out = rows.assembled(outs, out_moved)
    mod_total, grad_bqv, grad_bo, grad_b1, grad_b2 = unpacked(
        summed, [(latent_total, width_cols)] + bias_shapes
    )
    mod_rounded = mod_total.astype(jnp.bfloat16)
    cond_part = jnp.dot(mod_rounded, w_ada[0].T, preferred_element_type=jnp.float32)
    cond_part = jnp.pad(cond_part, ((0, -latent_total % 8), (0, 0)))
    cond_sum, moved = beside(
        functools.partial(small_sum, axes=("section", "tensor"), collective_id=5),
        [cond_part[None]],
        firsts[0] + firsts[1],
    )
    cond_sum = cond_sum[:latent_total]
    for which in (1, 2):
        shares[0][which] = block_total(shares[0][which], moved[: n_sec - 1])
        moved = moved[n_sec - 1 :]

    def mine(which):
        out = shares[-1][which]
        for b in range(n_sec - 1):
            out = jnp.where(section == b, shares[b][which], out)
        return out

    mlp_share, qkv_share, out_share = mine(0), mine(1), mine(2)
    share_rows = mlp_share.shape[0] // 2
    grad_w_ada = jnp.dot(cond_act.T, mod_rounded, preferred_element_type=jnp.float32)[None]
    grad_b_ada = jnp.sum(mod_total, axis=0)[None]
    sigmoid_c = jax.nn.sigmoid(condition)
    cond_grad = cond_sum * sigmoid_c * (1.0 + condition * (1.0 - sigmoid_c))
    return (
        block_out[None],
        in_grad[None],
        cond_grad,
        grad_w_ada,
        grad_b_ada,
        qkv_share.reshape(1, share_rows, 3, local_cols),
        grad_bqv[None],
        out_share.T[None],
        grad_bo[None],
        mlp_share[share_rows:][None],
        grad_b1[None],
        mlp_share[:share_rows].T[None],
        grad_b2[None],
    )


def solution(mesh):
    return jax.shard_map(
        local,
        mesh=mesh,
        in_specs=(
            P(None, "ctx", None),
            P(None, "ctx"),
            P(None, "ctx", None),
            P("section", "ctx", "tensor"),
            P("section", "tensor"),
            P("section", None, None, "tensor"),
            P("section", None, "tensor"),
            P("section", "tensor", None),
            P("section", None),
            P("section", None, "tensor"),
            P("section", "tensor"),
            P("section", "tensor", None),
            P("section", None),
        ),
        out_specs=(
            P("section", None, "ctx", None),
            P("section", None, "ctx", None),
            P(None, "ctx"),
            P("section", "ctx", "tensor"),
            P("section", "tensor"),
            P("section", "ctx", None, "tensor"),
            P("section", None, "tensor"),
            P("section", "tensor", "ctx"),
            P("section", None),
            P("section", "ctx", "tensor"),
            P("section", "tensor"),
            P("section", "tensor", "ctx"),
            P("section", None),
        ),
        check_vma=False,
    )
```

```python
import functools
import math

import jax
import jax.numpy as jnp
from jax import lax
from jax.experimental import pallas as pl
from jax.experimental.layout import Layout, with_layout_constraint
from jax.experimental.pallas import tpu as pltpu
from jax.sharding import PartitionSpec as P

HD = 72
EPSILON = 1e-06
MESH = pl.DeviceIdType.MESH
ROW_TILE = 16
VMEM = pl.BlockSpec(memory_space=pltpu.VMEM)


def inner_size(n):
    return 2 if n % 2 == 0 else 1


def remote(src, dst, send, recv, **to):
    return pltpu.make_async_remote_copy(
        src_ref=src,
        dst_ref=dst,
        send_sem=send,
        recv_sem=recv,
        device_id=to,
        device_id_type=MESH,
    )


def greet(peers):
    barrier = pltpu.get_barrier_semaphore()
    for peer in peers:
        pl.semaphore_signal(barrier, inc=1, device_id=peer, device_id_type=MESH)
    pl.semaphore_wait(barrier, len(peers))


def row_major(array):
    return with_layout_constraint(array, Layout(tuple(range(array.ndim))))


def link_cost(moved):
    return pl.CostEstimate(flops=0, bytes_accessed=moved, transcendentals=0)


def start_all(copies, sent):
    for copy in copies:
        copy.start()
        sent.append(copy)


def middle_role(d, n, pieces, rows, lag, x_refs, out_refs, acc, from_outer, from_middle, sems):
    up_send, up_recv, mid_send, mid_recv, down_send, down_recv = sems
    half = n // 2
    left = d < half
    outer, inner = (d - 1, d + 1) if left else (d + 1, d - 1)
    has_outer = 0 <= outer < n
    is_middle = d in (half - 1, half)
    to_middle = half - 1 - d if left else d - half
    each = pieces // len(x_refs)

    def term(refs, p):
        return refs[p // each].at[pl.ds(p % each * rows, rows)]

    def held(ref, p):
        return ref.at[pl.ds(p * rows, rows)]

    def hop(src, dst, send, recv, to, p):
        return remote(src, dst, send.at[p], recv.at[p], tensor=to)

    sent = []

    def gather(p):
        x, kept, came = term(x_refs, p), held(acc, p), held(from_outer, p)
        src = x
        if has_outer:
            hop(x, came, up_send, up_recv, inner, p).wait_recv()
            kept[...] = (x[...].astype(jnp.float32) + came[...].astype(jnp.float32)).astype(
                acc.dtype
            )
            src = kept
        if is_middle:
            start_all([hop(src, held(from_middle, p), mid_send, mid_recv, inner, p)], sent)
        else:
            start_all([hop(src, came, up_send, up_recv, inner, p)], sent)

    def spread_out(p):
        out, came = term(out_refs, p), held(from_middle, p)
        if is_middle:
            src = held(acc, p) if has_outer else term(x_refs, p)
            hop(src, came, mid_send, mid_recv, inner, p).wait_recv()
            out[...] = (src[...].astype(jnp.float32) + came[...].astype(jnp.float32)).astype(
                acc.dtype
            )
        else:
            hop(out, out, down_send, down_recv, inner, p).wait_recv()
        if has_outer:
            start_all([hop(out, out, down_send, down_recv, outer, p)], sent)

    lag = min(pieces, lag * (1 + 2 * to_middle)) if has_outer else pieces
    for p in range(pieces + lag):
        if p < pieces:
            gather(p)
        if p >= lag:
            spread_out(p - lag)
    for copy in sent:
        copy.wait_send()


def tensor_sum_kernel(n, count, pieces, rows, lag, *refs):
    x_refs, out_refs = refs[:count], refs[count : 2 * count]
    acc, from_outer, from_middle = refs[2 * count : 2 * count + 3]
    sems = refs[2 * count + 3 :]
    me = lax.axis_index("tensor")
    for d in range(n):

        @pl.when(me == d)
        def role():
            greet([{"tensor": at} for at in (d - 1, d + 1) if 0 <= at < n])
            middle_role(
                d, n, pieces, rows, lag, x_refs, out_refs, acc, from_outer, from_middle, sems
            )


def piece_count(rows, most):
    units = rows // ROW_TILE
    return max(p for p in range(1, most + 1) if units % p == 0)


def tensor_sum(*terms):
    n = lax.axis_size("tensor")
    if n == 1:
        return list(terms)
    count = len(terms)
    shape, dtype = terms[0].shape, terms[0].dtype
    each = piece_count(shape[0], 12)
    rows = shape[0] // each
    pieces = each * count
    sem = pltpu.SemaphoreType.DMA((pieces,))
    return pl.pallas_call(
        functools.partial(tensor_sum_kernel, n, count, pieces, rows, 2),
        out_shape=[jax.ShapeDtypeStruct(shape, dtype)] * count,
        in_specs=[VMEM] * count,
        out_specs=[VMEM] * count,
        scratch_shapes=[pltpu.VMEM((shape[0] * count, shape[1]), dtype)] * 3 + [sem] * 6,
        compiler_params=pltpu.CompilerParams(
            collective_id=0 if count == 1 else 6, has_side_effects=True
        ),
        cost_estimate=link_cost(100 * count * terms[0].size * dtype.itemsize),
        name="tensor_sum",
    )(*terms)


def opening_kernel(
    sizes,
    part_ref,
    add_ref,
    bias_ref,
    mod_ref,
    bias_all,
    held,
    ctx_send,
    ctx_recv,
    col_send,
    col_recv,
    bias_send,
    bias_recv,
):
    n_sec, n_ten, n_ctx = sizes
    sec, ten, ctx = (lax.axis_index(name) for name in ("section", "tensor", "ctx"))
    ctxs = [lax.rem(ctx + k, n_ctx) for k in range(n_ctx)]
    steps = [(a, b) for a in range(n_sec) for b in range(n_ten) if (a, b) != (0, 0)]
    places = [
        {"section": lax.rem(sec + a, n_sec), "tensor": lax.rem(ten + b, n_ten)} for a, b in steps
    ]
    greet([{"ctx": c} for c in ctxs[1:]] + places)
    sent = []

    def across(k, slot):
        return remote(
            part_ref, held.at[slot], ctx_send.at[k - 1], ctx_recv.at[k - 1], ctx=ctxs[k]
        )

    def biases(k, slot):
        return remote(
            bias_ref,
            bias_all.at[slot],
            bias_send.at[k - 1],
            bias_recv.at[k - 1],
            section=lax.rem(sec + k, n_sec),
        )

    for k in range(1, n_ctx):
        start_all([across(k, ctx)], sent)
    for k in range(1, n_sec):
        start_all([biases(k, sec)], sent)
    held[ctx] = part_ref[...]
    bias_all[sec] = bias_ref[...]
    for k in range(1, n_ctx):
        across(k, lax.rem(ctx + n_ctx - k, n_ctx)).wait_recv()
    total = add_ref[...]
    for k in range(n_ctx):
        total = total + held[k]
    mod_ref[sec, ten] = total

    def column(at, block):
        return remote(block, block, col_send.at[at], col_recv.at[at], **places[at])

    for at in range(len(steps)):
        start_all([column(at, mod_ref.at[sec, ten])], sent)
    for at, (a, b) in enumerate(steps):
        theirs = mod_ref.at[lax.rem(sec + n_sec - a, n_sec), lax.rem(ten + n_ten - b, n_ten)]
        column(at, theirs).wait_recv()
    for k in range(1, n_sec):
        biases(k, lax.rem(sec + n_sec - k, n_sec)).wait_recv()
    for copy in sent:
        copy.wait_send()


def opening(part, add, bias):
    sizes = n_sec, n_ten, n_ctx = tuple(
        lax.axis_size(name) for name in ("section", "tensor", "ctx")
    )
    dma = pltpu.SemaphoreType.DMA
    return pl.pallas_call(
        functools.partial(opening_kernel, sizes),
        out_shape=[
            jax.ShapeDtypeStruct((n_sec, n_ten) + part.shape, part.dtype),
            jax.ShapeDtypeStruct((n_sec,) + bias.shape, bias.dtype),
        ],
        in_specs=[VMEM] * 3,
        out_specs=[VMEM] * 2,
        scratch_shapes=[
            pltpu.VMEM((n_ctx,) + part.shape, part.dtype),
            dma((max(n_ctx - 1, 1),)),
            dma((max(n_ctx - 1, 1),)),
            dma((n_sec * n_ten,)),
            dma((n_sec * n_ten,)),
            dma((max(n_sec - 1, 1),)),
            dma((max(n_sec - 1, 1),)),
        ],
        compiler_params=pltpu.CompilerParams(collective_id=1, has_side_effects=True),
        cost_estimate=link_cost(40 * n_sec * n_ten * part.size * part.dtype.itemsize),
        name="opening",
    )(part, add, bias)


def group_peers(n_sec, n_ctx):
    ni = inner_size(n_ctx)
    no = n_ctx // ni
    sec, ctx = lax.axis_index("section"), lax.axis_index("ctx")
    i, o = lax.rem(ctx, ni), lax.div(ctx, ni)
    far = {
        (a, b): {"section": lax.rem(sec + a, n_sec), "ctx": lax.rem(o + b, no) * ni + i}
        for a in range(n_sec)
        for b in range(no)
        if (a, b) != (0, 0)
    }
    near = {m: {"ctx": o * ni + lax.rem(i + m, ni)} for m in range(1, ni)}
    return sec, i, o, ni, no, far, near


def spread_kernel(n_sec, n_ctx, own_ref, both_ref, own_all, both_all, *sems):
    far_send, far_recv, near_send, near_recv, own_sem = sems
    sec, i, o, ni, no, far, near = group_peers(n_sec, n_ctx)
    greet(list(far.values()) + list(near.values()))
    sent = []
    me = o * ni + i

    def far_copies(step):
        a, b = step
        at = a * no + b
        copies = []
        if a == 0:
            copies.append(
                remote(
                    own_ref, own_all.at[me], far_send.at[0, at], far_recv.at[0, at], **far[step]
                )
            )
        copies.append(
            remote(
                both_ref, both_all.at[sec, me], far_send.at[1, at], far_recv.at[1, at], **far[step]
            )
        )
        return copies

    def near_copies(m, a, b, own_src, both_src, s_at, c_at):
        at = a * no + b
        copies = []
        if a == 0:
            copies.append(
                remote(
                    own_src,
                    own_all.at[c_at],
                    near_send.at[0, m - 1, at],
                    near_recv.at[0, m - 1, at],
                    **near[m],
                )
            )
        copies.append(
            remote(
                both_src,
                both_all.at[s_at, c_at],
                near_send.at[1, m - 1, at],
                near_recv.at[1, m - 1, at],
                **near[m],
            )
        )
        return copies

    for step in far:
        start_all(far_copies(step), sent)
    for m in near:
        start_all(near_copies(m, 0, 0, own_ref, both_ref, sec, me), sent)
    keep = [
        pltpu.make_async_copy(own_ref, own_all.at[me], own_sem.at[0]),
        pltpu.make_async_copy(both_ref, both_all.at[sec, me], own_sem.at[1]),
    ]
    for copy in keep:
        copy.start()
    for step in far:
        a, b = step
        for copy in far_copies(step):
            copy.wait_recv()
        s_at = lax.rem(sec + n_sec - a, n_sec)
        c_at = lax.rem(o + no - b, no) * ni + i
        for m in near:
            start_all(
                near_copies(m, a, b, own_all.at[c_at], both_all.at[s_at, c_at], s_at, c_at), sent
            )
    for m in near:
        for a in range(n_sec):
            for b in range(no):
                s_at = lax.rem(sec + n_sec - a, n_sec)
                c_at = lax.rem(o + no - b, no) * ni + lax.rem(i + ni - m, ni)
                for copy in near_copies(
                    m, a, b, own_all.at[c_at], both_all.at[s_at, c_at], s_at, c_at
                ):
                    copy.wait_recv()
    for copy in keep:
        copy.wait()
    for copy in sent:
        copy.wait_send()


def spread(own, both):
    n_sec, n_ctx = lax.axis_size("section"), lax.axis_size("ctx")
    ni = inner_size(n_ctx)
    no = n_ctx // ni
    dma = pltpu.SemaphoreType.DMA
    return pl.pallas_call(
        functools.partial(spread_kernel, n_sec, n_ctx),
        out_shape=[
            jax.ShapeDtypeStruct((n_ctx,) + own.shape, own.dtype),
            jax.ShapeDtypeStruct((n_sec, n_ctx) + both.shape, both.dtype),
        ],
        in_specs=[VMEM, VMEM],
        out_specs=[VMEM, VMEM],
        scratch_shapes=[
            dma((2, n_sec * no)),
            dma((2, n_sec * no)),
            dma((2, ni, n_sec * no)),
            dma((2, ni, n_sec * no)),
            dma((2,)),
        ],
        compiler_params=pltpu.CompilerParams(collective_id=2, has_side_effects=True),
        name="spread",
    )(own, both)


def owner_kernel(n_sec, n_ctx, own_ref, both_ref, own_out, both_out, *refs):
    own_pair, both_pair, own_far, both_far = refs[:4]
    far_send, far_recv, near_send, near_recv = refs[4:]
    sec, i, o, ni, no, far, near = group_peers(n_sec, n_ctx)
    greet(list(far.values()) + list(near.values()))
    sent = []

    def near_copies(m, a, b):
        to = lax.rem(i + m, ni)
        s_at, o_at = lax.rem(sec + a, n_sec), lax.rem(o + b, no)
        at = a * no + b
        copies = []
        if a == 0:
            copies.append(
                remote(
                    own_ref.at[o_at * ni + to],
                    own_pair.at[m - 1, b],
                    near_send.at[0, m - 1, at],
                    near_recv.at[0, m - 1, at],
                    **near[m],
                )
            )
        copies.append(
            remote(
                both_ref.at[s_at, o_at * ni + to],
                both_pair.at[m - 1, at],
                near_send.at[1, m - 1, at],
                near_recv.at[1, m - 1, at],
                **near[m],
            )
        )
        return copies

    order = list(far) + [(0, 0)]
    for step in order:
        for m in near:
            start_all(near_copies(m, *step), sent)

    def far_copies(a, b):
        at = a * no + b
        copies = []
        if a == 0:
            copies.append(
                remote(
                    own_pair.at[ni - 1, b],
                    own_far.at[b],
                    far_send.at[0, at],
                    far_recv.at[0, at],
                    **far[(a, b)],
                )
            )
        copies.append(
            remote(
                both_pair.at[ni - 1, at],
                both_far.at[at],
                far_send.at[1, at],
                far_recv.at[1, at],
                **far[(a, b)],
            )
        )
        return copies

    for a, b in order:
        s_at, c_at = lax.rem(sec + a, n_sec), lax.rem(o + b, no) * ni + i
        at = a * no + b
        for m in near:
            for copy in near_copies(m, a, b):
                copy.wait_recv()
        total_both = both_ref[s_at, c_at].astype(jnp.float32)
        for m in near:
            total_both = total_both + both_pair[m - 1, at].astype(jnp.float32)
        total_own = None
        if a == 0:
            total_own = own_ref[c_at].astype(jnp.float32)
            for m in near:
                total_own = total_own + own_pair[m - 1, b].astype(jnp.float32)
        if (a, b) == (0, 0):
            own_out[...] = total_own
            both_out[...] = total_both
        else:
            if a == 0:
                own_pair[ni - 1, b] = total_own.astype(own_pair.dtype)
            both_pair[ni - 1, at] = total_both.astype(both_pair.dtype)
            start_all(far_copies(a, b), sent)
    for a, b in far:
        for copy in far_copies(a, b):
            copy.wait_recv()
        if a == 0:
            own_out[...] += own_far[b].astype(jnp.float32)
        both_out[...] += both_far[a * no + b].astype(jnp.float32)
    for copy in sent:
        copy.wait_send()


def owner_sum(own, both):
    n_sec, n_ctx = lax.axis_size("section"), lax.axis_size("ctx")
    ni = inner_size(n_ctx)
    no = n_ctx // ni
    dma = pltpu.SemaphoreType.DMA
    own_shape, both_shape = own.shape[1:], both.shape[2:]
    return pl.pallas_call(
        functools.partial(owner_kernel, n_sec, n_ctx),
        out_shape=[
            jax.ShapeDtypeStruct(own_shape, jnp.float32),
            jax.ShapeDtypeStruct(both_shape, jnp.float32),
        ],
        in_specs=[VMEM, VMEM],
        out_specs=[VMEM, VMEM],
        scratch_shapes=[
            pltpu.VMEM((ni, no) + own_shape, own.dtype),
            pltpu.VMEM((ni, n_sec * no) + both_shape, both.dtype),
            pltpu.VMEM((no,) + own_shape, own.dtype),
            pltpu.VMEM((n_sec * no,) + both_shape, both.dtype),
            dma((2, n_sec * no)),
            dma((2, n_sec * no)),
            dma((2, ni, n_sec * no)),
            dma((2, ni, n_sec * no)),
        ],
        compiler_params=pltpu.CompilerParams(collective_id=3, has_side_effects=True),
        name="owner_sum",
    )(own, both)


def small_kernel(axes, sizes, x_ref, out_ref, held, send, recv):
    at = [lax.axis_index(name) for name in axes]
    steps = [(a, b) for a in range(sizes[0]) for b in range(sizes[1])]
    places = [
        [lax.rem(here + sign * step + size, size) for here, step, size in zip(at, pair, sizes)]
        for sign in (1, -1)
        for pair in steps
    ]
    to, source = places[: len(steps)], places[len(steps) :]
    where = [dict(zip(axes, place)) for place in to]
    greet(where[1:])

    def block(place):
        return place[0] if x_ref.shape[0] > 1 else 0

    def copy(k, slot):
        return remote(
            x_ref.at[block(to[k])],
            held.at[slot[0] * sizes[1] + slot[1]],
            send.at[k - 1],
            recv.at[k - 1],
            **where[k],
        )

    copies = [copy(k, at) for k in range(1, len(steps))]
    for started in copies:
        started.start()
    held[at[0] * sizes[1] + at[1]] = x_ref[block(at)]
    for k in range(1, len(steps)):
        copy(k, source[k]).wait_recv()
    total = held[0]
    for k in range(1, len(steps)):
        total = total + held[k]
    out_ref[...] = total
    for started in copies:
        started.wait_send()


def small_sum(x, axes, collective_id):
    sizes = tuple(lax.axis_size(name) for name in axes)
    n = sizes[0] * sizes[1]
    dma = pltpu.SemaphoreType.DMA((max(n - 1, 1),))
    return pl.pallas_call(
        functools.partial(small_kernel, axes, sizes),
        out_shape=jax.ShapeDtypeStruct(x.shape[1:], x.dtype),
        in_specs=[VMEM],
        out_specs=VMEM,
        scratch_shapes=[pltpu.VMEM((n,) + x.shape[1:], x.dtype), dma, dma],
        compiler_params=pltpu.CompilerParams(collective_id=collective_id, has_side_effects=True),
        cost_estimate=link_cost(100 * n * x[0].size * x.dtype.itemsize),
        name="small_sum",
    )(x)


def packed(pieces, width):
    flat = jnp.concatenate([p.reshape(-1) for p in pieces])
    rows = -(-flat.shape[0] // width)
    rows = -(-rows // 8) * 8
    return jnp.pad(flat, (0, rows * width - flat.shape[0])).reshape(rows, width)


def compact(array):
    return packed([array], -(-array.size // 8))


def unpacked(block, shapes):
    flat, at, out = block.reshape(-1), 0, []
    for shape in shapes:
        size = math.prod(shape)
        out.append(flat[at : at + size].reshape(shape))
        at += size
    return out


def layer_norm(values):
    centre = jnp.mean(values, axis=-1, keepdims=True)
    centred = values - centre
    variance = jnp.mean(centred * centred, axis=-1, keepdims=True)
    inverse = lax.rsqrt(variance + EPSILON)
    return centred * inverse


def norm_back_kernel(scale_at, gate_at, up_ref, x_ref, base_ref, mod_ref, *refs):
    x = x_ref[...].astype(jnp.float32)
    centred = x - jnp.mean(x, axis=-1, keepdims=True)
    inverse = lax.rsqrt(jnp.mean(centred * centred, axis=-1, keepdims=True) + EPSILON)
    normed = centred * inverse
    upstream = up_ref[...].astype(jnp.float32)
    scaled = upstream * (1.0 + mod_ref[0, scale_at : scale_at + 1, :])
    mean_grad = jnp.mean(scaled, axis=-1, keepdims=True)
    mean_cross = jnp.mean(scaled * normed, axis=-1, keepdims=True)
    grad = base_ref[...] + inverse * (scaled - mean_grad - normed * mean_cross)
    if gate_at is None:
        grad_ref, sums_ref = refs
    else:
        term_ref, bias_ref, gate_ref, grad_ref, gated_ref, sums_ref = refs
        gated = grad * gate_ref[0, gate_at : gate_at + 1, :]
        gated_ref[...] = gated.astype(gated_ref.dtype)
        term = term_ref[...].astype(jnp.float32) + bias_ref[...]
        sums_ref[0, 2:3, :] = jnp.sum(grad * term, axis=0, keepdims=True)
        sums_ref[0, 3:4, :] = jnp.sum(gated, axis=0, keepdims=True)
    grad_ref[...] = grad
    sums_ref[0, 0:1, :] = jnp.sum(upstream, axis=0, keepdims=True)
    sums_ref[0, 1:2, :] = jnp.sum(upstream * normed, axis=0, keepdims=True)


def norm_back(rows, upstream, x, base, mods, scale_at, gate=None):
    part, width = rows.part, rows.width
    runs = rows.rows // part
    tile = pl.BlockSpec((part, width), lambda at: (at, 0))
    per_run = pl.BlockSpec((1, mods.shape[1], width), lambda at: (at, 0, 0))
    sums = pl.BlockSpec((1, 8, width), lambda at: (at, 0, 0))
    args, in_specs = [upstream, x, base, mods], [tile] * 3 + [per_run]
    shape = jax.ShapeDtypeStruct((rows.rows, width), jnp.float32)
    out_shape, out_specs = [shape], [tile]
    if gate:
        term, bias, gate_mods, gate_at = gate
        args += [term, bias[None], gate_mods]
        in_specs += [tile, pl.BlockSpec((1, width), lambda at: (0, 0)), per_run]
        out_shape.append(jax.ShapeDtypeStruct((rows.rows, width), jnp.bfloat16))
        out_specs.append(tile)
    return pl.pallas_call(
        functools.partial(norm_back_kernel, scale_at, gate_at if gate else None),
        grid=(runs,),
        out_shape=out_shape + [jax.ShapeDtypeStruct((runs, 8, width), jnp.float32)],
        in_specs=in_specs,
        out_specs=out_specs + [sums],
        compiler_params=pltpu.CompilerParams(vmem_limit_bytes=32 * 1024 * 1024),
        cost_estimate=pl.CostEstimate(
            flops=30 * rows.rows * width,
            bytes_accessed=18 * rows.rows * width,
            transcendentals=rows.rows,
        ),
        name="norm_back",
    )(*args)


def gelu_back(pre_act, upstream):
    unused_out, pullback = jax.vjp(
        lambda pre_value: jax.nn.gelu(pre_value, approximate=True), pre_act
    )
    return pullback(upstream)[0]


def heads(array):
    cols = array.shape[-2]
    return array.reshape(*array.shape[:-2], cols // HD, HD, array.shape[-1])


def score_columns(queries, keys):
    softmax_scale = 1.0 / math.sqrt(HD)
    return (
        jnp.einsum(
            "nhdk,hdq->hnkq", heads(keys), heads(queries), preferred_element_type=jnp.float32
        )
        * softmax_scale
    )


def attend(queries, keys, values):
    scores = score_columns(queries, keys)
    row_peak = jnp.max(scores, axis=(1, 2), keepdims=True)
    log_total = row_peak + jnp.log(jnp.sum(jnp.exp(scores - row_peak), axis=(1, 2), keepdims=True))
    prob_bf = jnp.exp(scores - log_total).astype(jnp.bfloat16)
    context = jnp.einsum(
        "nhdk,hnkq->hdq", heads(values), prob_bf, preferred_element_type=jnp.float32
    )
    return context.astype(jnp.bfloat16).reshape(queries.shape), log_total


def attention_grads(queries, keys, values, log_total, context, context_grad):
    softmax_scale = 1.0 / math.sqrt(HD)
    query_heads, grad_heads = heads(queries), heads(context_grad)
    delta = jnp.sum(
        grad_heads.astype(jnp.float32) * heads(context).astype(jnp.float32), axis=1
    )[:, None, None, :]
    prob_full = jnp.exp(score_columns(queries, keys) - log_total)
    prob_bf = prob_full.astype(jnp.bfloat16)
    prob_grad = jnp.einsum(
        "nhdk,hdq->hnkq", heads(values), grad_heads, preferred_element_type=jnp.float32
    )
    score_grad = (prob_full * (prob_grad - delta)).astype(jnp.bfloat16)
    query_grad = (
        jnp.einsum(
            "nhdk,hnkq->hdq", heads(keys), score_grad, preferred_element_type=jnp.float32
        )
        * softmax_scale
    ).reshape(queries.shape)
    key_part = (
        jnp.einsum("hnkq,hdq->nhdk", score_grad, query_heads, preferred_element_type=jnp.float32)
        * softmax_scale
    ).reshape(keys.shape)
    value_part = jnp.einsum(
        "hnkq,hdq->nhdk", prob_bf, grad_heads, preferred_element_type=jnp.float32
    ).reshape(values.shape)
    both = jnp.concatenate(
        [key_part.astype(jnp.bfloat16), value_part.astype(jnp.bfloat16)], axis=1
    )
    return query_grad, both


def contract(left, right, left_dim, right_dim):
    return lax.dot_general(
        left, right, (((left_dim,), (right_dim,)), ((), ())), preferred_element_type=jnp.float32
    )


class Rows:
    def __init__(self, latents, section):
        n_sec = lax.axis_size("section")
        self.n_sec = n_sec
        total, self.tokens, self.width = latents.shape
        self.section = section
        self.full = total // n_sec
        self.rest = total - self.full * n_sec
        self.part = self.tokens // n_sec
        self.own_rows = self.full * self.tokens
        self.both_rows = self.rest * self.part
        self.rows = self.own_rows + self.both_rows

    def take(self, array):
        own = lax.dynamic_slice_in_dim(array, self.section * self.full, self.full, 0)
        both = lax.dynamic_slice_in_dim(
            array[self.full * self.n_sec :], self.section * self.part, self.part, 1
        )
        return jnp.concatenate(
            [own.reshape(self.own_rows, -1), both.reshape(self.both_rows, -1)], axis=0
        )

    def split(self, array):
        return (
            array[: self.own_rows].reshape(self.full, self.tokens, -1),
            array[self.own_rows :].reshape(self.rest, self.part, -1),
        )

    def spans(self):
        out = [(at * self.tokens, self.tokens) for at in range(self.full)]
        return out + [
            (self.own_rows + at * self.part, self.part) for at in range(self.rest)
        ]

    def columns(self, array):
        return [array[:, start : start + size] for start, size in self.spans()]

    def mods(self, modulation):
        own = lax.dynamic_slice_in_dim(modulation, self.section * self.full, self.full, 0)
        return jnp.concatenate([own, modulation[self.full * self.n_sec :]], axis=0)

    def by_run(self, mods):
        runs = self.tokens // self.part
        return jnp.concatenate(
            [mods[at : at + 1] for at in range(self.full) for _ in range(runs)] + [mods[self.full :]]
        )

    def wide(self, pieces):
        row = lax.broadcasted_iota(jnp.int32, (self.rows, 1), 0)
        out = pieces[-1][None, :]
        for (start, size), piece in reversed(list(zip(self.spans(), pieces))[:-1]):
            out = jnp.where(row < start + size, piece[None, :], out)
        return out

    def sums(self, array):
        return jnp.sum(array.reshape(-1, self.part, self.width), axis=1)

    def placed(self, sums):
        runs = self.tokens // self.part
        own = sums[: self.full * runs].reshape(self.full, runs, -1).sum(axis=1)
        mine = [
            jnp.where(self.section == at // self.full, own[at % self.full], 0.0)
            for at in range(self.full * self.n_sec)
        ]
        both = [sums[self.full * runs + at] for at in range(self.rest)]
        return jnp.stack(mine + both)

    def assembled(self, per_block, received):
        own = per_block[-1]
        for b in range(self.n_sec - 1):
            own = jnp.where(self.section == b, per_block[b], own)
        others = []
        for k in range(1, self.n_sec):
            rows = received[-1][k - 1]
            for b in range(self.n_sec - 1):
                rows = jnp.where(self.section == b, received[b][k - 1], rows)
            others.append(rows)
        whole, shared = [], []
        for source in range(self.n_sec):
            rows = own
            for k, other in enumerate(others, 1):
                rows = jnp.where(lax.rem(self.section + k, self.n_sec) == source, other, rows)
            first, both = self.split(rows)
            whole.append(first)
            shared.append(both)
        return jnp.concatenate(whole + [jnp.concatenate(shared, axis=1)], axis=0)


def gathered(key_value, rows):
    spans = rows.spans()
    cols = [key_value[:, start : start + size] for start, size in spans]
    own = jnp.concatenate(cols[: rows.full], axis=0)
    both = jnp.concatenate(cols[rows.full :], axis=0)
    own_all, both_all = spread(own, both)
    both_all = both_all.reshape(-1, *both.shape)
    high = key_value.shape[0]
    return [own_all[:, at * high : (at + 1) * high] for at in range(rows.full)] + [
        both_all[:, at * high : (at + 1) * high] for at in range(rows.rest)
    ]


def returned(parts, rows):
    high = parts[0].shape[1]
    own = jnp.concatenate(parts[: rows.full], axis=1)
    both = jnp.concatenate(parts[rows.full :], axis=1)
    own, both = owner_sum(own, both.reshape(rows.n_sec, -1, *both.shape[1:]))
    return jnp.concatenate(
        [own[at * high : (at + 1) * high] for at in range(rows.full)]
        + [both[at * high : (at + 1) * high] for at in range(rows.rest)],
        axis=1,
    )


def forward_block(rows, block_in, mods, w_qkv, biases, prepare, mlp_weights, last):
    b_qv, b_out, b_fc1, b_fc2 = biases
    local_cols = w_qkv.shape[0] // 3
    shift_a, scale_a, gate_a, shift_m, scale_m, gate_m = (
        rows.wide([mods[at, k] for at in range(mods.shape[0])]) for k in range(6)
    )
    residual = block_in.astype(jnp.float32)
    normed_a = layer_norm(residual)
    attn_in = (normed_a * (1.0 + scale_a) + shift_a).astype(jnp.bfloat16)
    projected = contract(w_qkv, attn_in, 1, 1)
    bias = jnp.concatenate([b_qv[0], jnp.zeros_like(b_qv[0]), b_qv[1]])
    projected = (projected + bias[:, None]).astype(jnp.bfloat16)
    queries = rows.columns(projected[:local_cols])
    keys_values, w_out, sends = prepare(gathered(projected[local_cols:], rows))
    attended = [
        attend(q, kv[:, :local_cols], kv[:, local_cols:])
        for q, kv in zip(queries, keys_values)
    ]
    context = row_major(jnp.concatenate([row_major(c) for c, _ in attended], axis=1))
    attn_term = contract(context, w_out, 0, 0)
    (attn_sum,), moved = beside(tensor_sum, [attn_term.astype(jnp.bfloat16)], sends)
    w_fc1, w_fc2 = mlp_weights(moved)
    attn_out = attn_sum.astype(jnp.float32) + b_out
    middle = residual + gate_a * attn_out
    normed_m = layer_norm(middle)
    mlp_in = (normed_m * (1.0 + scale_m) + shift_m).astype(jnp.bfloat16)
    pre_act = jnp.dot(mlp_in, w_fc1, preferred_element_type=jnp.float32) + b_fc1
    hidden = jax.nn.gelu(pre_act, approximate=True).astype(jnp.bfloat16)
    mlp_term = jnp.dot(hidden, w_fc2, preferred_element_type=jnp.float32).astype(jnp.bfloat16)

    def close(mlp_sum):
        mlp_out = mlp_sum.astype(jnp.float32) + b_fc2
        return mlp_out, (middle + gate_m * mlp_out).astype(jnp.bfloat16)

    block_res, mlp_sum = None, None
    if not last:
        (mlp_sum,) = tensor_sum(mlp_term)
        block_res = close(mlp_sum)[1]
    stored = (
        block_in,
        attn_in,
        queries,
        keys_values,
        [log_total for _, log_total in attended],
        context,
        attn_sum,
        middle,
        mlp_in,
        pre_act,
        hidden,
        mlp_sum,
    )
    return block_res, stored, moved, (mlp_term, close) if last else None


def backward_block(
    rows, upstream, gated, stored, run_mods, weights, block, firsts, seconds, pending, b_out, below
):
    w_qkv, w_out, w_fc1, w_fc2 = weights
    (
        block_in,
        attn_in,
        queries,
        keys_values,
        log_totals,
        context,
        attn_sum,
        middle,
        mlp_in,
        pre_act,
        hidden,
        mlp_sum,
    ) = stored
    mlp_grad_b, gate_m_grad, grad_b2 = gated
    local_cols = w_qkv.shape[0] // 3
    pre_grad = gelu_back(pre_act, jnp.dot(mlp_grad_b, w_fc2.T, preferred_element_type=jnp.float32))
    pre_grad_b = pre_grad.astype(jnp.bfloat16)
    grad_b1 = jnp.sum(pre_grad, axis=0)
    mlp_pair = inner_pair(
        [contract(mlp_grad_b, hidden, 0, 0), contract(mlp_in, pre_grad_b, 0, 0)]
    )
    mlp_term = jnp.dot(pre_grad_b, w_fc1.T, preferred_element_type=jnp.float32)
    terms = [mlp_term.astype(jnp.bfloat16)]
    if pending:
        terms.append(pending[0])
    outer = outer_sends(mlp_pair)
    (mlp_in_grad, *sums), moved = beside(tensor_sum, terms, outer + firsts)
    block_res = None
    if pending:
        mlp_out, block_res = pending[1](sums[0])
        gate_m_grad = rows.sums(upstream * mlp_out)
    first_moved = moved[len(outer) :]
    mlp_share = outer_total(mlp_pair, moved[: len(outer)])
    middle_grad, attn_grad_b, m_sums = norm_back(
        rows, mlp_in_grad, middle, upstream, run_mods, 4, (attn_sum, b_out, run_mods, 2)
    )
    grad_bo = jnp.sum(m_sums[:, 3], axis=0)
    context_grad = contract(w_out, attn_grad_b, 1, 1).astype(jnp.bfloat16)
    query_grads, key_value_parts = zip(
        *(
            attention_grads(q, kv[:, :local_cols], kv[:, local_cols:], log_total, c, cg)
            for q, kv, log_total, c, cg in zip(
                queries, keys_values, log_totals, rows.columns(context), rows.columns(context_grad)
            )
        )
    )
    query_grad = row_major(jnp.concatenate([row_major(g) for g in query_grads], axis=1))
    key_value_grad = returned(key_value_parts, rows)
    grad_bqv = jnp.stack(
        [jnp.sum(query_grad, axis=1), jnp.sum(key_value_grad[local_cols:], axis=1)]
    )
    qkv_grad_b = jnp.concatenate([query_grad, key_value_grad], axis=0).astype(jnp.bfloat16)
    qkv_rows, context_rows = row_major(row_major(qkv_grad_b).T), row_major(row_major(context).T)
    attn_term = contract(qkv_rows, w_qkv, 1, 0)
    attn_pairs = [
        inner_pair([contract(attn_in, qkv_rows, 0, 0)]),
        inner_pair([contract(attn_grad_b, context_rows, 0, 0)]),
    ]
    outers = [outer_sends(pair) for pair in attn_pairs]
    across = block_sends(mlp_share, block)
    sends = [*outers, across, seconds]
    ((attn_in_grad,), moved) = beside(
        tensor_sum, [attn_term.astype(jnp.bfloat16)], [send for part in sends for send in part]
    )
    came = []
    for part in sends:
        came.append(moved[: len(part)])
        moved = moved[len(part) :]
    attn_shares = [outer_total(pair, part) for pair, part in zip(attn_pairs, came)]
    mlp_share = block_total(mlp_share, came[-2])
    second_moved = came[-1]
    input_grad, *gated, a_sums = norm_back(
        rows, attn_in_grad, block_in, middle_grad, run_mods, 1, below
    )
    if below:
        gated += [a_sums[:, 2], jnp.sum(a_sums[:, 3], axis=0)]
    mod_grad = jnp.concatenate(
        [a_sums[:, 0], a_sums[:, 1], m_sums[:, 2], m_sums[:, 0], m_sums[:, 1], gate_m_grad], axis=1
    )
    return (
        input_grad,
        gated,
        mod_grad,
        (grad_bqv, grad_bo, grad_b1, grad_b2),
        (mlp_share, *attn_shares),
        block_res,
        first_moved,
        second_moved,
    )


def to_inner(value, by):
    n = lax.axis_size("ctx")
    ni = inner_size(n)
    return lax.ppermute(value, "ctx", [(a, a // ni * ni + (a + by) % ni) for a in range(n)])


def to_outer(value, by):
    n = lax.axis_size("ctx")
    ni = inner_size(n)
    return lax.ppermute(value, "ctx", [(a, (a + by * ni) % n) for a in range(n)])


def to_section(value, by):
    n = lax.axis_size("section")
    return lax.ppermute(value, "section", [(a, (a + by) % n) for a in range(n)])


def to_block(value, block, by):
    n = lax.axis_size("section")
    return lax.ppermute(value, "section", [((block + by) % n, block)])


def ctx_place():
    n = lax.axis_size("ctx")
    ni = inner_size(n)
    at = lax.axis_index("ctx")
    return n // ni, ni, lax.div(at, ni), lax.rem(at, ni)


def beside(kernel, args, sends):
    args, values = lax.optimization_barrier((args, [value for value, _ in sends]))
    moved = [move(value) for value, (_, move) in zip(values, sends)]
    return lax.optimization_barrier((kernel(*args), moved))


def half_of(weights):
    _, ni, _, i = ctx_place()
    sizes = [w.shape[0] // ni for w in weights]
    return jnp.concatenate(
        [lax.dynamic_slice_in_dim(w, i * size, size, 0) for w, size in zip(weights, sizes)]
    )


def joined(own, passed, weights):
    _, ni, _, i = ctx_place()
    found, start = [], 0
    for w in weights:
        size = w.shape[0] // ni
        parts = [piece[start : start + size] for piece in [own] + passed]
        start += size
        ordered = []
        for at in range(ni):
            piece = parts[0]
            for m in range(1, ni):
                piece = jnp.where(lax.rem(i + ni - m, ni) == at, parts[m], piece)
            ordered.append(piece)
        found.append(jnp.concatenate(ordered))
    return found


def chosen_blocks(weights, others):
    n_sec = lax.axis_size("section")
    section = lax.axis_index("section")
    blocks = []
    for b in range(n_sec):
        chosen = list(weights)
        for k, found in enumerate(others, 1):
            is_source = lax.rem(section + n_sec - k, n_sec) == b
            chosen = [jnp.where(is_source, new, old) for new, old in zip(found, chosen)]
        blocks.append(chosen)
    return blocks


def fetched(weights):
    n_sec = lax.axis_size("section")
    groups = [
        [at for at, w in enumerate(weights) if w.shape[1] == width]
        for width in sorted({w.shape[1] for w in weights})
    ]
    halves = [half_of([weights[at] for at in group]) for group in groups]
    return groups, [[to_section(half, k) for k in range(1, n_sec)] for half in halves]


def passing(fetch):
    _, ni, _, _ = ctx_place()
    return [
        (half, functools.partial(to_inner, by=m))
        for of_group in fetch[1]
        for half in of_group
        for m in range(1, ni)
    ]


def every_block(weights, fetch, passed):
    _, ni, _, _ = ctx_place()
    n_sec = lax.axis_size("section")
    others = [[None] * len(weights) for _ in range(n_sec - 1)]
    passed = list(passed)
    for group, of_group in zip(*fetch):
        for k, half in enumerate(of_group):
            rest = [passed.pop(0) for _ in range(1, ni)]
            for at, whole in zip(group, joined(half, rest, [weights[at] for at in group])):
                others[k][at] = whole
    return chosen_blocks(weights, others)


def inner_pair(terms):
    no, ni, _, i = ctx_place()
    terms = [
        row_major(t.astype(jnp.bfloat16)).reshape(no, ni, -1, t.shape[-1]) for t in terms
    ]

    def inner(at):
        return row_major(
            jnp.concatenate(
                [lax.dynamic_index_in_dim(t, at, 1, keepdims=False) for t in terms], axis=1
            )
        )

    pair = inner(i).astype(jnp.float32)
    for m in range(1, ni):
        pair = pair + to_inner(inner(lax.rem(i + m, ni)), m).astype(jnp.float32)
    return pair.astype(jnp.bfloat16)


def outer_sends(pair):
    no, _, o, _ = ctx_place()
    return [
        (
            lax.dynamic_index_in_dim(pair, lax.rem(o + m, no), 0, keepdims=False),
            functools.partial(to_outer, by=m),
        )
        for m in range(1, no)
    ]


def outer_total(pair, moved):
    _, _, o, _ = ctx_place()
    total = lax.dynamic_index_in_dim(pair, o, 0, keepdims=False).astype(jnp.float32)
    for piece in moved:
        total = total + piece.astype(jnp.float32)
    return total


def block_sends(value, block):
    value = value.astype(jnp.bfloat16)
    return [
        (value, functools.partial(to_block, block=block, by=k))
        for k in range(1, lax.axis_size("section"))
    ]


def block_total(own, moved):
    for piece in moved:
        own = own + piece.astype(jnp.float32)
    return own


def local(
    latents,
    condition,
    cotangent,
    w_ada,
    b_ada,
    w_qkv,
    b_qv,
    w_out,
    b_out,
    w_fc1,
    b_fc1,
    w_fc2,
    b_fc2,
):
    section = lax.axis_index("section")
    n_sec = lax.axis_size("section")
    latent_total, token_count, width = latents.shape
    width_cols = b_ada.shape[-1]
    local_cols = w_qkv.shape[-1]
    rows = Rows(latents, section)
    cond_act = jax.nn.silu(condition).astype(jnp.bfloat16)
    mod_part = jnp.dot(cond_act, w_ada[0], preferred_element_type=jnp.float32)
    bias_shapes = [b_qv.shape[1:], b_out.shape[1:], b_fc1.shape[1:], b_fc2.shape[1:]]
    bias_flat = jnp.concatenate([b.reshape(-1) for b in (b_qv, b_out, b_fc1, b_fc2)])
    qkv_weights = [row_major(jnp.transpose(w_qkv[0], (1, 2, 0)).reshape(3 * local_cols, width))]
    qkv_fetch = fetched(qkv_weights)
    mod_all, bias_all = opening(
        compact(mod_part),
        compact(jnp.broadcast_to(b_ada, (latent_total, width_cols))),
        compact(bias_flat),
    )
    mod_all, fc1_weights = lax.optimization_barrier((mod_all, [w_fc1[0]]))
    fc1_fetch = fetched(fc1_weights)
    qkv_blocks = every_block(
        qkv_weights, qkv_fetch, [move(half) for half, move in passing(qkv_fetch)]
    )
    tensor = lax.axis_index("tensor")
    columns = mod_all.reshape(n_sec, -1, mod_all.shape[-2] * mod_all.shape[-1])
    columns = columns[..., : latent_total * width_cols]
    columns = columns.reshape(n_sec, -1, latent_total, width_cols)
    modulation = jnp.swapaxes(columns, 1, 2).reshape(n_sec, latent_total, 6, width)
    biases, mods = [], []
    for b in range(n_sec):
        biases.append(unpacked(bias_all[b], bias_shapes))
        mods.append(rows.mods(modulation[b]))
    residual = rows.take(latents)
    outs, out_moved, kept, out_blocks, mlp_blocks, pending = [], [], [], [], [], None
    for b in range(n_sec):
        if b == 0:
            late = []

            def prepare(keys_values):
                keys_values, weights = lax.optimization_barrier(
                    (keys_values, [w_out[0], w_fc2[0]])
                )
                for weight in weights:
                    late.append(([weight], fetched([weight])))
                weights, fetch = late[0]
                out_blocks.extend(
                    every_block(weights, fetch, [move(half) for half, move in passing(fetch)])
                )
                return keys_values, out_blocks[0][0], passing(fc1_fetch)

            def finish(moved):
                firsts = every_block(fc1_weights, fc1_fetch, moved)
                weights, fetch = late[1]
                seconds = every_block(
                    weights, fetch, [move(half) for half, move in passing(fetch)]
                )
                mlp_blocks.extend([*one, *two] for one, two in zip(firsts, seconds))
                return mlp_blocks[0]

        else:
            sends = block_sends(outs[-1], b - 1)

            def prepare(keys_values, sends=sends, b=b):
                return keys_values, out_blocks[b][0], sends

            def finish(moved, b=b):
                return mlp_blocks[b]

        residual, stored, moved, pending = forward_block(
            rows,
            residual,
            mods[b],
            qkv_blocks[b][0],
            biases[b],
            prepare,
            finish,
            b == n_sec - 1,
        )
        if b:
            out_moved.append(moved)
        outs.append(residual)
        kept.append(stored)
    upstream = rows.take(cotangent).astype(jnp.float32)
    run_mods = [rows.by_run(block_mods) for block_mods in mods]
    top_grad = upstream * rows.wide([mods[-1][at, 5] for at in range(mods[-1].shape[0])])
    gated = (top_grad.astype(jnp.bfloat16), None, jnp.sum(top_grad, axis=0))
    in_grads, in_moved, small, shares = ([None] * n_sec for _ in range(4))
    out_moved.append([])
    firsts, seconds = [[], []], []
    for b in reversed(range(n_sec)):
        below = (kept[b - 1][-1], biases[b - 1][3], run_mods[b - 1], 5) if b else None
        upstream, gated, mod_grad, bias_grads, shares[b], block_res, first_moved, second_moved = (
            backward_block(
                rows,
                upstream,
                gated,
                kept[b],
                run_mods[b],
                (*qkv_blocks[b], *out_blocks[b], *mlp_blocks[b]),
                b,
                [send for part in firsts for send in part],
                seconds,
                pending if b == n_sec - 1 else None,
                biases[b][1],
                below,
            )
        )
        if b == n_sec - 1:
            outs[b] = block_res
        else:
            at = 0
            for which in (1, 2):
                part = first_moved[at : at + n_sec - 1]
                at += n_sec - 1
                shares[b + 1][which] = block_total(shares[b + 1][which], part)
            if b == n_sec - 2:
                out_moved[-1] = first_moved[at:]
            in_moved[b + 1] = second_moved
        shares[b] = list(shares[b])
        in_grads[b] = upstream.astype(jnp.bfloat16)
        cols = mod_grad[:, :width_cols]
        for t in range(1, lax.axis_size("tensor")):
            cols = jnp.where(tensor == t, mod_grad[:, t * width_cols : (t + 1) * width_cols], cols)
        small[b] = packed([rows.placed(cols), *bias_grads], width)
        firsts = [block_sends(share, b) for share in shares[b][1:]]
        if b == n_sec - 1:
            firsts.append(block_sends(outs[b], b))
        seconds = block_sends(in_grads[b], b)
    def mine(which):
        out = shares[-1][which]
        for b in range(n_sec - 1):
            out = jnp.where(section == b, shares[b][which], out)
        return out

    last = firsts[0] + firsts[1] + seconds
    small_in, values = lax.optimization_barrier(
        (jnp.stack(small), [value for value, _ in last])
    )
    moved = [move(value) for value, (_, move) in zip(values, last)]
    mlp_share = mine(0)
    share_rows = mlp_share.shape[0] // 2
    grad_fc1, grad_fc2 = mlp_share[share_rows:][None], mlp_share[:share_rows].T[None]
    block_out = rows.assembled(outs, out_moved)[None]
    small_in, grad_fc1, grad_fc2, block_out = lax.optimization_barrier(
        (small_in, grad_fc1, grad_fc2, block_out)
    )
    summed, moved = lax.optimization_barrier(
        (small_sum(small_in, ("section", "ctx"), 4), moved)
    )
    for which in (1, 2):
        shares[0][which] = block_total(shares[0][which], moved[: n_sec - 1])
        moved = moved[n_sec - 1 :]
    in_moved[0] = moved
    in_grad = rows.assembled(in_grads, in_moved).astype(jnp.float32)
    qkv_share, out_share = mine(1), mine(2)
    mod_total, grad_bqv, grad_bo, grad_b1, grad_b2 = unpacked(
        summed, [(latent_total, width_cols)] + bias_shapes
    )
    mod_rounded = mod_total.astype(jnp.bfloat16)
    cond_part = jnp.dot(mod_rounded, w_ada[0].T, preferred_element_type=jnp.float32)
    cond_part = jnp.pad(cond_part, ((0, -latent_total % 8), (0, 0)))
    cond_sum = small_sum(cond_part[None], ("section", "tensor"), 5)[:latent_total]
    grad_w_ada = jnp.dot(cond_act.T, mod_rounded, preferred_element_type=jnp.float32)[None]
    grad_b_ada = jnp.sum(mod_total, axis=0)[None]
    sigmoid_c = jax.nn.sigmoid(condition)
    cond_grad = cond_sum * sigmoid_c * (1.0 + condition * (1.0 - sigmoid_c))
    return (
        block_out,
        in_grad[None],
        cond_grad,
        grad_w_ada,
        grad_b_ada,
        qkv_share.reshape(1, share_rows, 3, local_cols),
        grad_bqv[None],
        out_share.T[None],
        grad_bo[None],
        grad_fc1,
        grad_b1[None],
        grad_fc2,
        grad_b2[None],
    )


def solution(mesh):
    return jax.shard_map(
        local,
        mesh=mesh,
        in_specs=(
            P(None, "ctx", None),
            P(None, "ctx"),
            P(None, "ctx", None),
            P("section", "ctx", "tensor"),
            P("section", "tensor"),
            P("section", None, None, "tensor"),
            P("section", None, "tensor"),
            P("section", "tensor", None),
            P("section", None),
            P("section", None, "tensor"),
            P("section", "tensor"),
            P("section", "tensor", None),
            P("section", None),
        ),
        out_specs=(
            P("section", None, "ctx", None),
            P("section", None, "ctx", None),
            P(None, "ctx"),
            P("section", "ctx", "tensor"),
            P("section", "tensor"),
            P("section", "ctx", None, "tensor"),
            P("section", None, "tensor"),
            P("section", "tensor", "ctx"),
            P("section", None),
            P("section", "ctx", "tensor"),
            P("section", "tensor"),
            P("section", "tensor", "ctx"),
            P("section", None),
        ),
        check_vma=False,
    )
```

```python
import functools
import math

import jax
import jax.numpy as jnp
from jax import lax
from jax.experimental import pallas as pl
from jax.experimental.layout import Layout, with_layout_constraint
from jax.experimental.pallas import tpu as pltpu
from jax.sharding import PartitionSpec as P

HD = 72
EPSILON = 1e-06
MESH = pl.DeviceIdType.MESH
ROW_TILE = 16
VMEM = pl.BlockSpec(memory_space=pltpu.VMEM)


def inner_size(n):
    return 2 if n % 2 == 0 else 1


def remote(src, dst, send, recv, **to):
    return pltpu.make_async_remote_copy(
        src_ref=src,
        dst_ref=dst,
        send_sem=send,
        recv_sem=recv,
        device_id=to,
        device_id_type=MESH,
    )


def greet(peers):
    barrier = pltpu.get_barrier_semaphore()
    for peer in peers:
        pl.semaphore_signal(barrier, inc=1, device_id=peer, device_id_type=MESH)
    pl.semaphore_wait(barrier, len(peers))


def row_major(array):
    return with_layout_constraint(array, Layout(tuple(range(array.ndim))))


def link_cost(moved):
    return pl.CostEstimate(flops=0, bytes_accessed=moved, transcendentals=0)


def start_all(copies, sent):
    for copy in copies:
        copy.start()
        sent.append(copy)


def middle_role(d, n, pieces, rows, lag, x_refs, out_refs, acc, from_outer, from_middle, sems):
    up_send, up_recv, mid_send, mid_recv, down_send, down_recv = sems
    half = n // 2
    left = d < half
    outer, inner = (d - 1, d + 1) if left else (d + 1, d - 1)
    has_outer = 0 <= outer < n
    is_middle = d in (half - 1, half)
    to_middle = half - 1 - d if left else d - half
    each = pieces // len(x_refs)

    def term(refs, p):
        return refs[p // each].at[pl.ds(p % each * rows, rows)]

    def held(ref, p):
        return ref.at[pl.ds(p * rows, rows)]

    def hop(src, dst, send, recv, to, p):
        return remote(src, dst, send.at[p], recv.at[p], tensor=to)

    sent = []

    def gather(p):
        x, kept, came = term(x_refs, p), held(acc, p), held(from_outer, p)
        src = x
        if has_outer:
            hop(x, came, up_send, up_recv, inner, p).wait_recv()
            kept[...] = (x[...].astype(jnp.float32) + came[...].astype(jnp.float32)).astype(
                acc.dtype
            )
            src = kept
        if is_middle:
            start_all([hop(src, held(from_middle, p), mid_send, mid_recv, inner, p)], sent)
        else:
            start_all([hop(src, came, up_send, up_recv, inner, p)], sent)

    def spread_out(p):
        out, came = term(out_refs, p), held(from_middle, p)
        if is_middle:
            src = held(acc, p) if has_outer else term(x_refs, p)
            hop(src, came, mid_send, mid_recv, inner, p).wait_recv()
            out[...] = (src[...].astype(jnp.float32) + came[...].astype(jnp.float32)).astype(
                acc.dtype
            )
        else:
            hop(out, out, down_send, down_recv, inner, p).wait_recv()
        if has_outer:
            start_all([hop(out, out, down_send, down_recv, outer, p)], sent)

    lag = min(pieces, lag * (1 + 2 * to_middle)) if has_outer else pieces
    for p in range(pieces + lag):
        if p < pieces:
            gather(p)
        if p >= lag:
            spread_out(p - lag)
    for copy in sent:
        copy.wait_send()


def tensor_sum_kernel(n, count, pieces, rows, lag, *refs):
    x_refs, out_refs = refs[:count], refs[count : 2 * count]
    acc, from_outer, from_middle = refs[2 * count : 2 * count + 3]
    sems = refs[2 * count + 3 :]
    me = lax.axis_index("tensor")
    for d in range(n):

        @pl.when(me == d)
        def role():
            greet([{"tensor": at} for at in (d - 1, d + 1) if 0 <= at < n])
            middle_role(
                d, n, pieces, rows, lag, x_refs, out_refs, acc, from_outer, from_middle, sems
            )


def piece_count(rows, most):
    units = rows // ROW_TILE
    return max(p for p in range(1, most + 1) if units % p == 0)


def tensor_sum(*terms):
    n = lax.axis_size("tensor")
    if n == 1:
        return list(terms)
    count = len(terms)
    shape, dtype = terms[0].shape, terms[0].dtype
    each = piece_count(shape[0], 12)
    rows = shape[0] // each
    pieces = each * count
    sem = pltpu.SemaphoreType.DMA((pieces,))
    return pl.pallas_call(
        functools.partial(tensor_sum_kernel, n, count, pieces, rows, 2),
        out_shape=[jax.ShapeDtypeStruct(shape, dtype)] * count,
        in_specs=[VMEM] * count,
        out_specs=[VMEM] * count,
        scratch_shapes=[pltpu.VMEM((shape[0] * count, shape[1]), dtype)] * 3 + [sem] * 6,
        compiler_params=pltpu.CompilerParams(
            collective_id=0 if count == 1 else 6, has_side_effects=True
        ),
        cost_estimate=link_cost(100 * count * terms[0].size * dtype.itemsize),
        name="tensor_sum",
    )(*terms)


def opening_kernel(
    sizes,
    part_ref,
    add_ref,
    bias_ref,
    mod_ref,
    bias_all,
    held,
    ctx_send,
    ctx_recv,
    col_send,
    col_recv,
    bias_send,
    bias_recv,
):
    n_sec, n_ten, n_ctx = sizes
    sec, ten, ctx = (lax.axis_index(name) for name in ("section", "tensor", "ctx"))
    ctxs = [lax.rem(ctx + k, n_ctx) for k in range(n_ctx)]
    steps = [(a, b) for a in range(n_sec) for b in range(n_ten) if (a, b) != (0, 0)]
    places = [
        {"section": lax.rem(sec + a, n_sec), "tensor": lax.rem(ten + b, n_ten)} for a, b in steps
    ]
    greet([{"ctx": c} for c in ctxs[1:]] + places)
    sent = []

    def across(k, slot):
        return remote(
            part_ref, held.at[slot], ctx_send.at[k - 1], ctx_recv.at[k - 1], ctx=ctxs[k]
        )

    def biases(k, slot):
        return remote(
            bias_ref,
            bias_all.at[slot],
            bias_send.at[k - 1],
            bias_recv.at[k - 1],
            section=lax.rem(sec + k, n_sec),
        )

    for k in range(1, n_ctx):
        start_all([across(k, ctx)], sent)
    for k in range(1, n_sec):
        start_all([biases(k, sec)], sent)
    held[ctx] = part_ref[...]
    bias_all[sec] = bias_ref[...]
    for k in range(1, n_ctx):
        across(k, lax.rem(ctx + n_ctx - k, n_ctx)).wait_recv()
    total = add_ref[...]
    for k in range(n_ctx):
        total = total + held[k]
    mod_ref[sec, ten] = total

    def column(at, block):
        return remote(block, block, col_send.at[at], col_recv.at[at], **places[at])

    for at in range(len(steps)):
        start_all([column(at, mod_ref.at[sec, ten])], sent)
    for at, (a, b) in enumerate(steps):
        theirs = mod_ref.at[lax.rem(sec + n_sec - a, n_sec), lax.rem(ten + n_ten - b, n_ten)]
        column(at, theirs).wait_recv()
    for k in range(1, n_sec):
        biases(k, lax.rem(sec + n_sec - k, n_sec)).wait_recv()
    for copy in sent:
        copy.wait_send()


def opening(part, add, bias):
    sizes = n_sec, n_ten, n_ctx = tuple(
        lax.axis_size(name) for name in ("section", "tensor", "ctx")
    )
    dma = pltpu.SemaphoreType.DMA
    return pl.pallas_call(
        functools.partial(opening_kernel, sizes),
        out_shape=[
            jax.ShapeDtypeStruct((n_sec, n_ten) + part.shape, part.dtype),
            jax.ShapeDtypeStruct((n_sec,) + bias.shape, bias.dtype),
        ],
        in_specs=[VMEM] * 3,
        out_specs=[VMEM] * 2,
        scratch_shapes=[
            pltpu.VMEM((n_ctx,) + part.shape, part.dtype),
            dma((max(n_ctx - 1, 1),)),
            dma((max(n_ctx - 1, 1),)),
            dma((n_sec * n_ten,)),
            dma((n_sec * n_ten,)),
            dma((max(n_sec - 1, 1),)),
            dma((max(n_sec - 1, 1),)),
        ],
        compiler_params=pltpu.CompilerParams(collective_id=1, has_side_effects=True),
        cost_estimate=link_cost(40 * n_sec * n_ten * part.size * part.dtype.itemsize),
        name="opening",
    )(part, add, bias)


def group_peers(n_sec, n_ctx):
    ni = inner_size(n_ctx)
    no = n_ctx // ni
    sec, ctx = lax.axis_index("section"), lax.axis_index("ctx")
    i, o = lax.rem(ctx, ni), lax.div(ctx, ni)
    far = {
        (a, b): {"section": lax.rem(sec + a, n_sec), "ctx": lax.rem(o + b, no) * ni + i}
        for a in range(n_sec)
        for b in range(no)
        if (a, b) != (0, 0)
    }
    near = {m: {"ctx": o * ni + lax.rem(i + m, ni)} for m in range(1, ni)}
    return sec, i, o, ni, no, far, near


def spread_kernel(n_sec, n_ctx, own_ref, both_ref, own_all, both_all, *sems):
    far_send, far_recv, near_send, near_recv, own_sem = sems
    sec, i, o, ni, no, far, near = group_peers(n_sec, n_ctx)
    greet(list(far.values()) + list(near.values()))
    sent = []
    me = o * ni + i

    def far_copies(step):
        a, b = step
        at = a * no + b
        copies = []
        if a == 0:
            copies.append(
                remote(
                    own_ref, own_all.at[me], far_send.at[0, at], far_recv.at[0, at], **far[step]
                )
            )
        copies.append(
            remote(
                both_ref, both_all.at[sec, me], far_send.at[1, at], far_recv.at[1, at], **far[step]
            )
        )
        return copies

    def near_copies(m, a, b, own_src, both_src, s_at, c_at):
        at = a * no + b
        copies = []
        if a == 0:
            copies.append(
                remote(
                    own_src,
                    own_all.at[c_at],
                    near_send.at[0, m - 1, at],
                    near_recv.at[0, m - 1, at],
                    **near[m],
                )
            )
        copies.append(
            remote(
                both_src,
                both_all.at[s_at, c_at],
                near_send.at[1, m - 1, at],
                near_recv.at[1, m - 1, at],
                **near[m],
            )
        )
        return copies

    for step in far:
        start_all(far_copies(step), sent)
    for m in near:
        start_all(near_copies(m, 0, 0, own_ref, both_ref, sec, me), sent)
    keep = [
        pltpu.make_async_copy(own_ref, own_all.at[me], own_sem.at[0]),
        pltpu.make_async_copy(both_ref, both_all.at[sec, me], own_sem.at[1]),
    ]
    for copy in keep:
        copy.start()
    for step in far:
        a, b = step
        for copy in far_copies(step):
            copy.wait_recv()
        s_at = lax.rem(sec + n_sec - a, n_sec)
        c_at = lax.rem(o + no - b, no) * ni + i
        for m in near:
            start_all(
                near_copies(m, a, b, own_all.at[c_at], both_all.at[s_at, c_at], s_at, c_at), sent
            )
    for m in near:
        for a in range(n_sec):
            for b in range(no):
                s_at = lax.rem(sec + n_sec - a, n_sec)
                c_at = lax.rem(o + no - b, no) * ni + lax.rem(i + ni - m, ni)
                for copy in near_copies(
                    m, a, b, own_all.at[c_at], both_all.at[s_at, c_at], s_at, c_at
                ):
                    copy.wait_recv()
    for copy in keep:
        copy.wait()
    for copy in sent:
        copy.wait_send()


def spread(own, both):
    n_sec, n_ctx = lax.axis_size("section"), lax.axis_size("ctx")
    ni = inner_size(n_ctx)
    no = n_ctx // ni
    dma = pltpu.SemaphoreType.DMA
    return pl.pallas_call(
        functools.partial(spread_kernel, n_sec, n_ctx),
        out_shape=[
            jax.ShapeDtypeStruct((n_ctx,) + own.shape, own.dtype),
            jax.ShapeDtypeStruct((n_sec, n_ctx) + both.shape, both.dtype),
        ],
        in_specs=[VMEM, VMEM],
        out_specs=[VMEM, VMEM],
        scratch_shapes=[
            dma((2, n_sec * no)),
            dma((2, n_sec * no)),
            dma((2, ni, n_sec * no)),
            dma((2, ni, n_sec * no)),
            dma((2,)),
        ],
        compiler_params=pltpu.CompilerParams(collective_id=2, has_side_effects=True),
        name="spread",
    )(own, both)


def owner_kernel(n_sec, n_ctx, own_ref, both_ref, own_out, both_out, *refs):
    own_pair, both_pair, own_far, both_far = refs[:4]
    far_send, far_recv, near_send, near_recv = refs[4:]
    sec, i, o, ni, no, far, near = group_peers(n_sec, n_ctx)
    greet(list(far.values()) + list(near.values()))
    sent = []

    def near_copies(m, a, b):
        to = lax.rem(i + m, ni)
        s_at, o_at = lax.rem(sec + a, n_sec), lax.rem(o + b, no)
        at = a * no + b
        copies = []
        if a == 0:
            copies.append(
                remote(
                    own_ref.at[o_at * ni + to],
                    own_pair.at[m - 1, b],
                    near_send.at[0, m - 1, at],
                    near_recv.at[0, m - 1, at],
                    **near[m],
                )
            )
        copies.append(
            remote(
                both_ref.at[s_at, o_at * ni + to],
                both_pair.at[m - 1, at],
                near_send.at[1, m - 1, at],
                near_recv.at[1, m - 1, at],
                **near[m],
            )
        )
        return copies

    order = list(far) + [(0, 0)]
    for step in order:
        for m in near:
            start_all(near_copies(m, *step), sent)

    def far_copies(a, b):
        at = a * no + b
        copies = []
        if a == 0:
            copies.append(
                remote(
                    own_pair.at[ni - 1, b],
                    own_far.at[b],
                    far_send.at[0, at],
                    far_recv.at[0, at],
                    **far[(a, b)],
                )
            )
        copies.append(
            remote(
                both_pair.at[ni - 1, at],
                both_far.at[at],
                far_send.at[1, at],
                far_recv.at[1, at],
                **far[(a, b)],
            )
        )
        return copies

    for a, b in order:
        s_at, c_at = lax.rem(sec + a, n_sec), lax.rem(o + b, no) * ni + i
        at = a * no + b
        for m in near:
            for copy in near_copies(m, a, b):
                copy.wait_recv()
        total_both = both_ref[s_at, c_at].astype(jnp.float32)
        for m in near:
            total_both = total_both + both_pair[m - 1, at].astype(jnp.float32)
        total_own = None
        if a == 0:
            total_own = own_ref[c_at].astype(jnp.float32)
            for m in near:
                total_own = total_own + own_pair[m - 1, b].astype(jnp.float32)
        if (a, b) == (0, 0):
            own_out[...] = total_own
            both_out[...] = total_both
        else:
            if a == 0:
                own_pair[ni - 1, b] = total_own.astype(own_pair.dtype)
            both_pair[ni - 1, at] = total_both.astype(both_pair.dtype)
            start_all(far_copies(a, b), sent)
    for a, b in far:
        for copy in far_copies(a, b):
            copy.wait_recv()
        if a == 0:
            own_out[...] += own_far[b].astype(jnp.float32)
        both_out[...] += both_far[a * no + b].astype(jnp.float32)
    for copy in sent:
        copy.wait_send()


def owner_sum(own, both):
    n_sec, n_ctx = lax.axis_size("section"), lax.axis_size("ctx")
    ni = inner_size(n_ctx)
    no = n_ctx // ni
    dma = pltpu.SemaphoreType.DMA
    own_shape, both_shape = own.shape[1:], both.shape[2:]
    return pl.pallas_call(
        functools.partial(owner_kernel, n_sec, n_ctx),
        out_shape=[
            jax.ShapeDtypeStruct(own_shape, jnp.float32),
            jax.ShapeDtypeStruct(both_shape, jnp.float32),
        ],
        in_specs=[VMEM, VMEM],
        out_specs=[VMEM, VMEM],
        scratch_shapes=[
            pltpu.VMEM((ni, no) + own_shape, own.dtype),
            pltpu.VMEM((ni, n_sec * no) + both_shape, both.dtype),
            pltpu.VMEM((no,) + own_shape, own.dtype),
            pltpu.VMEM((n_sec * no,) + both_shape, both.dtype),
            dma((2, n_sec * no)),
            dma((2, n_sec * no)),
            dma((2, ni, n_sec * no)),
            dma((2, ni, n_sec * no)),
        ],
        compiler_params=pltpu.CompilerParams(collective_id=3, has_side_effects=True),
        name="owner_sum",
    )(own, both)


def small_kernel(axes, sizes, x_ref, out_ref, held, send, recv):
    at = [lax.axis_index(name) for name in axes]
    steps = [(a, b) for a in range(sizes[0]) for b in range(sizes[1])]
    places = [
        [lax.rem(here + sign * step + size, size) for here, step, size in zip(at, pair, sizes)]
        for sign in (1, -1)
        for pair in steps
    ]
    to, source = places[: len(steps)], places[len(steps) :]
    where = [dict(zip(axes, place)) for place in to]
    greet(where[1:])

    def block(place):
        return place[0] if x_ref.shape[0] > 1 else 0

    def copy(k, slot):
        return remote(
            x_ref.at[block(to[k])],
            held.at[slot[0] * sizes[1] + slot[1]],
            send.at[k - 1],
            recv.at[k - 1],
            **where[k],
        )

    copies = [copy(k, at) for k in range(1, len(steps))]
    for started in copies:
        started.start()
    held[at[0] * sizes[1] + at[1]] = x_ref[block(at)]
    for k in range(1, len(steps)):
        copy(k, source[k]).wait_recv()
    total = held[0]
    for k in range(1, len(steps)):
        total = total + held[k]
    out_ref[...] = total
    for started in copies:
        started.wait_send()


def small_sum(x, axes, collective_id):
    sizes = tuple(lax.axis_size(name) for name in axes)
    n = sizes[0] * sizes[1]
    dma = pltpu.SemaphoreType.DMA((max(n - 1, 1),))
    return pl.pallas_call(
        functools.partial(small_kernel, axes, sizes),
        out_shape=jax.ShapeDtypeStruct(x.shape[1:], x.dtype),
        in_specs=[VMEM],
        out_specs=VMEM,
        scratch_shapes=[pltpu.VMEM((n,) + x.shape[1:], x.dtype), dma, dma],
        compiler_params=pltpu.CompilerParams(collective_id=collective_id, has_side_effects=True),
        cost_estimate=link_cost(100 * n * x[0].size * x.dtype.itemsize),
        name="small_sum",
    )(x)


def packed(pieces, width):
    flat = jnp.concatenate([p.reshape(-1) for p in pieces])
    rows = -(-flat.shape[0] // width)
    rows = -(-rows // 8) * 8
    return jnp.pad(flat, (0, rows * width - flat.shape[0])).reshape(rows, width)


def compact(array):
    return packed([array], -(-array.size // 8))


def in_rows(pieces):
    width = max(p.shape[-1] for p in pieces)
    rows = [jnp.pad(p, ((0, 0), (0, width - p.shape[-1]))) for p in pieces]
    block = jnp.concatenate(rows)
    return jnp.pad(block, ((0, -block.shape[0] % 8), (0, 0)))


def from_rows(block, shapes):
    at, out = 0, []
    for rows, width in shapes:
        out.append(block[at : at + rows, :width])
        at += rows
    return out


def unpacked(block, shapes):
    flat, at, out = block.reshape(-1), 0, []
    for shape in shapes:
        size = math.prod(shape)
        out.append(flat[at : at + size].reshape(shape))
        at += size
    return out


def layer_norm(values):
    centre = jnp.mean(values, axis=-1, keepdims=True)
    centred = values - centre
    variance = jnp.mean(centred * centred, axis=-1, keepdims=True)
    inverse = lax.rsqrt(variance + EPSILON)
    return centred * inverse


def norm_back_kernel(scale_at, gate_at, up_ref, x_ref, base_ref, mod_ref, *refs):
    x = x_ref[...].astype(jnp.float32)
    centred = x - jnp.mean(x, axis=-1, keepdims=True)
    inverse = lax.rsqrt(jnp.mean(centred * centred, axis=-1, keepdims=True) + EPSILON)
    normed = centred * inverse
    upstream = up_ref[...].astype(jnp.float32)
    scaled = upstream * (1.0 + mod_ref[0, scale_at : scale_at + 1, :])
    mean_grad = jnp.mean(scaled, axis=-1, keepdims=True)
    mean_cross = jnp.mean(scaled * normed, axis=-1, keepdims=True)
    grad = base_ref[...] + inverse * (scaled - mean_grad - normed * mean_cross)
    if gate_at is None:
        grad_ref, sums_ref = refs
    else:
        term_ref, bias_ref, gate_ref, grad_ref, gated_ref, sums_ref = refs
        gated = grad * gate_ref[0, gate_at : gate_at + 1, :]
        gated_ref[...] = gated.astype(gated_ref.dtype)
        term = term_ref[...].astype(jnp.float32) + bias_ref[...]
        sums_ref[0, 2:3, :] = jnp.sum(grad * term, axis=0, keepdims=True)
        sums_ref[0, 3:4, :] = jnp.sum(gated, axis=0, keepdims=True)
    grad_ref[...] = grad
    sums_ref[0, 0:1, :] = jnp.sum(upstream, axis=0, keepdims=True)
    sums_ref[0, 1:2, :] = jnp.sum(upstream * normed, axis=0, keepdims=True)


def norm_back(rows, upstream, x, base, mods, scale_at, gate=None):
    part, width = rows.part, rows.width
    runs = rows.rows // part
    tile = pl.BlockSpec((part, width), lambda at: (at, 0))
    per_run = pl.BlockSpec((1, mods.shape[1], width), lambda at: (at, 0, 0))
    sums = pl.BlockSpec((1, 8, width), lambda at: (at, 0, 0))
    args, in_specs = [upstream, x, base, mods], [tile] * 3 + [per_run]
    shape = jax.ShapeDtypeStruct((rows.rows, width), jnp.float32)
    out_shape, out_specs = [shape], [tile]
    if gate:
        term, bias, gate_mods, gate_at = gate
        args += [term, bias[None], gate_mods]
        in_specs += [tile, pl.BlockSpec((1, width), lambda at: (0, 0)), per_run]
        out_shape.append(jax.ShapeDtypeStruct((rows.rows, width), jnp.bfloat16))
        out_specs.append(tile)
    return pl.pallas_call(
        functools.partial(norm_back_kernel, scale_at, gate_at if gate else None),
        grid=(runs,),
        out_shape=out_shape + [jax.ShapeDtypeStruct((runs, 8, width), jnp.float32)],
        in_specs=in_specs,
        out_specs=out_specs + [sums],
        compiler_params=pltpu.CompilerParams(vmem_limit_bytes=32 * 1024 * 1024),
        cost_estimate=pl.CostEstimate(
            flops=30 * rows.rows * width,
            bytes_accessed=18 * rows.rows * width,
            transcendentals=rows.rows,
        ),
        name="norm_back",
    )(*args)


def gelu_back(pre_act, upstream):
    unused_out, pullback = jax.vjp(
        lambda pre_value: jax.nn.gelu(pre_value, approximate=True), pre_act
    )
    return pullback(upstream)[0]


def heads(array):
    cols = array.shape[-2]
    return array.reshape(*array.shape[:-2], cols // HD, HD, array.shape[-1])


def score_columns(queries, keys):
    softmax_scale = 1.0 / math.sqrt(HD)
    return (
        jnp.einsum(
            "nhdk,hdq->hnkq", heads(keys), heads(queries), preferred_element_type=jnp.float32
        )
        * softmax_scale
    )


def attend(queries, keys, values):
    scores = score_columns(queries, keys)
    row_peak = jnp.max(scores, axis=(1, 2), keepdims=True)
    log_total = row_peak + jnp.log(jnp.sum(jnp.exp(scores - row_peak), axis=(1, 2), keepdims=True))
    prob_bf = jnp.exp(scores - log_total).astype(jnp.bfloat16)
    context = jnp.einsum(
        "nhdk,hnkq->hdq", heads(values), prob_bf, preferred_element_type=jnp.float32
    )
    return context.astype(jnp.bfloat16).reshape(queries.shape), log_total


def attention_grads(queries, keys, values, log_total, context, context_grad):
    softmax_scale = 1.0 / math.sqrt(HD)
    query_heads, grad_heads = heads(queries), heads(context_grad)
    delta = jnp.sum(
        grad_heads.astype(jnp.float32) * heads(context).astype(jnp.float32), axis=1
    )[:, None, None, :]
    prob_full = jnp.exp(score_columns(queries, keys) - log_total)
    prob_bf = prob_full.astype(jnp.bfloat16)
    prob_grad = jnp.einsum(
        "nhdk,hdq->hnkq", heads(values), grad_heads, preferred_element_type=jnp.float32
    )
    score_grad = (prob_full * (prob_grad - delta)).astype(jnp.bfloat16)
    query_grad = (
        jnp.einsum(
            "nhdk,hnkq->hdq", heads(keys), score_grad, preferred_element_type=jnp.float32
        )
        * softmax_scale
    ).reshape(queries.shape)
    key_part = (
        jnp.einsum("hnkq,hdq->nhdk", score_grad, query_heads, preferred_element_type=jnp.float32)
        * softmax_scale
    ).reshape(keys.shape)
    value_part = jnp.einsum(
        "hnkq,hdq->nhdk", prob_bf, grad_heads, preferred_element_type=jnp.float32
    ).reshape(values.shape)
    both = jnp.concatenate(
        [key_part.astype(jnp.bfloat16), value_part.astype(jnp.bfloat16)], axis=1
    )
    return query_grad, both


def contract(left, right, left_dim, right_dim):
    return lax.dot_general(
        left, right, (((left_dim,), (right_dim,)), ((), ())), preferred_element_type=jnp.float32
    )


class Rows:
    def __init__(self, latents, section):
        n_sec = lax.axis_size("section")
        self.n_sec = n_sec
        total, self.tokens, self.width = latents.shape
        self.section = section
        self.full = total // n_sec
        self.rest = total - self.full * n_sec
        self.part = self.tokens // n_sec
        self.own_rows = self.full * self.tokens
        self.both_rows = self.rest * self.part
        self.rows = self.own_rows + self.both_rows

    def take(self, array):
        own = lax.dynamic_slice_in_dim(array, self.section * self.full, self.full, 0)
        both = lax.dynamic_slice_in_dim(
            array[self.full * self.n_sec :], self.section * self.part, self.part, 1
        )
        return jnp.concatenate(
            [own.reshape(self.own_rows, -1), both.reshape(self.both_rows, -1)], axis=0
        )

    def split(self, array):
        return (
            array[: self.own_rows].reshape(self.full, self.tokens, -1),
            array[self.own_rows :].reshape(self.rest, self.part, -1),
        )

    def spans(self):
        out = [(at * self.tokens, self.tokens) for at in range(self.full)]
        return out + [
            (self.own_rows + at * self.part, self.part) for at in range(self.rest)
        ]

    def columns(self, array):
        return [array[:, start : start + size] for start, size in self.spans()]

    def mods(self, modulation):
        own = lax.dynamic_slice_in_dim(modulation, self.section * self.full, self.full, 0)
        return jnp.concatenate([own, modulation[self.full * self.n_sec :]], axis=0)

    def by_run(self, mods):
        runs = self.tokens // self.part
        return jnp.concatenate(
            [mods[at : at + 1] for at in range(self.full) for _ in range(runs)] + [mods[self.full :]]
        )

    def wide(self, pieces):
        row = lax.broadcasted_iota(jnp.int32, (self.rows, 1), 0)
        out = pieces[-1][None, :]
        for (start, size), piece in reversed(list(zip(self.spans(), pieces))[:-1]):
            out = jnp.where(row < start + size, piece[None, :], out)
        return out

    def sums(self, array):
        return jnp.sum(array.reshape(-1, self.part, self.width), axis=1)

    def placed(self, sums):
        runs = self.tokens // self.part
        own = sums[: self.full * runs].reshape(self.full, runs, -1).sum(axis=1)
        mine = [
            jnp.where(self.section == at // self.full, own[at % self.full], 0.0)
            for at in range(self.full * self.n_sec)
        ]
        both = [sums[self.full * runs + at] for at in range(self.rest)]
        return jnp.stack(mine + both)

    def assembled(self, per_block, received):
        own = per_block[-1]
        for b in range(self.n_sec - 1):
            own = jnp.where(self.section == b, per_block[b], own)
        others = []
        for k in range(1, self.n_sec):
            rows = received[-1][k - 1]
            for b in range(self.n_sec - 1):
                rows = jnp.where(self.section == b, received[b][k - 1], rows)
            others.append(rows)
        whole, shared = [], []
        for source in range(self.n_sec):
            rows = own
            for k, other in enumerate(others, 1):
                rows = jnp.where(lax.rem(self.section + k, self.n_sec) == source, other, rows)
            first, both = self.split(rows)
            whole.append(first)
            shared.append(both)
        return jnp.concatenate(whole + [jnp.concatenate(shared, axis=1)], axis=0)


def gathered(key_value, rows):
    spans = rows.spans()
    cols = [key_value[:, start : start + size] for start, size in spans]
    own = jnp.concatenate(cols[: rows.full], axis=0)
    both = jnp.concatenate(cols[rows.full :], axis=0)
    own_all, both_all = spread(own, both)
    both_all = both_all.reshape(-1, *both.shape)
    high = key_value.shape[0]
    return [own_all[:, at * high : (at + 1) * high] for at in range(rows.full)] + [
        both_all[:, at * high : (at + 1) * high] for at in range(rows.rest)
    ]


def returned(parts, rows):
    high = parts[0].shape[1]
    own = jnp.concatenate(parts[: rows.full], axis=1)
    both = jnp.concatenate(parts[rows.full :], axis=1)
    own, both = owner_sum(own, both.reshape(rows.n_sec, -1, *both.shape[1:]))
    return jnp.concatenate(
        [own[at * high : (at + 1) * high] for at in range(rows.full)]
        + [both[at * high : (at + 1) * high] for at in range(rows.rest)],
        axis=1,
    )


def forward_block(rows, block_in, mods, w_qkv, biases, prepare, mlp_weights, last):
    b_qv, b_out, b_fc1, b_fc2 = biases
    local_cols = w_qkv.shape[0] // 3
    shift_a, scale_a, gate_a, shift_m, scale_m, gate_m = (
        rows.wide([mods[at, k] for at in range(mods.shape[0])]) for k in range(6)
    )
    residual = block_in.astype(jnp.float32)
    normed_a = layer_norm(residual)
    attn_in = (normed_a * (1.0 + scale_a) + shift_a).astype(jnp.bfloat16)
    projected = contract(w_qkv, attn_in, 1, 1)
    bias = jnp.concatenate([b_qv[0], jnp.zeros_like(b_qv[0]), b_qv[1]])
    projected = (projected + bias[:, None]).astype(jnp.bfloat16)
    queries = rows.columns(projected[:local_cols])
    keys_values, w_out, sends = prepare(gathered(projected[local_cols:], rows))
    attended = [
        attend(q, kv[:, :local_cols], kv[:, local_cols:])
        for q, kv in zip(queries, keys_values)
    ]
    context = row_major(jnp.concatenate([row_major(c) for c, _ in attended], axis=1))
    attn_term = contract(context, w_out, 0, 0)
    (attn_sum,), moved = beside(tensor_sum, [attn_term.astype(jnp.bfloat16)], sends)
    w_fc1, w_fc2 = mlp_weights(moved)
    attn_out = attn_sum.astype(jnp.float32) + b_out
    middle = residual + gate_a * attn_out
    normed_m = layer_norm(middle)
    mlp_in = (normed_m * (1.0 + scale_m) + shift_m).astype(jnp.bfloat16)
    pre_act = jnp.dot(mlp_in, w_fc1, preferred_element_type=jnp.float32) + b_fc1
    hidden = jax.nn.gelu(pre_act, approximate=True).astype(jnp.bfloat16)
    mlp_term = jnp.dot(hidden, w_fc2, preferred_element_type=jnp.float32).astype(jnp.bfloat16)

    def close(mlp_sum):
        mlp_out = mlp_sum.astype(jnp.float32) + b_fc2
        return mlp_out, (middle + gate_m * mlp_out).astype(jnp.bfloat16)

    block_res, mlp_sum = None, None
    if not last:
        (mlp_sum,) = tensor_sum(mlp_term)
        block_res = close(mlp_sum)[1]
    stored = (
        block_in,
        attn_in,
        queries,
        keys_values,
        [log_total for _, log_total in attended],
        context,
        attn_sum,
        middle,
        mlp_in,
        pre_act,
        hidden,
        mlp_sum,
    )
    return block_res, stored, moved, (mlp_term, close) if last else None


def backward_block(
    rows, upstream, gated, stored, run_mods, weights, block, firsts, seconds, pending, b_out, below
):
    w_qkv, w_out, w_fc1, w_fc2 = weights
    (
        block_in,
        attn_in,
        queries,
        keys_values,
        log_totals,
        context,
        attn_sum,
        middle,
        mlp_in,
        pre_act,
        hidden,
        mlp_sum,
    ) = stored
    mlp_grad_b, gate_m_grad, grad_b2 = gated
    local_cols = w_qkv.shape[0] // 3
    pre_grad = gelu_back(pre_act, jnp.dot(mlp_grad_b, w_fc2.T, preferred_element_type=jnp.float32))
    pre_grad_b = pre_grad.astype(jnp.bfloat16)
    grad_b1 = jnp.sum(pre_grad, axis=0)
    mlp_pair = inner_pair(
        [contract(mlp_grad_b, hidden, 0, 0), contract(mlp_in, pre_grad_b, 0, 0)]
    )
    mlp_term = jnp.dot(pre_grad_b, w_fc1.T, preferred_element_type=jnp.float32)
    terms = [mlp_term.astype(jnp.bfloat16)]
    if pending:
        terms.append(pending[0])
    outer = outer_sends(mlp_pair)
    (mlp_in_grad, *sums), moved = beside(tensor_sum, terms, outer + firsts)
    block_res = None
    if pending:
        mlp_out, block_res = pending[1](sums[0])
        gate_m_grad = rows.sums(upstream * mlp_out)
    first_moved = moved[len(outer) :]
    mlp_share = outer_total(mlp_pair, moved[: len(outer)])
    middle_grad, attn_grad_b, m_sums = norm_back(
        rows, mlp_in_grad, middle, upstream, run_mods, 4, (attn_sum, b_out, run_mods, 2)
    )
    grad_bo = jnp.sum(m_sums[:, 3], axis=0)
    context_grad = contract(w_out, attn_grad_b, 1, 1).astype(jnp.bfloat16)
    query_grads, key_value_parts = zip(
        *(
            attention_grads(q, kv[:, :local_cols], kv[:, local_cols:], log_total, c, cg)
            for q, kv, log_total, c, cg in zip(
                queries, keys_values, log_totals, rows.columns(context), rows.columns(context_grad)
            )
        )
    )
    query_grad = row_major(jnp.concatenate([row_major(g) for g in query_grads], axis=1))
    key_value_grad = returned(key_value_parts, rows)
    grad_bqv = jnp.stack(
        [jnp.sum(query_grad, axis=1), jnp.sum(key_value_grad[local_cols:], axis=1)]
    )
    qkv_grad_b = jnp.concatenate([query_grad, key_value_grad], axis=0).astype(jnp.bfloat16)
    qkv_rows, context_rows = row_major(row_major(qkv_grad_b).T), row_major(row_major(context).T)
    attn_term = contract(qkv_rows, w_qkv, 1, 0)
    attn_pairs = [
        inner_pair([contract(attn_in, qkv_rows, 0, 0)]),
        inner_pair([contract(attn_grad_b, context_rows, 0, 0)]),
    ]
    outers = [outer_sends(pair) for pair in attn_pairs]
    across = block_sends(mlp_share, block)
    sends = [*outers, across, seconds]
    ((attn_in_grad,), moved) = beside(
        tensor_sum, [attn_term.astype(jnp.bfloat16)], [send for part in sends for send in part]
    )
    came = []
    for part in sends:
        came.append(moved[: len(part)])
        moved = moved[len(part) :]
    attn_shares = [outer_total(pair, part) for pair, part in zip(attn_pairs, came)]
    mlp_share = block_total(mlp_share, came[-2])
    second_moved = came[-1]
    attn_in_grad, attn_values = lax.optimization_barrier(
        (attn_in_grad, [share.astype(jnp.bfloat16) for share in attn_shares])
    )
    input_grad, *gated, a_sums = norm_back(
        rows, attn_in_grad, block_in, middle_grad, run_mods, 1, below
    )
    if below:
        gated += [a_sums[:, 2], jnp.sum(a_sums[:, 3], axis=0)]
    mod_grad = jnp.concatenate(
        [a_sums[:, 0], a_sums[:, 1], m_sums[:, 2], m_sums[:, 0], m_sums[:, 1], gate_m_grad], axis=1
    )
    return (
        input_grad,
        gated,
        mod_grad,
        (grad_bqv, grad_bo, grad_b1, grad_b2),
        (mlp_share, *attn_shares),
        attn_values,
        block_res,
        first_moved,
        second_moved,
    )


def to_inner(value, by):
    n = lax.axis_size("ctx")
    ni = inner_size(n)
    return lax.ppermute(value, "ctx", [(a, a // ni * ni + (a + by) % ni) for a in range(n)])


def to_outer(value, by):
    n = lax.axis_size("ctx")
    ni = inner_size(n)
    return lax.ppermute(value, "ctx", [(a, (a + by * ni) % n) for a in range(n)])


def to_section(value, by):
    n = lax.axis_size("section")
    return lax.ppermute(value, "section", [(a, (a + by) % n) for a in range(n)])


def to_block(value, block, by):
    n = lax.axis_size("section")
    return lax.ppermute(value, "section", [((block + by) % n, block)])


def ctx_place():
    n = lax.axis_size("ctx")
    ni = inner_size(n)
    at = lax.axis_index("ctx")
    return n // ni, ni, lax.div(at, ni), lax.rem(at, ni)


def beside(kernel, args, sends):
    args, values = lax.optimization_barrier((args, [value for value, _ in sends]))
    moved = [move(value) for value, (_, move) in zip(values, sends)]
    return lax.optimization_barrier((kernel(*args), moved))


def half_of(weights):
    _, ni, _, i = ctx_place()
    sizes = [w.shape[0] // ni for w in weights]
    return jnp.concatenate(
        [lax.dynamic_slice_in_dim(w, i * size, size, 0) for w, size in zip(weights, sizes)]
    )


def joined(own, passed, weights):
    _, ni, _, i = ctx_place()
    found, start = [], 0
    for w in weights:
        size = w.shape[0] // ni
        parts = [piece[start : start + size] for piece in [own] + passed]
        start += size
        ordered = []
        for at in range(ni):
            piece = parts[0]
            for m in range(1, ni):
                piece = jnp.where(lax.rem(i + ni - m, ni) == at, parts[m], piece)
            ordered.append(piece)
        found.append(jnp.concatenate(ordered))
    return found


def chosen_blocks(weights, others):
    n_sec = lax.axis_size("section")
    section = lax.axis_index("section")
    blocks = []
    for b in range(n_sec):
        chosen = list(weights)
        for k, found in enumerate(others, 1):
            is_source = lax.rem(section + n_sec - k, n_sec) == b
            chosen = [jnp.where(is_source, new, old) for new, old in zip(found, chosen)]
        blocks.append(chosen)
    return blocks


def fetched(weights):
    n_sec = lax.axis_size("section")
    groups = [
        [at for at, w in enumerate(weights) if w.shape[1] == width]
        for width in sorted({w.shape[1] for w in weights})
    ]
    halves = [half_of([weights[at] for at in group]) for group in groups]
    return groups, [[to_section(half, k) for k in range(1, n_sec)] for half in halves]


def passing(fetch):
    _, ni, _, _ = ctx_place()
    return [
        (half, functools.partial(to_inner, by=m))
        for of_group in fetch[1]
        for half in of_group
        for m in range(1, ni)
    ]


def every_block(weights, fetch, passed):
    _, ni, _, _ = ctx_place()
    n_sec = lax.axis_size("section")
    others = [[None] * len(weights) for _ in range(n_sec - 1)]
    passed = list(passed)
    for group, of_group in zip(*fetch):
        for k, half in enumerate(of_group):
            rest = [passed.pop(0) for _ in range(1, ni)]
            for at, whole in zip(group, joined(half, rest, [weights[at] for at in group])):
                others[k][at] = whole
    return chosen_blocks(weights, others)


def inner_pair(terms):
    no, ni, _, i = ctx_place()
    terms = [
        row_major(t.astype(jnp.bfloat16)).reshape(no, ni, -1, t.shape[-1]) for t in terms
    ]

    def inner(at):
        return row_major(
            jnp.concatenate(
                [lax.dynamic_index_in_dim(t, at, 1, keepdims=False) for t in terms], axis=1
            )
        )

    pair = inner(i).astype(jnp.float32)
    for m in range(1, ni):
        pair = pair + to_inner(inner(lax.rem(i + m, ni)), m).astype(jnp.float32)
    return pair.astype(jnp.bfloat16)


def outer_sends(pair):
    no, _, o, _ = ctx_place()
    return [
        (
            lax.dynamic_index_in_dim(pair, lax.rem(o + m, no), 0, keepdims=False),
            functools.partial(to_outer, by=m),
        )
        for m in range(1, no)
    ]


def outer_total(pair, moved):
    _, _, o, _ = ctx_place()
    total = lax.dynamic_index_in_dim(pair, o, 0, keepdims=False).astype(jnp.float32)
    for piece in moved:
        total = total + piece.astype(jnp.float32)
    return total


def block_sends(value, block):
    value = value.astype(jnp.bfloat16)
    return [
        (value, functools.partial(to_block, block=block, by=k))
        for k in range(1, lax.axis_size("section"))
    ]


def block_total(own, moved):
    for piece in moved:
        own = own + piece.astype(jnp.float32)
    return own


def local(
    latents,
    condition,
    cotangent,
    w_ada,
    b_ada,
    w_qkv,
    b_qv,
    w_out,
    b_out,
    w_fc1,
    b_fc1,
    w_fc2,
    b_fc2,
):
    section = lax.axis_index("section")
    n_sec = lax.axis_size("section")
    latent_total, token_count, width = latents.shape
    width_cols = b_ada.shape[-1]
    local_cols = w_qkv.shape[-1]
    rows = Rows(latents, section)
    cond_act = jax.nn.silu(condition).astype(jnp.bfloat16)
    mod_part = jnp.dot(cond_act, w_ada[0], preferred_element_type=jnp.float32)
    bias_shapes = [b_qv.shape[1:], b_out.shape[1:], b_fc1.shape[1:], b_fc2.shape[1:]]
    bias_flat = jnp.concatenate([b.reshape(-1) for b in (b_qv, b_out, b_fc1, b_fc2)])
    qkv_weights = [row_major(jnp.transpose(w_qkv[0], (1, 2, 0)).reshape(3 * local_cols, width))]
    qkv_fetch = fetched(qkv_weights)
    mod_all, bias_all = opening(
        compact(mod_part),
        compact(jnp.broadcast_to(b_ada, (latent_total, width_cols))),
        compact(bias_flat),
    )
    mod_all, fc1_weights = lax.optimization_barrier((mod_all, [w_fc1[0]]))
    fc1_fetch = fetched(fc1_weights)
    qkv_blocks = every_block(
        qkv_weights, qkv_fetch, [move(half) for half, move in passing(qkv_fetch)]
    )
    tensor = lax.axis_index("tensor")
    columns = mod_all.reshape(n_sec, -1, mod_all.shape[-2] * mod_all.shape[-1])
    columns = columns[..., : latent_total * width_cols]
    columns = columns.reshape(n_sec, -1, latent_total, width_cols)
    modulation = jnp.swapaxes(columns, 1, 2).reshape(n_sec, latent_total, 6, width)
    biases, mods = [], []
    for b in range(n_sec):
        biases.append(unpacked(bias_all[b], bias_shapes))
        mods.append(rows.mods(modulation[b]))
    residual = rows.take(latents)
    outs, out_moved, kept, out_blocks, mlp_blocks, pending = [], [], [], [], [], None
    for b in range(n_sec):
        if b == 0:
            late = []

            def prepare(keys_values):
                keys_values, weights = lax.optimization_barrier(
                    (keys_values, [w_out[0], w_fc2[0]])
                )
                for weight in weights:
                    late.append(([weight], fetched([weight])))
                weights, fetch = late[0]
                out_blocks.extend(
                    every_block(weights, fetch, [move(half) for half, move in passing(fetch)])
                )
                return keys_values, out_blocks[0][0], passing(fc1_fetch)

            def finish(moved):
                firsts = every_block(fc1_weights, fc1_fetch, moved)
                weights, fetch = late[1]
                seconds = every_block(
                    weights, fetch, [move(half) for half, move in passing(fetch)]
                )
                mlp_blocks.extend([*one, *two] for one, two in zip(firsts, seconds))
                return mlp_blocks[0]

        else:
            sends = block_sends(outs[-1], b - 1)

            def prepare(keys_values, sends=sends, b=b):
                return keys_values, out_blocks[b][0], sends

            def finish(moved, b=b):
                return mlp_blocks[b]

        residual, stored, moved, pending = forward_block(
            rows,
            residual,
            mods[b],
            qkv_blocks[b][0],
            biases[b],
            prepare,
            finish,
            b == n_sec - 1,
        )
        if b:
            out_moved.append(moved)
        outs.append(residual)
        kept.append(stored)
    upstream = rows.take(cotangent).astype(jnp.float32)
    run_mods = [rows.by_run(block_mods) for block_mods in mods]
    top_grad = upstream * rows.wide([mods[-1][at, 5] for at in range(mods[-1].shape[0])])
    gated = (top_grad.astype(jnp.bfloat16), None, jnp.sum(top_grad, axis=0))
    in_grads, in_moved, small, shares = ([None] * n_sec for _ in range(4))
    out_moved.append([])
    firsts, seconds = [[], []], []
    for b in reversed(range(n_sec)):
        below = (kept[b - 1][-1], biases[b - 1][3], run_mods[b - 1], 5) if b else None
        (
            upstream,
            gated,
            mod_grad,
            bias_grads,
            shares[b],
            attn_values,
            block_res,
            first_moved,
            second_moved,
        ) = (
            backward_block(
                rows,
                upstream,
                gated,
                kept[b],
                run_mods[b],
                (*qkv_blocks[b], *out_blocks[b], *mlp_blocks[b]),
                b,
                [send for part in firsts for send in part],
                seconds,
                pending if b == n_sec - 1 else None,
                biases[b][1],
                below,
            )
        )
        if b == n_sec - 1:
            outs[b] = block_res
        else:
            at = 0
            for which in (1, 2):
                part = first_moved[at : at + n_sec - 1]
                at += n_sec - 1
                shares[b + 1][which] = block_total(shares[b + 1][which], part)
            if b == n_sec - 2:
                out_moved[-1] = first_moved[at:]
            in_moved[b + 1] = second_moved
        shares[b] = list(shares[b])
        in_grads[b] = upstream.astype(jnp.bfloat16)
        cols = mod_grad[:, :width_cols]
        for t in range(1, lax.axis_size("tensor")):
            cols = jnp.where(tensor == t, mod_grad[:, t * width_cols : (t + 1) * width_cols], cols)
        small[b] = in_rows(
            [rows.placed(cols), *(grad.reshape(-1, grad.shape[-1]) for grad in bias_grads)]
        )
        firsts = [block_sends(value, b) for value in attn_values]
        if b == n_sec - 1:
            firsts.append(block_sends(outs[b], b))
        seconds = block_sends(in_grads[b], b)
    def mine(which):
        out = shares[-1][which]
        for b in range(n_sec - 1):
            out = jnp.where(section == b, shares[b][which], out)
        return out

    small_in = jnp.stack(small)
    moved = [move(value) for part in firsts[:2] for value, move in part]
    summed = small_sum(small_in, ("section", "ctx"), 4)
    summed, moved, values = lax.optimization_barrier(
        (summed, moved, [value for value, _ in seconds])
    )
    in_moved[0] = [move(value) for value, (_, move) in zip(values, seconds)]
    for which in (1, 2):
        shares[0][which] = block_total(shares[0][which], moved[: n_sec - 1])
        moved = moved[n_sec - 1 :]
    mlp_share, qkv_share, out_share = (mine(which) for which in range(3))
    share_rows = mlp_share.shape[0] // 2
    mod_total, grad_bqv, grad_bo, grad_b1, grad_b2 = from_rows(
        summed,
        [(latent_total, width_cols)]
        + [(math.prod(shape[:-1]), shape[-1]) for shape in bias_shapes],
    )
    mod_rounded = mod_total.astype(jnp.bfloat16)
    cond_part = jnp.dot(mod_rounded, w_ada[0].T, preferred_element_type=jnp.float32)
    cond_part = jnp.pad(cond_part, ((0, -latent_total % 8), (0, 0)))
    block_out = rows.assembled(outs, out_moved)
    cond_part, in_moved[0], mlp_share, qkv_share, out_share, block_out = lax.optimization_barrier(
        (cond_part, in_moved[0], mlp_share, qkv_share, out_share, block_out)
    )
    cond_sum = small_sum(cond_part[None], ("section", "tensor"), 5)[:latent_total]
    in_grad = rows.assembled(in_grads, in_moved).astype(jnp.float32)
    grad_w_ada = jnp.dot(cond_act.T, mod_rounded, preferred_element_type=jnp.float32)[None]
    grad_b_ada = jnp.sum(mod_total, axis=0)[None]
    sigmoid_c = jax.nn.sigmoid(condition)
    cond_grad = cond_sum * sigmoid_c * (1.0 + condition * (1.0 - sigmoid_c))
    return (
        block_out[None],
        in_grad[None],
        cond_grad,
        grad_w_ada,
        grad_b_ada,
        qkv_share.reshape(1, share_rows, 3, local_cols),
        grad_bqv[None],
        out_share.T[None],
        grad_bo,
        mlp_share[share_rows:][None],
        grad_b1,
        mlp_share[:share_rows].T[None],
        grad_b2,
    )


def solution(mesh):
    return jax.shard_map(
        local,
        mesh=mesh,
        in_specs=(
            P(None, "ctx", None),
            P(None, "ctx"),
            P(None, "ctx", None),
            P("section", "ctx", "tensor"),
            P("section", "tensor"),
            P("section", None, None, "tensor"),
            P("section", None, "tensor"),
            P("section", "tensor", None),
            P("section", None),
            P("section", None, "tensor"),
            P("section", "tensor"),
            P("section", "tensor", None),
            P("section", None),
        ),
        out_specs=(
            P("section", None, "ctx", None),
            P("section", None, "ctx", None),
            P(None, "ctx"),
            P("section", "ctx", "tensor"),
            P("section", "tensor"),
            P("section", "ctx", None, "tensor"),
            P("section", None, "tensor"),
            P("section", "tensor", "ctx"),
            P("section", None),
            P("section", "ctx", "tensor"),
            P("section", "tensor"),
            P("section", "tensor", "ctx"),
            P("section", None),
        ),
        check_vma=False,
    )
```
